32 devices in a mesh: runs: 2 (over x), sky: 16 (over z, y, core).
Axes of the slice: x: 2, y: 2, z: 4, core: 2. Of those that a mesh axis runs over, the one named last changes fastest.
Arguments:
- start_x: float32 [2048, 128], P(('runs', 'sky')), parts along dimension 0, may hold values from 2 to 125
- start_y: float32 [2048, 128], P(('runs', 'sky')), parts along dimension 0, may hold values from 2 to 13
- gradients: bfloat16 [3, 2, 8192, 256], P(None, None, ('runs', 'sky')), parts along dimension 2, may hold values from -6 to 6
- tile_map: int32 [3, 2048, 1], P(None, ('runs', 'sky')), parts along dimension 1, may hold values from 0 to 15; in each aligned block of 64 rows (0 to 63, 64 to 127, ..., all dimensions but the last counted through in order) at most 8 rows name the same one
- row_anchor: int32 [3, 2048], P(None, ('runs', 'sky')), parts along dimension 1, may hold values from 0 to 240
- col_anchor: int32 [3, 2048], P(None, ('runs', 'sky')), parts along dimension 1, may hold values from 0 to 128
Outputs:
- final_pos: float32 [2048, 2, 128], P(('runs', 'sky')), parts along dimension 0
- jacobian: float32 [2048, 4, 128], P(('runs', 'sky')), parts along dimension 0
The draws below stay inside these ranges and needn't reach their ends.
There are 2 independent parts, one for each index of `runs`. The reference program is written for one: setup_inputs(seed, part) draws one part's arguments, and reference() takes and returns one part's arrays. A program takes and returns all parts, laid end to end along the dimension named above; each array names one. Nothing has to cross between parts.
Inputs may be any that keep to these rules, and one draw needn't show every extreme that they name: `tile_map`: in each plane at most 8 of one device's 64 ray blocks name the same tile, and that many do for some tile.
All inputs are finite; a program needn't handle non-finite values.
Results may differ from the reference program's by a relative error of at most 0.0033.
Values may be sent and summed in bfloat16 or wider, within the bound.
No kernel may reach another device: no remote copies, remote signals or barrier semaphores. Data moves between devices by JAX's collectives and lax.ppermute only.
A program may use at most 64 MiB of HBM per device.

```python
import math
import jax
import jax.numpy as jnp
import numpy as np
from jax import lax

RB = 128
WR = 16
WC = 128
TROWS = 256
TCOLS = 256
PLANES = 3
NBLK = 64
BLOCKS = 1024
CAP = 8
N_SKY = 16


def touch_ends(values, rng, least, top_value):
    longest = values.shape.index(max(values.shape))
    spots = []
    for shift in (0, 1):
        where = [jax.random.randint(jax.random.fold_in(rng, axis), (), 0, length) for axis, length in enumerate(values.shape)]
        where[longest] = (where[longest] + shift) % values.shape[longest]
        spots.append(tuple(where))
    return values.at[spots[0]].set(least).at[spots[1]].set(top_value)


def steps_of(own_key, dims, split, smallest, high):
    factor_of = 1.0
    for axis_at, parts in split:
        heights = jax.random.uniform(jax.random.fold_in(jax.random.fold_in(own_key, 6), axis_at), (parts,), jnp.float32, smallest / len(split), high / len(split))
        factor_of = factor_of * jnp.repeat(jnp.exp(heights), dims[axis_at] // parts).reshape((-1,) + (1,) * (len(dims) - 1 - axis_at))
    return factor_of


def deal_out(rng, own, number, rows, count, top, reach, slope):
    ranking = jax.random.permutation(rng, count)
    crowded, common = shares(count, rows * top, reach, slope, True), shares(count, rows * top, reach, slope, False)
    places = jnp.arange(count)

    def named(lengths, offset_by):
        used = int((lengths > 0).sum())
        fixed = max(1, used // 4)
        moved = fixed + (places - fixed + offset_by * (used - fixed)) % max(1, count - fixed)
        return jnp.zeros((count,), jnp.int32).at[ranking[jnp.where(places < fixed, places, moved)]].set(jnp.asarray(lengths, jnp.int32))

    lengths = jnp.where(number % 4 == 0, named(crowded, number // 4), named(common, number - number // 4 - 1))
    mixed = jax.random.permutation(jax.random.fold_in(own, 3), count)
    giver, taker = mixed[0:count // 2 * 2:2], mixed[1:count // 2 * 2:2]
    room = jnp.minimum(lengths[giver] - 1, reach - lengths[taker]) // 2
    room = jnp.where((giver == ranking[0]) | (taker == ranking[0]) | (lengths[taker] == 0), 0, jnp.maximum(room, 0))
    moved = jax.random.randint(jax.random.fold_in(own, 4), (count // 2,), 0, 1 << 20) % (room + 1)
    lengths = lengths.at[giver].add(-moved).at[taker].add(moved)
    items = jnp.searchsorted(jnp.cumsum(lengths), jnp.arange(rows * top), side="right").astype(jnp.int32)
    listing = items.reshape(top, rows).T
    listing = listing[jax.random.permutation(jax.random.fold_in(own, 1), rows)]
    offset_by = jax.random.randint(jax.random.fold_in(own, 2), (rows, 1), 0, top)
    return jnp.take_along_axis(listing, (jnp.arange(top)[None, :] + offset_by) % top, axis=1)


def shares(number_of, total, reach, skew, full):
    weights = [(1 << 20) // math.isqrt(grade ** skew) + 1 for grade in range(1, number_of + 1)]
    largest = reach if full else min(reach, max(-(-total // number_of), total * weights[0] // sum(weights)))
    least = 1 if total - largest >= number_of - 1 else 0
    holding, surplus = [largest] + [least] * (number_of - 1), total - largest - least * (number_of - 1)
    while surplus > 0:
        free = [i for i in range(1, number_of) if holding[i] < largest] or [i for i in range(1, number_of) if holding[i] < reach]
        mass, remaining = sum([weights[i] for i in free]), surplus
        for i in free:
            addition = min(reach - holding[i], max(1, remaining * weights[i] // mass), surplus)
            holding[i] = holding[i] + addition
            surplus = surplus - addition
    return np.array(holding)


def bell_draw(rng, extent, scale, reach, split=(), kind=jnp.bfloat16):
    gain = steps_of(rng, extent, split, -0.22, 0.18) if split else 1.0
    values = jax.random.normal(rng, extent, jnp.float32) * scale * gain
    return jnp.minimum(jnp.maximum(values, -reach), reach).astype(kind)


def setup_inputs(seed: int = 0, part: int = 0) -> dict:
    streams_of = jax.random.split(jax.random.key(seed), 7)
    own_keys = jax.random.split(jax.random.fold_in(streams_of[6], part), 7)
    start_x = jnp.clip(2.0 + 123.0 * jax.random.uniform(own_keys[0], (BLOCKS, RB), jnp.float32) ** steps_of(own_keys[0], (BLOCKS, RB), ((0, 16),), -0.2, 0.2), 2.0, 125.0)
    start_y = jnp.clip(2.0 + 11.0 * jax.random.uniform(own_keys[1], (BLOCKS, RB), jnp.float32) ** steps_of(own_keys[1], (BLOCKS, RB), ((0, 16),), -0.2, 0.2), 2.0, 13.0)
    gradients = bell_draw(own_keys[2], (PLANES, 2, TROWS * N_SKY, TCOLS), 1.0, 6.0, ((2, 16),))
    tile_map_keys = jax.random.split(jax.random.fold_in(own_keys[3], 1), PLANES * BLOCKS // NBLK)
    tile_map_turns = jax.random.permutation(jax.random.fold_in(own_keys[3], 3), PLANES * BLOCKS // NBLK)
    tile_map = jax.vmap(lambda own, number: deal_out(jax.random.fold_in(own_keys[3], 2), own, number, NBLK, N_SKY, 1, CAP, 2))(tile_map_keys, tile_map_turns).reshape((PLANES, BLOCKS, 1))
    row_anchor = touch_ends(jax.random.randint(own_keys[4], (PLANES, BLOCKS), 0, TROWS - WR + 1), jax.random.fold_in(own_keys[4], 1), 0, TROWS - WR).astype(jnp.int32)
    col_anchor = touch_ends(jax.random.randint(own_keys[5], (PLANES, BLOCKS), 0, TCOLS - WC + 1), jax.random.fold_in(own_keys[5], 1), 0, TCOLS - WC).astype(jnp.int32)
    return {"start_x": start_x, "start_y": start_y, "gradients": gradients, "tile_map": tile_map, "row_anchor": row_anchor, "col_anchor": col_anchor}


lens_ratio = (0.85, 0.7, 0.9)
lens_strength = (0.5, 0.6, 0.45)


def spline(dist):
    mag = jnp.abs(dist)
    inner = 2.0 / 3.0 - mag * mag + 0.5 * mag * mag * mag
    outer_base = jnp.maximum(2.0 - mag, 0.0)
    outer = outer_base * outer_base * outer_base / 6.0
    return jnp.where(mag < 1.0, inner, outer)


def spline_slope(dist):
    mag = jnp.abs(dist)
    inner = -2.0 * mag + 1.5 * mag * mag
    outer_base = jnp.maximum(2.0 - mag, 0.0)
    outer = -0.5 * outer_base * outer_base
    return jnp.where(dist < 0.0, -1.0, 1.0) * jnp.where(mag < 1.0, inner, outer)


def interp_group(pos, win):
    count = pos.shape[0]
    rays = pos.shape[2]
    cols = jnp.arange(WC).astype(pos.dtype)
    rows = jnp.arange(WR).astype(pos.dtype)
    dx = pos[:, 0, None, :] - cols[None, :, None]
    kern = jnp.concatenate([spline(dx), spline_slope(dx)], axis=2).astype(jnp.bfloat16)
    mixed = jnp.einsum("nqs,nsr->nqr", win.reshape(count, 2 * WR, WC).astype(jnp.float32), kern.astype(jnp.float32), precision=lax.Precision.HIGHEST)
    mixed = mixed.reshape(count, 2, WR, 2, rays)
    dy = pos[:, 1, None, :] - rows[None, :, None]
    row_kern = spline(dy)[:, None]
    row_slope = spline_slope(dy)[:, None]
    alpha = jnp.sum(row_kern * mixed[:, :, :, 0], axis=2)
    along_x = jnp.sum(row_kern * mixed[:, :, :, 1], axis=2)
    along_y = jnp.sum(row_slope * mixed[:, :, :, 0], axis=2)
    return jnp.concatenate([alpha, along_x[:, 0:1], along_y[:, 0:1], along_x[:, 1:2], along_y[:, 1:2]], axis=1)


def advance(state, local, plane):
    pos, vel, jac, djac = state
    ratio = lens_ratio[plane]
    strength = lens_strength[plane]
    alpha = local[:, 0:2]
    hxx, hxy, hyx, hyy = local[:, 2], local[:, 3], local[:, 4], local[:, 5]
    axx, axy, ayx, ayy = jac[:, 0], jac[:, 1], jac[:, 2], jac[:, 3]
    product = jnp.stack([hxx * axx + hxy * ayx, hxx * axy + hxy * ayy, hyx * axx + hyy * ayx, hyx * axy + hyy * ayy], axis=1)
    vel = ratio * vel - strength * alpha
    pos = pos + vel
    djac = ratio * djac - strength * product
    jac = jac + djac
    return (pos, vel, jac, djac)


def reference(start_x, start_y, gradients, tile_map, row_anchor, col_anchor):
    pos = jnp.stack([start_x, start_y], axis=1)
    vel = jnp.zeros_like(pos)
    unit = jnp.array([1.0, 0.0, 0.0, 1.0], dtype=pos.dtype)
    jac = jnp.zeros((BLOCKS, 4, RB), pos.dtype) + unit[None, :, None]
    djac = jnp.zeros_like(jac)
    state = (pos, vel, jac, djac)
    group = math.gcd(BLOCKS, 256)
    steps_count = BLOCKS // group
    for plane in range(PLANES):
        sheet = gradients[plane]
        rows = (tile_map[plane, :, 0] * TROWS + row_anchor[plane]).astype(jnp.int32)
        cols = col_anchor[plane].astype(jnp.int32)

        def cut(row, col):
            zero = jnp.zeros((), jnp.int32)
            return lax.dynamic_slice(sheet, (zero, row.astype(jnp.int32), col.astype(jnp.int32)), (2, WR, WC))

        def one(items):
            part_pos, part_rows, part_cols = items
            return interp_group(part_pos, jax.vmap(cut)(part_rows, part_cols))

        local = lax.map(one, (state[0].reshape(steps_count, group, 2, RB), rows.reshape(steps_count, group), cols.reshape(steps_count, group)))
        state = advance(state, local.reshape(BLOCKS, 6, RB), plane)
    return state[0], state[2]
```

```python
import functools
import math

import jax
import jax.numpy as jnp
from jax import lax
from jax.experimental import pallas as pl
from jax.experimental.pallas import tpu as pltpu
from jax.sharding import PartitionSpec as P

WR = 16
WC = 128
PLANES = 3

lens_ratio = (0.85, 0.7, 0.9)
lens_strength = (0.5, 0.6, 0.45)

VMEM = pltpu.VMEM
SMEM = pltpu.SMEM


def whole(space=VMEM):
    return pl.BlockSpec(memory_space=space)


def dot_last(a, b):
    return lax.dot_general(
        a, b, (((1,), (1,)), ((), ())), preferred_element_type=jnp.float32
    )


def prep_kernel(peers, cap, tile_ref, row_ref, col_ref, req_ref, slot_ref):
    nblk = tile_ref.shape[1]
    lanes = req_ref.shape[1]
    owner = lax.broadcasted_iota(jnp.int32, (peers, nblk), 0)
    earlier = (
        lax.broadcasted_iota(jnp.int32, (nblk, nblk), 1)
        < lax.broadcasted_iota(jnp.int32, (nblk, nblk), 0)
    ).astype(jnp.float32).astype(jnp.bfloat16)
    lane = lax.broadcasted_iota(jnp.int32, (lanes, nblk), 0)
    rows = jnp.zeros((peers, lanes), jnp.float32)
    cols = jnp.zeros((peers, lanes), jnp.float32)
    for k in range(PLANES):
        tile = tile_ref[k : k + 1, :]
        hit = (owner == tile).astype(jnp.float32)
        hit16 = hit.astype(jnp.bfloat16)
        before = dot_last(hit16, earlier)
        rank = jnp.sum(before * hit, axis=0, keepdims=True).astype(jnp.int32)
        slot_ref[k : k + 1, :] = tile * cap + rank
        here = lane == (rank + k * cap)
        zero = jnp.zeros((), jnp.float32)
        row = jnp.where(here, row_ref[k : k + 1, :].astype(jnp.float32), zero)
        col = jnp.where(here, col_ref[k : k + 1, :].astype(jnp.float32), zero)
        rows += dot_last(hit16, row.astype(jnp.bfloat16))
        cols += dot_last(hit16, col.astype(jnp.bfloat16))
    req_ref[...] = rows.astype(jnp.int32) * 65536 + cols.astype(jnp.int32)


def prep(tile_map, row_anchor, col_anchor, peers, cap):
    nblk = tile_map.shape[1]
    lanes = -(-PLANES * cap // 128) * 128
    return pl.pallas_call(
        functools.partial(prep_kernel, peers, cap),
        out_shape=(
            jax.ShapeDtypeStruct((peers, lanes), jnp.int32),
            jax.ShapeDtypeStruct((PLANES, nblk), jnp.int32),
        ),
        in_specs=[whole()] * 3,
        out_specs=(whole(), whole()),
        name="prep",
    )(tile_map, row_anchor, col_anchor)


def cut_kernel(plane, cap, req_ref, sheet_ref, out_ref, half_ref):
    halves = sheet_ref.shape[3] // WC
    for c in range(2):
        for h in range(halves):
            half_ref[c * halves + h] = sheet_ref[plane, c, :, h * WC : (h + 1) * WC].astype(jnp.float32)
    lane = lax.broadcasted_iota(jnp.int32, (WR, WC), 1)

    def one(slot, carry):
        packed = req_ref[slot // cap, plane * cap + slot % cap]
        row = packed >> 16
        col = packed & 65535
        turn = (WC - col) & (WC - 1)
        left = lane < WC - col
        for c in range(2):
            part = [
                pltpu.roll(half_ref[c * halves + h, pl.ds(row, WR), :], turn, 1)
                for h in range(halves)
            ]
            out_ref[slot, c * WR : (c + 1) * WR, :] = jnp.where(left, part[0], part[1]).astype(jnp.bfloat16)
        return carry

    lax.fori_loop(0, out_ref.shape[0], one, 0, unroll=8)


def cut(plane, cap, requests, sheet):
    count = requests.shape[0] * cap
    return pl.pallas_call(
        functools.partial(cut_kernel, plane, cap),
        out_shape=jax.ShapeDtypeStruct((count, 2 * WR, WC), jnp.bfloat16),
        in_specs=[whole(SMEM), whole()],
        out_specs=whole(),
        scratch_shapes=[VMEM((2 * sheet.shape[3] // WC, sheet.shape[2], WC), jnp.float32)],
        name=f"cut{plane}",
    )(requests, sheet)


def taps(pos):
    cell = jnp.floor(pos)
    f = pos - cell
    g = 1.0 - f
    f2, g2 = f * f, g * g
    value = (
        g2 * g / 6.0,
        2.0 / 3.0 - f2 + 0.5 * f2 * f,
        2.0 / 3.0 - g2 + 0.5 * g2 * g,
        f2 * f / 6.0,
    )
    slope = (-0.5 * g2, -2.0 * f + 1.5 * f2, 2.0 * g - 1.5 * g2, 0.5 * f2)
    return cell, value, slope


def interp_kernel(plane, slot_ref, win_ref, *refs):
    first, last = plane == 0, plane == PLANES - 1
    if first:
        x_ref, y_ref = refs[:2]
        refs = refs[2:]
    else:
        state_ref = refs[0]
        refs = refs[1:]
    if last:
        pos_out, jac_out = refs[:2]
        refs = refs[2:]
    else:
        state_out = refs[0]
        refs = refs[1:]
    tap_ref, res_ref = refs
    nblk, rays = res_ref.shape[1:]

    if first:
        px, py = x_ref[...], y_ref[...]
    else:
        px, py = state_ref[0], state_ref[1]
    for at, pos in ((0, px), (9, py)):
        cell, value, slope = taps(pos)
        tap_ref[at] = cell
        for j in range(4):
            tap_ref[at + 1 + j] = value[j]
            tap_ref[at + 5 + j] = slope[j]

    def one(b, carry):
        def row(j):
            return tap_ref[j, pl.ds(b, 1), :]

        def spread(at, size):
            near = lax.broadcasted_iota(jnp.int32, (size, rays), 0).astype(jnp.float32) - row(at)
            zero = jnp.zeros((size, rays), jnp.float32)
            value, slope = zero, zero
            for j in range(4):
                here = near == (j - 1.0)
                value = jnp.where(here, row(at + 1 + j), value)
                slope = jnp.where(here, row(at + 5 + j), slope)
            return value, slope

        kx, kxd = spread(0, WC)
        kern = jnp.concatenate([kx.astype(jnp.bfloat16), kxd.astype(jnp.bfloat16)], axis=1)
        mixed = jnp.dot(win_ref[slot_ref[plane, b]], kern, preferred_element_type=jnp.float32)
        ky, kyd = spread(9, WR)
        for c in range(2):
            part = mixed[c * WR : (c + 1) * WR]
            mixed0, mixed1 = part[:, :rays], part[:, rays:]
            for at, product in ((0, ky * mixed0), (2, ky * mixed1), (4, kyd * mixed0)):
                res_ref[at + c, pl.ds(b, 1), :] = jnp.sum(product, axis=0, keepdims=True)
        return carry

    lax.fori_loop(0, nblk, one, 0, unroll=4)

    ratio, strength = lens_ratio[plane], lens_strength[plane]
    ax, ay = res_ref[0], res_ref[1]
    hxx, hyx, hxy, hyy = res_ref[2], res_ref[3], res_ref[4], res_ref[5]
    if first:
        vx, vy = -strength * ax, -strength * ay
        dj = [-strength * h for h in (hxx, hxy, hyx, hyy)]
        jac = [1.0 + dj[0], dj[1], dj[2], 1.0 + dj[3]]
    else:
        vx = ratio * state_ref[2] - strength * ax
        vy = ratio * state_ref[3] - strength * ay
        axx, axy, ayx, ayy = [state_ref[4 + j] for j in range(4)]
        product = (
            hxx * axx + hxy * ayx,
            hxx * axy + hxy * ayy,
            hyx * axx + hyy * ayx,
            hyx * axy + hyy * ayy,
        )
        dj = [ratio * state_ref[8 + j] - strength * product[j] for j in range(4)]
        jac = [old + d for old, d in zip((axx, axy, ayx, ayy), dj)]
    px, py = px + vx, py + vy
    if last:
        pos_out[:, 0, :] = px
        pos_out[:, 1, :] = py
        for j in range(4):
            jac_out[:, j, :] = jac[j]
    else:
        for j, value in enumerate([px, py, vx, vy] + jac + dj):
            state_out[j] = value


def interp(plane, slots, windows, state):
    nblk = slots.shape[1]
    rays = state[0].shape[-1]
    if plane == PLANES - 1:
        out_shape = (
            jax.ShapeDtypeStruct((nblk, 2, rays), jnp.float32),
            jax.ShapeDtypeStruct((nblk, 4, rays), jnp.float32),
        )
    else:
        out_shape = (jax.ShapeDtypeStruct((12, nblk, rays), jnp.float32),)
    return pl.pallas_call(
        functools.partial(interp_kernel, plane),
        out_shape=out_shape,
        in_specs=[whole(SMEM), whole()] + [whole()] * len(state),
        out_specs=(whole(),) * len(out_shape),
        scratch_shapes=[
            VMEM((18, nblk, rays), jnp.float32),
            VMEM((6, nblk, rays), jnp.float32),
        ],
        name=f"interp{plane}",
    )(slots, windows, *state)


def body(start_x, start_y, gradients, tile_map, row_anchor, col_anchor):
    peers = lax.axis_size("sky")
    nblk = start_x.shape[0]
    cap = max(2, 2 * nblk // peers)
    requests, slots = prep(tile_map[:, :, 0], row_anchor, col_anchor, peers, cap)
    asked = lax.all_to_all(requests, "sky", split_axis=0, concat_axis=0, tiled=True)
    received = []
    for plane in range(PLANES):
        windows = cut(plane, cap, asked, gradients)
        got = lax.all_to_all(
            windows.reshape(peers, cap, 2 * WR, WC), "sky", split_axis=0, concat_axis=0, tiled=True
        )
        received.append(got.reshape(peers * cap, 2 * WR, WC))
    state = (start_x, start_y)
    for plane in range(PLANES):
        state = interp(plane, slots, received[plane], state)
    return state


def solution(mesh):
    return jax.shard_map(
        body,
        mesh=mesh,
        in_specs=(
            P(("runs", "sky"), None),
            P(("runs", "sky"), None),
            P(None, None, ("runs", "sky"), None),
            P(None, ("runs", "sky"), None),
            P(None, ("runs", "sky")),
            P(None, ("runs", "sky")),
        ),
        out_specs=(P(("runs", "sky"), None, None), P(("runs", "sky"), None, None)),
        check_vma=False,
    )
```

```python
import functools
import math

import jax
import jax.numpy as jnp
from jax import lax
from jax.experimental import pallas as pl
from jax.experimental.pallas import tpu as pltpu
from jax.sharding import PartitionSpec as P

WR = 16
WC = 128
PLANES = 3

lens_ratio = (0.85, 0.7, 0.9)
lens_strength = (0.5, 0.6, 0.45)

VMEM = pltpu.VMEM
SMEM = pltpu.SMEM


def whole(space=VMEM):
    return pl.BlockSpec(memory_space=space)


def dot_last(a, b):
    return lax.dot_general(
        a, b, (((1,), (1,)), ((), ())), preferred_element_type=jnp.float32
    )


def prep_kernel(peers, halves, cap, tile_ref, row_ref, col_ref, req_ref, slot_ref):
    relays = peers // halves
    nblk = tile_ref.shape[1]
    lanes = req_ref.shape[1]
    owner = lax.broadcasted_iota(jnp.int32, (peers, nblk), 0)
    earlier = (
        lax.broadcasted_iota(jnp.int32, (nblk, nblk), 1)
        < lax.broadcasted_iota(jnp.int32, (nblk, nblk), 0)
    ).astype(jnp.float32).astype(jnp.bfloat16)
    lane = lax.broadcasted_iota(jnp.int32, (lanes, nblk), 0)
    rows = jnp.zeros((relays, lanes), jnp.float32)
    cols = jnp.zeros((relays, lanes), jnp.float32)
    for k in range(PLANES):
        tile = tile_ref[k : k + 1, :]
        hit = (owner == tile).astype(jnp.float32)
        hit16 = hit.astype(jnp.bfloat16)
        before = dot_last(hit16, earlier)
        rank = jnp.sum(before * hit, axis=0, keepdims=True).astype(jnp.int32)
        side = tile // relays
        rank = rank + side * cap
        slot_ref[k : k + 1, :] = (tile - side * relays) * (halves * cap) + rank
        here = lane == (rank + k * halves * cap)
        zero = jnp.zeros((), jnp.float32)
        row = jnp.where(here, row_ref[k : k + 1, :].astype(jnp.float32), zero)
        col = jnp.where(here, col_ref[k : k + 1, :].astype(jnp.float32), zero)
        fold = sum(hit[h * relays : (h + 1) * relays] for h in range(halves)).astype(jnp.bfloat16)
        rows += dot_last(fold, row.astype(jnp.bfloat16))
        cols += dot_last(fold, col.astype(jnp.bfloat16))
    req_ref[...] = rows.astype(jnp.int32) * 65536 + cols.astype(jnp.int32)


def prep(tile_map, row_anchor, col_anchor, peers, halves, cap):
    nblk = tile_map.shape[1]
    lanes = -(-PLANES * halves * cap // 128) * 128
    return pl.pallas_call(
        functools.partial(prep_kernel, peers, halves, cap),
        out_shape=(
            jax.ShapeDtypeStruct((peers // halves, lanes), jnp.int32),
            jax.ShapeDtypeStruct((PLANES, nblk), jnp.int32),
        ),
        in_specs=[whole()] * 3,
        out_specs=(whole(), whole()),
        name="prep",
    )(tile_map, row_anchor, col_anchor)


def cut_kernel(plane, cap, side_ref, req_ref, own_ref, mirror_ref, out_ref, half_ref):
    parts = own_ref.shape[3] // WC
    for c in range(2):
        for h in range(parts):
            lanes = slice(h * WC, (h + 1) * WC)
            half_ref[c * parts + h] = own_ref[plane, c, :, lanes].astype(jnp.float32)
            half_ref[(2 + c) * parts + h] = mirror_ref[c, :, lanes].astype(jnp.float32)
    lane = lax.broadcasted_iota(jnp.int32, (WR, WC), 1)
    side = side_ref[0]
    each = 2 * cap

    def one(source, carry):
        for place in range(each):
            packed = req_ref[source, plane * each + place]
            base = jnp.where(side == place // cap, 0, 2 * parts)
            row = packed >> 16
            col = packed & 65535
            turn = (WC - col) & (WC - 1)
            left = lane < WC - col
            for c in range(2):
                part = [
                    pltpu.roll(half_ref[base + c * parts + h, pl.ds(row, WR), :], turn, 1)
                    for h in range(parts)
                ]
                out_ref[source * each + place, c * WR : (c + 1) * WR, :] = jnp.where(
                    left, part[0], part[1]
                ).astype(jnp.bfloat16)
        return carry

    lax.fori_loop(0, req_ref.shape[0], one, 0)


def cut(plane, cap, side, requests, sheet, mirror):
    count = requests.shape[0] * 2 * cap
    return pl.pallas_call(
        functools.partial(cut_kernel, plane, cap),
        out_shape=jax.ShapeDtypeStruct((count, 2 * WR, WC), jnp.bfloat16),
        in_specs=[whole(SMEM), whole(SMEM), whole(), whole()],
        out_specs=whole(),
        scratch_shapes=[VMEM((4 * sheet.shape[3] // WC, sheet.shape[2], WC), jnp.float32)],
        name=f"cut{plane}",
    )(side, requests, sheet, mirror)


def taps(pos):
    cell = jnp.floor(pos)
    f = pos - cell
    g = 1.0 - f
    f2, g2 = f * f, g * g
    value = (
        g2 * g / 6.0,
        2.0 / 3.0 - f2 + 0.5 * f2 * f,
        2.0 / 3.0 - g2 + 0.5 * g2 * g,
        f2 * f / 6.0,
    )
    slope = (-0.5 * g2, -2.0 * f + 1.5 * f2, 2.0 * g - 1.5 * g2, 0.5 * f2)
    return cell, value, slope


def interp_kernel(plane, slot_ref, win_ref, *refs):
    first, last = plane == 0, plane == PLANES - 1
    if first:
        x_ref, y_ref = refs[:2]
        refs = refs[2:]
    else:
        state_ref = refs[0]
        refs = refs[1:]
    if last:
        pos_out, jac_out = refs[:2]
        refs = refs[2:]
    else:
        state_out = refs[0]
        refs = refs[1:]
    tap_ref, res_ref = refs
    nblk, rays = res_ref.shape[1:]

    if first:
        px, py = x_ref[...], y_ref[...]
    else:
        px, py = state_ref[0], state_ref[1]
    for at, pos in ((0, px), (9, py)):
        cell, value, slope = taps(pos)
        tap_ref[at] = cell
        for j in range(4):
            tap_ref[at + 1 + j] = value[j]
            tap_ref[at + 5 + j] = slope[j]

    def one(b, carry):
        def row(j):
            return tap_ref[j, pl.ds(b, 1), :]

        def spread(at, size):
            near = lax.broadcasted_iota(jnp.int32, (size, rays), 0).astype(jnp.float32) - row(at)
            zero = jnp.zeros((size, rays), jnp.float32)
            value, slope = zero, zero
            for j in range(4):
                here = near == (j - 1.0)
                value = jnp.where(here, row(at + 1 + j), value)
                slope = jnp.where(here, row(at + 5 + j), slope)
            return value, slope

        kx, kxd = spread(0, WC)
        kern = jnp.concatenate([kx.astype(jnp.bfloat16), kxd.astype(jnp.bfloat16)], axis=1)
        mixed = jnp.dot(win_ref[slot_ref[plane, b]], kern, preferred_element_type=jnp.float32)
        ky, kyd = spread(9, WR)
        for c in range(2):
            part = mixed[c * WR : (c + 1) * WR]
            mixed0, mixed1 = part[:, :rays], part[:, rays:]
            for at, product in ((0, ky * mixed0), (2, ky * mixed1), (4, kyd * mixed0)):
                res_ref[at + c, pl.ds(b, 1), :] = jnp.sum(product, axis=0, keepdims=True)
        return carry

    lax.fori_loop(0, nblk, one, 0, unroll=4)

    ratio, strength = lens_ratio[plane], lens_strength[plane]
    ax, ay = res_ref[0], res_ref[1]
    hxx, hyx, hxy, hyy = res_ref[2], res_ref[3], res_ref[4], res_ref[5]
    if first:
        vx, vy = -strength * ax, -strength * ay
        dj = [-strength * h for h in (hxx, hxy, hyx, hyy)]
        jac = [1.0 + dj[0], dj[1], dj[2], 1.0 + dj[3]]
    else:
        vx = ratio * state_ref[2] - strength * ax
        vy = ratio * state_ref[3] - strength * ay
        axx, axy, ayx, ayy = [state_ref[4 + j] for j in range(4)]
        product = (
            hxx * axx + hxy * ayx,
            hxx * axy + hxy * ayy,
            hyx * axx + hyy * ayx,
            hyx * axy + hyy * ayy,
        )
        dj = [ratio * state_ref[8 + j] - strength * product[j] for j in range(4)]
        jac = [old + d for old, d in zip((axx, axy, ayx, ayy), dj)]
    px, py = px + vx, py + vy
    if last:
        pos_out[:, 0, :] = px
        pos_out[:, 1, :] = py
        for j in range(4):
            jac_out[:, j, :] = jac[j]
    else:
        for j, value in enumerate([px, py, vx, vy] + jac + dj):
            state_out[j] = value


def interp(plane, slots, windows, state):
    nblk = slots.shape[1]
    rays = state[0].shape[-1]
    if plane == PLANES - 1:
        out_shape = (
            jax.ShapeDtypeStruct((nblk, 2, rays), jnp.float32),
            jax.ShapeDtypeStruct((nblk, 4, rays), jnp.float32),
        )
    else:
        out_shape = (jax.ShapeDtypeStruct((12, nblk, rays), jnp.float32),)
    return pl.pallas_call(
        functools.partial(interp_kernel, plane),
        out_shape=out_shape,
        in_specs=[whole(SMEM), whole()] + [whole()] * len(state),
        out_specs=(whole(),) * len(out_shape),
        scratch_shapes=[
            VMEM((18, nblk, rays), jnp.float32),
            VMEM((6, nblk, rays), jnp.float32),
        ],
        name=f"interp{plane}",
    )(slots, windows, *state)


def body(start_x, start_y, gradients, tile_map, row_anchor, col_anchor):
    peers = lax.axis_size("sky")
    nblk = start_x.shape[0]
    cap = max(2, 2 * nblk // peers)
    relays = peers // 2
    groups = [[h * relays + r for r in range(relays)] for h in range(2)]
    swap = [(i, (i + relays) % peers) for i in range(peers)]
    mirrors = [lax.ppermute(gradients[plane], "sky", swap) for plane in range(PLANES)]

    def exchange(x):
        return lax.all_to_all(
            x, "sky", split_axis=0, concat_axis=0, axis_index_groups=groups, tiled=True
        )

    requests, slots = prep(tile_map[:, :, 0], row_anchor, col_anchor, peers, 2, cap)
    asked = exchange(requests)
    side = (lax.axis_index("sky") // relays).astype(jnp.int32).reshape(1)
    received = []
    for plane in range(PLANES):
        windows = cut(plane, cap, side, asked, gradients, mirrors[plane])
        got = exchange(windows.reshape(relays, 2 * cap, 2 * WR, WC))
        received.append(got.reshape(peers * cap, 2 * WR, WC))
    state = (start_x, start_y)
    for plane in range(PLANES):
        state = interp(plane, slots, received[plane], state)
    return state


def solution(mesh):
    return jax.shard_map(
        body,
        mesh=mesh,
        in_specs=(
            P(("runs", "sky"), None),
            P(("runs", "sky"), None),
            P(None, None, ("runs", "sky"), None),
            P(None, ("runs", "sky"), None),
            P(None, ("runs", "sky")),
            P(None, ("runs", "sky")),
        ),
        out_specs=(P(("runs", "sky"), None, None), P(("runs", "sky"), None, None)),
        check_vma=False,
    )
```

```python
import functools

import jax
import jax.numpy as jnp
from jax import lax
from jax.experimental import pallas as pl
from jax.experimental.pallas import tpu as pltpu
from jax.sharding import PartitionSpec as P


WR = 16
WC = 128
PLANES = 3

lens_ratio = (0.85, 0.7, 0.9)
lens_strength = (0.5, 0.6, 0.45)

VMEM = pltpu.VMEM
SMEM = pltpu.SMEM


def whole(space=VMEM):
    return pl.BlockSpec(memory_space=space)


def dot_last(a, b):
    return lax.dot_general(
        a, b, (((1,), (1,)), ((), ())), preferred_element_type=jnp.float32
    )


def prep_kernel(peers, halves, cap, tile_ref, row_ref, col_ref, req_ref, slot_ref):
    relays = peers // halves
    nblk = tile_ref.shape[1]
    lanes = req_ref.shape[1]
    owner = lax.broadcasted_iota(jnp.int32, (peers, nblk), 0)
    earlier = (
        lax.broadcasted_iota(jnp.int32, (nblk, nblk), 1)
        < lax.broadcasted_iota(jnp.int32, (nblk, nblk), 0)
    ).astype(jnp.float32).astype(jnp.bfloat16)
    lane = lax.broadcasted_iota(jnp.int32, (lanes, nblk), 0)
    rows = jnp.zeros((relays, lanes), jnp.float32)
    cols = jnp.zeros((relays, lanes), jnp.float32)
    for k in range(PLANES):
        tile = tile_ref[k : k + 1, :]
        hit = (owner == tile).astype(jnp.float32)
        hit16 = hit.astype(jnp.bfloat16)
        before = dot_last(hit16, earlier)
        rank = jnp.sum(before * hit, axis=0, keepdims=True).astype(jnp.int32)
        side = tile // relays
        rank = rank + side * cap
        slot_ref[k : k + 1, :] = (tile - side * relays) * (halves * cap) + rank
        here = lane == (rank + k * halves * cap)
        zero = jnp.zeros((), jnp.float32)
        row = jnp.where(here, row_ref[k : k + 1, :].astype(jnp.float32), zero)
        col = jnp.where(here, col_ref[k : k + 1, :].astype(jnp.float32), zero)
        fold = sum(hit[h * relays : (h + 1) * relays] for h in range(halves)).astype(jnp.bfloat16)
        rows += dot_last(fold, row.astype(jnp.bfloat16))
        cols += dot_last(fold, col.astype(jnp.bfloat16))
    req_ref[...] = rows.astype(jnp.int32) * 65536 + cols.astype(jnp.int32)


def prep(tile_map, row_anchor, col_anchor, peers, halves, cap):
    nblk = tile_map.shape[1]
    lanes = -(-PLANES * halves * cap // 128) * 128
    return pl.pallas_call(
        functools.partial(prep_kernel, peers, halves, cap),
        out_shape=(
            jax.ShapeDtypeStruct((peers // halves, lanes), jnp.int32),
            jax.ShapeDtypeStruct((PLANES, nblk), jnp.int32),
        ),
        in_specs=[whole()] * 3,
        out_specs=(whole(), whole()),
        name="prep",
    )(tile_map, row_anchor, col_anchor)


def cut_kernel(plane, cap, side_ref, req_ref, own_ref, mirror_ref, out_ref, half_ref):
    parts = own_ref.shape[3] // WC
    for c in range(2):
        for h in range(parts):
            lanes = slice(h * WC, (h + 1) * WC)
            half_ref[c * parts + h] = own_ref[plane, c, :, lanes].astype(jnp.float32)
            half_ref[(2 + c) * parts + h] = mirror_ref[c, :, lanes].astype(jnp.float32)
    lane = lax.broadcasted_iota(jnp.int32, (WR, WC), 1)
    side = side_ref[0]
    each = 2 * cap

    def one(source, carry):
        for place in range(each):
            packed = req_ref[source, plane * each + place]
            base = jnp.where(side == place // cap, 0, 2 * parts)
            row = packed >> 16
            col = packed & 65535
            turn = (WC - col) & (WC - 1)
            left = lane < WC - col
            for c in range(2):
                part = [
                    pltpu.roll(half_ref[base + c * parts + h, pl.ds(row, WR), :], turn, 1)
                    for h in range(parts)
                ]
                out_ref[source * each + place, c * WR : (c + 1) * WR, :] = jnp.where(
                    left, part[0], part[1]
                ).astype(jnp.bfloat16)
        return carry

    lax.fori_loop(0, req_ref.shape[0], one, 0)


def cut(plane, cap, side, requests, sheet, mirror):
    count = requests.shape[0] * 2 * cap
    return pl.pallas_call(
        functools.partial(cut_kernel, plane, cap),
        out_shape=jax.ShapeDtypeStruct((count, 2 * WR, WC), jnp.bfloat16),
        in_specs=[whole(SMEM), whole(SMEM), whole(), whole()],
        out_specs=whole(),
        scratch_shapes=[VMEM((4 * sheet.shape[3] // WC, sheet.shape[2], WC), jnp.float32)],
    )(side, requests, sheet, mirror)


def taps(pos):
    cell = jnp.floor(pos)
    f = pos - cell
    g = 1.0 - f
    f2, g2 = f * f, g * g
    value = (
        g2 * g / 6.0,
        2.0 / 3.0 - f2 + 0.5 * f2 * f,
        2.0 / 3.0 - g2 + 0.5 * g2 * g,
        f2 * f / 6.0,
    )
    slope = (-0.5 * g2, -2.0 * f + 1.5 * f2, 2.0 * g - 1.5 * g2, 0.5 * f2)
    return cell, value, slope


def interp_kernel(plane, slot_ref, win_ref, *refs):
    first, last = plane == 0, plane == PLANES - 1
    if first:
        x_ref, y_ref = refs[:2]
        refs = refs[2:]
    else:
        state_ref = refs[0]
        refs = refs[1:]
    if last:
        pos_out, jac_out = refs[:2]
        refs = refs[2:]
    else:
        state_out = refs[0]
        refs = refs[1:]
    tap_ref, res_ref = refs
    nblk, rays = res_ref.shape[1:]

    if first:
        px, py = x_ref[...], y_ref[...]
    else:
        px, py = state_ref[0], state_ref[1]
    for at, pos in ((0, px), (9, py)):
        cell, value, slope = taps(pos)
        tap_ref[at] = cell
        for j in range(4):
            tap_ref[at + 1 + j] = value[j]
            tap_ref[at + 5 + j] = slope[j]

    def one(b, carry):
        def row(j):
            return tap_ref[j, pl.ds(b, 1), :]

        def spread(at, size):
            near = lax.broadcasted_iota(jnp.int32, (size, rays), 0).astype(jnp.float32) - row(at)
            zero = jnp.zeros((size, rays), jnp.float32)
            value, slope = zero, zero
            for j in range(4):
                here = near == (j - 1.0)
                value = jnp.where(here, row(at + 1 + j), value)
                slope = jnp.where(here, row(at + 5 + j), slope)
            return value, slope

        kx, kxd = spread(0, WC)
        kern = jnp.concatenate([kx.astype(jnp.bfloat16), kxd.astype(jnp.bfloat16)], axis=1)
        mixed = jnp.dot(win_ref[slot_ref[plane, b]], kern, preferred_element_type=jnp.float32)
        ky, kyd = spread(9, WR)
        for c in range(2):
            part = mixed[c * WR : (c + 1) * WR]
            mixed0, mixed1 = part[:, :rays], part[:, rays:]
            for at, product in ((0, ky * mixed0), (2, ky * mixed1), (4, kyd * mixed0)):
                res_ref[at + c, pl.ds(b, 1), :] = jnp.sum(product, axis=0, keepdims=True)
        return carry

    lax.fori_loop(0, nblk, one, 0, unroll=4)

    ratio, strength = lens_ratio[plane], lens_strength[plane]
    ax, ay = res_ref[0], res_ref[1]
    hxx, hyx, hxy, hyy = res_ref[2], res_ref[3], res_ref[4], res_ref[5]
    if first:
        vx, vy = -strength * ax, -strength * ay
        dj = [-strength * h for h in (hxx, hxy, hyx, hyy)]
        jac = [1.0 + dj[0], dj[1], dj[2], 1.0 + dj[3]]
    else:
        vx = ratio * state_ref[2] - strength * ax
        vy = ratio * state_ref[3] - strength * ay
        axx, axy, ayx, ayy = [state_ref[4 + j] for j in range(4)]
        product = (
            hxx * axx + hxy * ayx,
            hxx * axy + hxy * ayy,
            hyx * axx + hyy * ayx,
            hyx * axy + hyy * ayy,
        )
        dj = [ratio * state_ref[8 + j] - strength * product[j] for j in range(4)]
        jac = [old + d for old, d in zip((axx, axy, ayx, ayy), dj)]
    px, py = px + vx, py + vy
    if last:
        pos_out[:, 0, :] = px
        pos_out[:, 1, :] = py
        for j in range(4):
            jac_out[:, j, :] = jac[j]
    else:
        for j, value in enumerate([px, py, vx, vy] + jac + dj):
            state_out[j] = value


def interp(plane, slots, windows, state):
    nblk = slots.shape[1]
    rays = state[0].shape[-1]
    if plane == PLANES - 1:
        out_shape = (
            jax.ShapeDtypeStruct((nblk, 2, rays), jnp.float32),
            jax.ShapeDtypeStruct((nblk, 4, rays), jnp.float32),
        )
    else:
        out_shape = (jax.ShapeDtypeStruct((12, nblk, rays), jnp.float32),)
    return pl.pallas_call(
        functools.partial(interp_kernel, plane),
        out_shape=out_shape,
        in_specs=[whole(SMEM), whole()] + [whole()] * len(state),
        out_specs=(whole(),) * len(out_shape),
        scratch_shapes=[
            VMEM((18, nblk, rays), jnp.float32),
            VMEM((6, nblk, rays), jnp.float32),
        ],
    )(slots, windows, *state)


def body(start_x, start_y, gradients, tile_map, row_anchor, col_anchor):
    peers = lax.axis_size("sky")
    nblk = start_x.shape[0]
    cap = max(2, 2 * nblk // peers)
    relays = peers // 2
    groups = [[h * relays + r for r in range(relays)] for h in range(2)]
    swap = [(i, (i + relays) % peers) for i in range(peers)]
    mirrors = []
    for plane in range(PLANES):
        mirrors.append(lax.ppermute(gradients[plane], "sky", swap))

    def exchange(x):
        return lax.all_to_all(
            x, "sky", split_axis=0, concat_axis=0, axis_index_groups=groups, tiled=True
        )

    requests, slots = prep(tile_map[:, :, 0], row_anchor, col_anchor, peers, 2, cap)
    asked = exchange(requests)
    side = (lax.axis_index("sky") // relays).astype(jnp.int32).reshape(1)
    received = []
    for plane in range(PLANES):
        windows = cut(plane, cap, side, asked, gradients, mirrors[plane])
        got = exchange(windows.reshape(relays, 2 * cap, 2 * WR, WC))
        received.append(got.reshape(peers * cap, 2 * WR, WC))
    state = (start_x, start_y)
    for plane in range(PLANES):
        state = interp(plane, slots, received[plane], state)
    return state


def solution(mesh):
    return jax.shard_map(
        body,
        mesh=mesh,
        in_specs=(
            P(("runs", "sky"), None),
            P(("runs", "sky"), None),
            P(None, None, ("runs", "sky"), None),
            P(None, ("runs", "sky"), None),
            P(None, ("runs", "sky")),
            P(None, ("runs", "sky")),
        ),
        out_specs=(P(("runs", "sky"), None, None), P(("runs", "sky"), None, None)),
        check_vma=False,
    )
```

```python
import functools

import jax
import jax.numpy as jnp
from jax import lax
from jax.experimental import pallas as pl
from jax.experimental.pallas import tpu as pltpu
from jax.sharding import PartitionSpec as P


WR = 16
WC = 128
PLANES = 3

lens_ratio = (0.85, 0.7, 0.9)
lens_strength = (0.5, 0.6, 0.45)

GRANT = pltpu.CompilerParams(vmem_limit_bytes=16 << 20)
VMEM = pltpu.VMEM
SMEM = pltpu.SMEM


def whole(space=VMEM):
    return pl.BlockSpec(memory_space=space)


def dot_last(a, b):
    return lax.dot_general(
        a, b, (((1,), (1,)), ((), ())), preferred_element_type=jnp.float32
    )


def prep_kernel(peers, halves, cap, tile_ref, row_ref, col_ref, req_ref, slot_ref):
    relays = peers // halves
    nblk = tile_ref.shape[1]
    lanes = req_ref.shape[1]
    owner = lax.broadcasted_iota(jnp.int32, (peers, nblk), 0)
    earlier = (
        lax.broadcasted_iota(jnp.int32, (nblk, nblk), 1)
        < lax.broadcasted_iota(jnp.int32, (nblk, nblk), 0)
    ).astype(jnp.float32).astype(jnp.bfloat16)
    lane = lax.broadcasted_iota(jnp.int32, (lanes, nblk), 0)
    rows = jnp.zeros((relays, lanes), jnp.float32)
    cols = jnp.zeros((relays, lanes), jnp.float32)
    for k in range(PLANES):
        tile = tile_ref[k : k + 1, :]
        hit = (owner == tile).astype(jnp.float32)
        hit16 = hit.astype(jnp.bfloat16)
        before = dot_last(hit16, earlier)
        rank = jnp.sum(before * hit, axis=0, keepdims=True).astype(jnp.int32)
        side = tile // relays
        rank = rank + side * cap
        slot_ref[k : k + 1, :] = (tile - side * relays) * (halves * cap) + rank
        here = lane == (rank + k * halves * cap)
        zero = jnp.zeros((), jnp.float32)
        row = jnp.where(here, row_ref[k : k + 1, :].astype(jnp.float32), zero)
        col = jnp.where(here, col_ref[k : k + 1, :].astype(jnp.float32), zero)
        fold = sum(hit[h * relays : (h + 1) * relays] for h in range(halves)).astype(jnp.bfloat16)
        rows += dot_last(fold, row.astype(jnp.bfloat16))
        cols += dot_last(fold, col.astype(jnp.bfloat16))
    req_ref[...] = rows.astype(jnp.int32) * 65536 + cols.astype(jnp.int32)


def prep(tile_map, row_anchor, col_anchor, peers, halves, cap):
    nblk = tile_map.shape[1]
    lanes = -(-PLANES * halves * cap // 128) * 128
    return pl.pallas_call(
        functools.partial(prep_kernel, peers, halves, cap),
        out_shape=(
            jax.ShapeDtypeStruct((peers // halves, lanes), jnp.int32),
            jax.ShapeDtypeStruct((PLANES, nblk), jnp.int32),
        ),
        in_specs=[whole()] * 3,
        out_specs=(whole(), whole()),
        name="prep",
    )(tile_map, row_anchor, col_anchor)


def cut_kernel(plane, cap, side_ref, req_ref, own_ref, mirror_ref, out_ref, half_ref):
    parts = own_ref.shape[3] // WC
    for c in range(2):
        for h in range(parts):
            lanes = slice(h * WC, (h + 1) * WC)
            half_ref[c * parts + h] = own_ref[plane, c, :, lanes].astype(jnp.float32)
            half_ref[(2 + c) * parts + h] = mirror_ref[c, :, lanes].astype(jnp.float32)
    lane = lax.broadcasted_iota(jnp.int32, (WR, WC), 1)
    side = side_ref[0]
    each = 2 * cap

    def one(source, carry):
        for place in range(each):
            packed = req_ref[source, plane * each + place]
            base = jnp.where(side == place // cap, 0, 2 * parts)
            row = packed >> 16
            col = packed & 65535
            turn = (WC - col) & (WC - 1)
            left = lane < WC - col
            for c in range(2):
                part = [
                    pltpu.roll(half_ref[base + c * parts + h, pl.ds(row, WR), :], turn, 1)
                    for h in range(parts)
                ]
                out_ref[source * each + place, c * WR : (c + 1) * WR, :] = jnp.where(
                    left, part[0], part[1]
                ).astype(jnp.bfloat16)
        return carry

    lax.fori_loop(0, req_ref.shape[0], one, 0)


def cut(plane, cap, side, requests, sheet, mirror):
    count = requests.shape[0] * 2 * cap
    return pl.pallas_call(
        functools.partial(cut_kernel, plane, cap),
        out_shape=jax.ShapeDtypeStruct((count, 2 * WR, WC), jnp.bfloat16),
        in_specs=[whole(SMEM), whole(SMEM), whole(), whole()],
        out_specs=whole(),
        scratch_shapes=[VMEM((4 * sheet.shape[3] // WC, sheet.shape[2], WC), jnp.float32)],
        compiler_params=GRANT,
    )(side, requests, sheet, mirror)


def taps(pos):
    cell = jnp.floor(pos)
    f = pos - cell
    g = 1.0 - f
    f2, g2 = f * f, g * g
    value = (
        g2 * g / 6.0,
        2.0 / 3.0 - f2 + 0.5 * f2 * f,
        2.0 / 3.0 - g2 + 0.5 * g2 * g,
        f2 * f / 6.0,
    )
    slope = (-0.5 * g2, -2.0 * f + 1.5 * f2, 2.0 * g - 1.5 * g2, 0.5 * f2)
    return cell, value, slope


def interp_kernel(plane, slot_ref, win_ref, *refs):
    first, last = plane == 0, plane == PLANES - 1
    if first:
        x_ref, y_ref = refs[:2]
        refs = refs[2:]
    else:
        state_ref = refs[0]
        refs = refs[1:]
    if last:
        pos_out, jac_out = refs[:2]
        refs = refs[2:]
    else:
        state_out = refs[0]
        refs = refs[1:]
    tap_ref, res_ref = refs
    nblk, rays = res_ref.shape[1:]

    if first:
        px, py = x_ref[...], y_ref[...]
    else:
        px, py = state_ref[0], state_ref[1]
    for at, pos in ((0, px), (9, py)):
        cell, value, slope = taps(pos)
        tap_ref[at] = jnp.clip(cell, -4.0, WC + 4.0)
        for j in range(4):
            tap_ref[at + 1 + j] = value[j]
            tap_ref[at + 5 + j] = slope[j]

    def one(b, carry):
        def row(j):
            return tap_ref[j, pl.ds(b, 1), :]

        def spread(at, size, dtype):
            tile = 8 * 4 // jnp.dtype(dtype).itemsize

            def lay(j):
                return jnp.broadcast_to(row(j), (tile, rays)).astype(dtype)[None]

            place = lax.broadcasted_iota(jnp.int32, (size // tile, tile, rays), 0) * tile
            place = (place + lax.broadcasted_iota(jnp.int32, place.shape, 1)).astype(jnp.float32)
            near = place.astype(dtype) - lay(at)
            value = jnp.zeros(near.shape, dtype)
            slope = value
            for j in range(4):
                here = near == jnp.asarray(j - 1, dtype)
                value = jnp.where(here, lay(at + 1 + j), value)
                slope = jnp.where(here, lay(at + 5 + j), slope)
            return value.reshape(size, rays), slope.reshape(size, rays)

        kern = jnp.concatenate(spread(0, WC, jnp.bfloat16), axis=1)
        mixed = jnp.dot(win_ref[slot_ref[plane, b]], kern, preferred_element_type=jnp.float32)
        ky, kyd = spread(9, WR, jnp.float32)
        for c in range(2):
            part = mixed[c * WR : (c + 1) * WR]
            mixed0, mixed1 = part[:, :rays], part[:, rays:]
            for at, product in ((0, ky * mixed0), (2, ky * mixed1), (4, kyd * mixed0)):
                res_ref[at + c, pl.ds(b, 1), :] = jnp.sum(product, axis=0, keepdims=True)
        return carry

    lax.fori_loop(0, nblk, one, 0, unroll=16)

    ratio, strength = lens_ratio[plane], lens_strength[plane]
    ax, ay = res_ref[0], res_ref[1]
    hxx, hyx, hxy, hyy = res_ref[2], res_ref[3], res_ref[4], res_ref[5]
    if first:
        vx, vy = -strength * ax, -strength * ay
        dj = [-strength * h for h in (hxx, hxy, hyx, hyy)]
        jac = [1.0 + dj[0], dj[1], dj[2], 1.0 + dj[3]]
    else:
        vx = ratio * state_ref[2] - strength * ax
        vy = ratio * state_ref[3] - strength * ay
        axx, axy, ayx, ayy = [state_ref[4 + j] for j in range(4)]
        product = (
            hxx * axx + hxy * ayx,
            hxx * axy + hxy * ayy,
            hyx * axx + hyy * ayx,
            hyx * axy + hyy * ayy,
        )
        dj = [ratio * state_ref[8 + j] - strength * product[j] for j in range(4)]
        jac = [old + d for old, d in zip((axx, axy, ayx, ayy), dj)]
    px, py = px + vx, py + vy
    if last:
        pos_out[:, 0, :] = px
        pos_out[:, 1, :] = py
        for j in range(4):
            jac_out[:, j, :] = jac[j]
    else:
        for j, value in enumerate([px, py, vx, vy] + jac + dj):
            state_out[j] = value


def interp(plane, slots, windows, state):
    nblk = slots.shape[1]
    rays = state[0].shape[-1]
    if plane == PLANES - 1:
        out_shape = (
            jax.ShapeDtypeStruct((nblk, 2, rays), jnp.float32),
            jax.ShapeDtypeStruct((nblk, 4, rays), jnp.float32),
        )
    else:
        out_shape = (jax.ShapeDtypeStruct((12, nblk, rays), jnp.float32),)
    return pl.pallas_call(
        functools.partial(interp_kernel, plane),
        out_shape=out_shape,
        in_specs=[whole(SMEM), whole()] + [whole()] * len(state),
        out_specs=(whole(),) * len(out_shape),
        scratch_shapes=[
            VMEM((18, nblk, rays), jnp.float32),
            VMEM((6, nblk, rays), jnp.float32),
        ],
        compiler_params=GRANT,
    )(slots, windows, *state)


def body(start_x, start_y, gradients, tile_map, row_anchor, col_anchor):
    peers = lax.axis_size("sky")
    nblk = start_x.shape[0]
    cap = max(2, 2 * nblk // peers)
    relays = peers // 2
    groups = [[h * relays + r for r in range(relays)] for h in range(2)]
    swap = [(i, (i + relays) % peers) for i in range(peers)]
    mirrors = []
    for plane in range(PLANES):
        mirrors.append(lax.ppermute(gradients[plane], "sky", swap))

    def exchange(x):
        return lax.all_to_all(
            x, "sky", split_axis=0, concat_axis=0, axis_index_groups=groups, tiled=True
        )

    requests, slots = prep(tile_map[:, :, 0], row_anchor, col_anchor, peers, 2, cap)
    asked = exchange(requests)
    side = (lax.axis_index("sky") // relays).astype(jnp.int32).reshape(1)
    received = []
    for plane in range(PLANES):
        windows = cut(plane, cap, side, asked, gradients, mirrors[plane])
        got = exchange(windows.reshape(relays, 2 * cap, 2 * WR, WC))
        received.append(got.reshape(peers * cap, 2 * WR, WC))
    state = (start_x, start_y)
    for plane in range(PLANES):
        state = interp(plane, slots, received[plane], state)
    return state


def solution(mesh):
    return jax.shard_map(
        body,
        mesh=mesh,
        in_specs=(
            P(("runs", "sky"), None),
            P(("runs", "sky"), None),
            P(None, None, ("runs", "sky"), None),
            P(None, ("runs", "sky"), None),
            P(None, ("runs", "sky")),
            P(None, ("runs", "sky")),
        ),
        out_specs=(P(("runs", "sky"), None, None), P(("runs", "sky"), None, None)),
        check_vma=False,
    )
```

```python
import functools

import jax
import jax.numpy as jnp
from jax import lax
from jax.experimental import pallas as pl
from jax.experimental.pallas import tpu as pltpu
from jax.sharding import PartitionSpec as P


WR = 16
WC = 128
PLANES = 3

lens_ratio = (0.85, 0.7, 0.9)
lens_strength = (0.5, 0.6, 0.45)

GRANT = pltpu.CompilerParams(vmem_limit_bytes=16 << 20)
VMEM = pltpu.VMEM
SMEM = pltpu.SMEM


def whole(space=VMEM):
    return pl.BlockSpec(memory_space=space)


def dot_last(a, b):
    return lax.dot_general(
        a, b, (((1,), (1,)), ((), ())), preferred_element_type=jnp.float32
    )


def prep_kernel(peers, halves, cap, direct, me_ref, tile_ref, row_ref, col_ref, req_ref, slot_ref):
    relays = peers // halves
    nblk = tile_ref.shape[1]
    lanes = req_ref.shape[1]
    owner = lax.broadcasted_iota(jnp.int32, (peers, nblk), 0)
    earlier = (
        lax.broadcasted_iota(jnp.int32, (nblk, nblk), 1)
        < lax.broadcasted_iota(jnp.int32, (nblk, nblk), 0)
    ).astype(jnp.float32).astype(jnp.bfloat16)
    lane = lax.broadcasted_iota(jnp.int32, (lanes, nblk), 0)
    rows = jnp.zeros((relays, lanes), jnp.float32)
    cols = jnp.zeros((relays, lanes), jnp.float32)
    for k in range(PLANES):
        tile = tile_ref[k : k + 1, :]
        hit = (owner == tile).astype(jnp.float32)
        hit16 = hit.astype(jnp.bfloat16)
        before = dot_last(hit16, earlier)
        rank = jnp.sum(before * hit, axis=0, keepdims=True).astype(jnp.int32)
        side = tile // relays
        rank = rank + side * cap
        relay = (tile - side * relays) ^ me_ref[0]
        if not direct:
            relay = (relay & 1) * (relays // 2) + (relay >> 1)
        slot_ref[k : k + 1, :] = relay * (halves * cap) + rank
        here = lane == (rank + k * halves * cap)
        zero = jnp.zeros((), jnp.float32)
        row = jnp.where(here, row_ref[k : k + 1, :].astype(jnp.float32), zero)
        col = jnp.where(here, col_ref[k : k + 1, :].astype(jnp.float32), zero)
        fold = sum(hit[h * relays : (h + 1) * relays] for h in range(halves)).astype(jnp.bfloat16)
        rows += dot_last(fold, row.astype(jnp.bfloat16))
        cols += dot_last(fold, col.astype(jnp.bfloat16))
    req_ref[...] = rows.astype(jnp.int32) * 65536 + cols.astype(jnp.int32)


def prep(me, tile_map, row_anchor, col_anchor, peers, halves, cap, direct):
    nblk = tile_map.shape[1]
    lanes = -(-PLANES * halves * cap // 128) * 128
    return pl.pallas_call(
        functools.partial(prep_kernel, peers, halves, cap, direct),
        out_shape=(
            jax.ShapeDtypeStruct((peers // halves, lanes), jnp.int32),
            jax.ShapeDtypeStruct((PLANES, nblk), jnp.int32),
        ),
        in_specs=[whole(SMEM)] + [whole()] * 3,
        out_specs=(whole(), whole()),
        name="prep",
    )(me, tile_map, row_anchor, col_anchor)


def cut_kernel(plane, cap, place_ref, req_ref, own_ref, mirror_ref, *refs):
    out_refs, half_ref = refs[:-1], refs[-1]
    parts = own_ref.shape[3] // WC
    for c in range(2):
        for h in range(parts):
            lanes = slice(h * WC, (h + 1) * WC)
            half_ref[c * parts + h] = own_ref[plane, c, :, lanes].astype(jnp.float32)
            half_ref[(2 + c) * parts + h] = mirror_ref[c, :, lanes].astype(jnp.float32)
    lane = lax.broadcasted_iota(jnp.int32, (WR, WC), 1)
    side, me = place_ref[0], place_ref[1]
    each = 2 * cap
    span = req_ref.shape[0] // len(out_refs)

    def one(at, carry):
        for m, out_ref in enumerate(out_refs):
            source = (m * span + at) ^ me
            for place in range(each):
                packed = req_ref[source, plane * each + place]
                base = jnp.where(side == place // cap, 0, 2 * parts)
                row = packed >> 16
                col = packed & 65535
                turn = (WC - col) & (WC - 1)
                left = lane < WC - col
                for c in range(2):
                    part = [
                        pltpu.roll(half_ref[base + c * parts + h, pl.ds(row, WR), :], turn, 1)
                        for h in range(parts)
                    ]
                    out_ref[at * each + place, c * WR : (c + 1) * WR, :] = jnp.where(
                        left, part[0], part[1]
                    ).astype(jnp.bfloat16)
        return carry

    lax.fori_loop(0, span, one, 0)


def cut(plane, cap, outs, place, requests, sheet, mirror):
    count = requests.shape[0] // outs * 2 * cap
    return pl.pallas_call(
        functools.partial(cut_kernel, plane, cap),
        out_shape=(jax.ShapeDtypeStruct((count, 2 * WR, WC), jnp.bfloat16),) * outs,
        in_specs=[whole(SMEM), whole(SMEM), whole(), whole()],
        out_specs=(whole(),) * outs,
        scratch_shapes=[VMEM((4 * sheet.shape[3] // WC, sheet.shape[2], WC), jnp.float32)],
        compiler_params=GRANT,
    )(place, requests, sheet, mirror)


def taps(pos):
    cell = jnp.floor(pos)
    f = pos - cell
    g = 1.0 - f
    f2, g2 = f * f, g * g
    value = (
        g2 * g / 6.0,
        2.0 / 3.0 - f2 + 0.5 * f2 * f,
        2.0 / 3.0 - g2 + 0.5 * g2 * g,
        f2 * f / 6.0,
    )
    slope = (-0.5 * g2, -2.0 * f + 1.5 * f2, 2.0 * g - 1.5 * g2, 0.5 * f2)
    return cell, value, slope


def interp_kernel(plane, slot_ref, win_ref, *refs):
    first, last = plane == 0, plane == PLANES - 1
    if first:
        x_ref, y_ref = refs[:2]
        refs = refs[2:]
    else:
        state_ref = refs[0]
        refs = refs[1:]
    if last:
        pos_out, jac_out = refs[:2]
        refs = refs[2:]
    else:
        state_out = refs[0]
        refs = refs[1:]
    tap_ref, res_ref = refs
    nblk, rays = res_ref.shape[1:]

    if first:
        px, py = x_ref[...], y_ref[...]
    else:
        px, py = state_ref[0], state_ref[1]
    for at, pos in ((0, px), (9, py)):
        cell, value, slope = taps(pos)
        tap_ref[at] = jnp.clip(cell, -4.0, WC + 4.0)
        for j in range(4):
            tap_ref[at + 1 + j] = value[j]
            tap_ref[at + 5 + j] = slope[j]

    def one(b, carry):
        def row(j):
            return tap_ref[j, pl.ds(b, 1), :]

        def spread(at, size, dtype):
            tile = 8 * 4 // jnp.dtype(dtype).itemsize

            def lay(j):
                return jnp.broadcast_to(row(j), (tile, rays)).astype(dtype)[None]

            place = lax.broadcasted_iota(jnp.int32, (size // tile, tile, rays), 0) * tile
            place = (place + lax.broadcasted_iota(jnp.int32, place.shape, 1)).astype(jnp.float32)
            near = place.astype(dtype) - lay(at)
            value = jnp.zeros(near.shape, dtype)
            slope = value
            for j in range(4):
                here = near == jnp.asarray(j - 1, dtype)
                value = jnp.where(here, lay(at + 1 + j), value)
                slope = jnp.where(here, lay(at + 5 + j), slope)
            return value.reshape(size, rays), slope.reshape(size, rays)

        kern = jnp.concatenate(spread(0, WC, jnp.bfloat16), axis=1)
        mixed = jnp.dot(win_ref[slot_ref[plane, b]], kern, preferred_element_type=jnp.float32)
        ky, kyd = spread(9, WR, jnp.float32)
        for c in range(2):
            part = mixed[c * WR : (c + 1) * WR]
            mixed0, mixed1 = part[:, :rays], part[:, rays:]
            for at, product in ((0, ky * mixed0), (2, ky * mixed1), (4, kyd * mixed0)):
                res_ref[at + c, pl.ds(b, 1), :] = jnp.sum(product, axis=0, keepdims=True)
        return carry

    lax.fori_loop(0, nblk, one, 0, unroll=16)

    ratio, strength = lens_ratio[plane], lens_strength[plane]
    ax, ay = res_ref[0], res_ref[1]
    hxx, hyx, hxy, hyy = res_ref[2], res_ref[3], res_ref[4], res_ref[5]
    if first:
        vx, vy = -strength * ax, -strength * ay
        dj = [-strength * h for h in (hxx, hxy, hyx, hyy)]
        jac = [1.0 + dj[0], dj[1], dj[2], 1.0 + dj[3]]
    else:
        vx = ratio * state_ref[2] - strength * ax
        vy = ratio * state_ref[3] - strength * ay
        axx, axy, ayx, ayy = [state_ref[4 + j] for j in range(4)]
        product = (
            hxx * axx + hxy * ayx,
            hxx * axy + hxy * ayy,
            hyx * axx + hyy * ayx,
            hyx * axy + hyy * ayy,
        )
        dj = [ratio * state_ref[8 + j] - strength * product[j] for j in range(4)]
        jac = [old + d for old, d in zip((axx, axy, ayx, ayy), dj)]
    px, py = px + vx, py + vy
    if last:
        pos_out[:, 0, :] = px
        pos_out[:, 1, :] = py
        for j in range(4):
            jac_out[:, j, :] = jac[j]
    else:
        for j, value in enumerate([px, py, vx, vy] + jac + dj):
            state_out[j] = value


def interp(plane, slots, windows, state):
    nblk = slots.shape[1]
    rays = state[0].shape[-1]
    if plane == PLANES - 1:
        out_shape = (
            jax.ShapeDtypeStruct((nblk, 2, rays), jnp.float32),
            jax.ShapeDtypeStruct((nblk, 4, rays), jnp.float32),
        )
    else:
        out_shape = (jax.ShapeDtypeStruct((12, nblk, rays), jnp.float32),)
    return pl.pallas_call(
        functools.partial(interp_kernel, plane),
        out_shape=out_shape,
        in_specs=[whole(SMEM), whole()] + [whole()] * len(state),
        out_specs=(whole(),) * len(out_shape),
        scratch_shapes=[
            VMEM((18, nblk, rays), jnp.float32),
            VMEM((6, nblk, rays), jnp.float32),
        ],
        compiler_params=GRANT,
    )(slots, windows, *state)


def body(start_x, start_y, gradients, tile_map, row_anchor, col_anchor):
    peers = lax.axis_size("sky")
    nblk = start_x.shape[0]
    cap = max(2, 2 * nblk // peers)
    relays = peers // 2
    chips = relays // 2
    direct = chips > 4 or chips & (chips - 1) != 0
    groups = [[h * relays + r for r in range(relays)] for h in range(2)]

    def swap(bits):
        return [(i, i ^ bits) for i in range(peers)]

    mirror_pairs = [(i, (i + relays) % peers) for i in range(peers)]
    mirrors = []
    for plane in range(PLANES):
        mirrors.append(lax.ppermute(gradients[plane], "sky", mirror_pairs))

    def exchange(x):
        return lax.all_to_all(
            x, "sky", split_axis=0, concat_axis=0, axis_index_groups=groups, tiled=True
        )

    def send(outs):
        if direct:
            got = exchange(outs[0].reshape(relays, 2 * cap, 2 * WR, WC))
            return got.reshape(peers * cap, 2 * WR, WC)
        got = [outs[0]]
        for m in range(1, chips):
            got.append(lax.ppermute(outs[m], "sky", swap(2 * m)))
        mine = [part[: 2 * cap] for part in got]
        other = jnp.concatenate([part[2 * cap :] for part in got], axis=0)
        other = lax.ppermute(other, "sky", swap(1))
        return jnp.concatenate(mine + [other], axis=0)

    index = lax.axis_index("sky").astype(jnp.int32)
    me = jnp.zeros_like(index) if direct else index % relays
    place = jnp.stack([index // relays, me])
    requests, slots = prep(
        me.reshape(1), tile_map[:, :, 0], row_anchor, col_anchor, peers, 2, cap, direct
    )
    asked = exchange(requests)
    received = []
    for plane in range(PLANES):
        outs = cut(plane, cap, 1 if direct else chips, place, asked, gradients, mirrors[plane])
        received.append(send(outs))
    state = (start_x, start_y)
    for plane in range(PLANES):
        state = interp(plane, slots, received[plane], state)
    return state


def solution(mesh):
    return jax.shard_map(
        body,
        mesh=mesh,
        in_specs=(
            P(("runs", "sky"), None),
            P(("runs", "sky"), None),
            P(None, None, ("runs", "sky"), None),
            P(None, ("runs", "sky"), None),
            P(None, ("runs", "sky")),
            P(None, ("runs", "sky")),
        ),
        out_specs=(P(("runs", "sky"), None, None), P(("runs", "sky"), None, None)),
        check_vma=False,
    )
```

```python
import functools

import jax
import jax.numpy as jnp
from jax import lax
from jax.experimental import pallas as pl
from jax.experimental.pallas import tpu as pltpu
from jax.sharding import PartitionSpec as P


WR = 16
WC = 128
PLANES = 3

lens_ratio = (0.85, 0.7, 0.9)
lens_strength = (0.5, 0.6, 0.45)

GRANT = pltpu.CompilerParams(vmem_limit_bytes=16 << 20)
VMEM = pltpu.VMEM
SMEM = pltpu.SMEM


def whole(space=VMEM):
    return pl.BlockSpec(memory_space=space)


def dot_last(a, b):
    return lax.dot_general(
        a, b, (((1,), (1,)), ((), ())), preferred_element_type=jnp.float32
    )


def ranks(peers, tile_ref, plane):
    nblk = tile_ref.shape[2]
    tile = tile_ref[plane]
    hit = (lax.broadcasted_iota(jnp.int32, (peers, nblk), 0) == tile).astype(jnp.float32)
    earlier = (
        lax.broadcasted_iota(jnp.int32, (nblk, nblk), 1)
        < lax.broadcasted_iota(jnp.int32, (nblk, nblk), 0)
    ).astype(jnp.float32).astype(jnp.bfloat16)
    before = dot_last(hit.astype(jnp.bfloat16), earlier)
    return tile, hit, jnp.sum(before * hit, axis=0, keepdims=True).astype(jnp.int32)


def want_kernel(peers, cap, tile_ref, row_ref, col_ref, req_ref):
    nblk = tile_ref.shape[2]
    relays, lanes = req_ref.shape
    lane = lax.broadcasted_iota(jnp.int32, (lanes, nblk), 0)
    rows = jnp.zeros((relays, lanes), jnp.float32)
    cols = jnp.zeros((relays, lanes), jnp.float32)
    for k in range(PLANES):
        tile, hit, rank = ranks(peers, tile_ref, k)
        here = lane == (rank + (tile // relays + 2 * k) * cap)
        zero = jnp.zeros((), jnp.float32)
        row = jnp.where(here, row_ref[k : k + 1, :].astype(jnp.float32), zero)
        col = jnp.where(here, col_ref[k : k + 1, :].astype(jnp.float32), zero)
        fold = (hit[:relays] + hit[relays:]).astype(jnp.bfloat16)
        rows += dot_last(fold, row.astype(jnp.bfloat16))
        cols += dot_last(fold, col.astype(jnp.bfloat16))
    req_ref[...] = rows.astype(jnp.int32) * 65536 + cols.astype(jnp.int32)


def want(tile_map, row_anchor, col_anchor, peers, cap):
    lanes = -(-PLANES * 2 * cap // 128) * 128
    return pl.pallas_call(
        functools.partial(want_kernel, peers, cap),
        out_shape=jax.ShapeDtypeStruct((peers // 2, lanes), jnp.int32),
        in_specs=[whole()] * 3,
        out_specs=whole(),
        name="want",
    )(tile_map, row_anchor, col_anchor)


def slot_kernel(peers, cap, direct, place_ref, tile_ref, slot_ref):
    relays = peers // 2
    for k in range(PLANES):
        tile, _, rank = ranks(peers, tile_ref, k)
        side = tile // relays
        relay = (tile - side * relays) ^ place_ref[1]
        if not direct:
            relay = (relay & 1) * (relays // 2) + (relay >> 1)
        far = (side != place_ref[0]).astype(jnp.int32)
        slot_ref[k : k + 1, :] = (far * relays + relay) * cap + rank


def find_slots(place, tile_map, peers, cap, direct):
    return pl.pallas_call(
        functools.partial(slot_kernel, peers, cap, direct),
        out_shape=jax.ShapeDtypeStruct((PLANES, tile_map.shape[2]), jnp.int32),
        in_specs=[whole(SMEM), whole()],
        out_specs=whole(),
        name="slots",
    )(place, tile_map)


def cut_kernel(planes, cap, mirrored, place_ref, req_ref, sheet_ref, *refs):
    out_refs, half_ref = refs[:-1], refs[-1]
    parts = sheet_ref.shape[-1] // WC
    for at, k in enumerate(planes):
        for c in range(2):
            for h in range(parts):
                lanes = slice(h * WC, (h + 1) * WC)
                part = sheet_ref[c, :, lanes] if mirrored else sheet_ref[k, c, :, lanes]
                half_ref[(at * 2 + c) * parts + h] = part.astype(jnp.float32)
    lane = lax.broadcasted_iota(jnp.int32, (WR, WC), 1)
    me = place_ref[1]
    side = 1 - place_ref[0] if mirrored else place_ref[0]
    span = req_ref.shape[0] // len(out_refs)

    def one(now, carry):
        for m, out_ref in enumerate(out_refs):
            source = (m * span + now) ^ me
            for at, k in enumerate(planes):
                for place in range(cap):
                    packed = req_ref[source, (2 * k + side) * cap + place]
                    row = packed >> 16
                    col = packed & 65535
                    turn = (WC - col) & (WC - 1)
                    left = lane < WC - col
                    slot = (now * len(planes) + at) * cap + place
                    for c in range(2):
                        part = [
                            pltpu.roll(half_ref[(at * 2 + c) * parts + h, pl.ds(row, WR), :], turn, 1)
                            for h in range(parts)
                        ]
                        out_ref[slot, c * WR : (c + 1) * WR, :] = jnp.where(
                            left, part[0], part[1]
                        ).astype(jnp.bfloat16)
        return carry

    lax.fori_loop(0, span, one, 0)


def cut(planes, cap, outs, place, requests, sheet):
    mirrored = sheet.ndim == 3
    count = requests.shape[0] // outs * len(planes) * cap
    height, width = sheet.shape[-2:]
    return pl.pallas_call(
        functools.partial(cut_kernel, planes, cap, mirrored),
        out_shape=(jax.ShapeDtypeStruct((count, 2 * WR, WC), jnp.bfloat16),) * outs,
        in_specs=[whole(SMEM), whole(SMEM), whole()],
        out_specs=(whole(),) * outs,
        scratch_shapes=[VMEM((len(planes) * 2 * width // WC, height, WC), jnp.float32)],
        compiler_params=GRANT,
        name="cut",
    )(place, requests, sheet)


def taps(pos):
    cell = jnp.floor(pos)
    f = pos - cell
    g = 1.0 - f
    f2, g2 = f * f, g * g
    value = (
        g2 * g / 6.0,
        2.0 / 3.0 - f2 + 0.5 * f2 * f,
        2.0 / 3.0 - g2 + 0.5 * g2 * g,
        f2 * f / 6.0,
    )
    slope = (-0.5 * g2, -2.0 * f + 1.5 * f2, 2.0 * g - 1.5 * g2, 0.5 * f2)
    return cell, value, slope


def interp_kernel(plane, slot_ref, win_ref, *refs):
    first, last = plane == 0, plane == PLANES - 1
    if first:
        x_ref, y_ref = refs[:2]
        refs = refs[2:]
    else:
        state_ref = refs[0]
        refs = refs[1:]
    if last:
        pos_out, jac_out = refs[:2]
        refs = refs[2:]
    else:
        state_out = refs[0]
        refs = refs[1:]
    tap_ref, res_ref = refs
    nblk, rays = res_ref.shape[1:]

    if first:
        px, py = x_ref[...], y_ref[...]
    else:
        px, py = state_ref[0], state_ref[1]
    for at, pos in ((0, px), (9, py)):
        cell, value, slope = taps(pos)
        tap_ref[at] = jnp.clip(cell, -4.0, WC + 4.0)
        for j in range(4):
            tap_ref[at + 1 + j] = value[j]
            tap_ref[at + 5 + j] = slope[j]

    def one(b, carry):
        def row(j):
            return tap_ref[j, pl.ds(b, 1), :]

        def spread(at, size, dtype):
            tile = 8 * 4 // jnp.dtype(dtype).itemsize

            def lay(j):
                return jnp.broadcast_to(row(j), (tile, rays)).astype(dtype)[None]

            place = lax.broadcasted_iota(jnp.int32, (size // tile, tile, rays), 0) * tile
            place = (place + lax.broadcasted_iota(jnp.int32, place.shape, 1)).astype(jnp.float32)
            near = place.astype(dtype) - lay(at)
            value = jnp.zeros(near.shape, dtype)
            slope = value
            for j in range(4):
                here = near == jnp.asarray(j - 1, dtype)
                value = jnp.where(here, lay(at + 1 + j), value)
                slope = jnp.where(here, lay(at + 5 + j), slope)
            return value.reshape(size, rays), slope.reshape(size, rays)

        kern = jnp.concatenate(spread(0, WC, jnp.bfloat16), axis=1)
        mixed = jnp.dot(win_ref[slot_ref[plane, b]], kern, preferred_element_type=jnp.float32)
        ky, kyd = spread(9, WR, jnp.float32)
        for c in range(2):
            part = mixed[c * WR : (c + 1) * WR]
            mixed0, mixed1 = part[:, :rays], part[:, rays:]
            for at, product in ((0, ky * mixed0), (2, ky * mixed1), (4, kyd * mixed0)):
                res_ref[at + c, pl.ds(b, 1), :] = jnp.sum(product, axis=0, keepdims=True)
        return carry

    lax.fori_loop(0, nblk, one, 0, unroll=16)

    ratio, strength = lens_ratio[plane], lens_strength[plane]
    ax, ay = res_ref[0], res_ref[1]
    hxx, hyx, hxy, hyy = res_ref[2], res_ref[3], res_ref[4], res_ref[5]
    if first:
        vx, vy = -strength * ax, -strength * ay
        dj = [-strength * h for h in (hxx, hxy, hyx, hyy)]
        jac = [1.0 + dj[0], dj[1], dj[2], 1.0 + dj[3]]
    else:
        vx = ratio * state_ref[2] - strength * ax
        vy = ratio * state_ref[3] - strength * ay
        axx, axy, ayx, ayy = [state_ref[4 + j] for j in range(4)]
        product = (
            hxx * axx + hxy * ayx,
            hxx * axy + hxy * ayy,
            hyx * axx + hyy * ayx,
            hyx * axy + hyy * ayy,
        )
        dj = [ratio * state_ref[8 + j] - strength * product[j] for j in range(4)]
        jac = [old + d for old, d in zip((axx, axy, ayx, ayy), dj)]
    px, py = px + vx, py + vy
    if last:
        pos_out[:, 0, :] = px
        pos_out[:, 1, :] = py
        for j in range(4):
            jac_out[:, j, :] = jac[j]
    else:
        for j, value in enumerate([px, py, vx, vy] + jac + dj):
            state_out[j] = value


def interp(plane, slots, windows, state):
    nblk = slots.shape[1]
    rays = state[0].shape[-1]
    if plane == PLANES - 1:
        out_shape = (
            jax.ShapeDtypeStruct((nblk, 2, rays), jnp.float32),
            jax.ShapeDtypeStruct((nblk, 4, rays), jnp.float32),
        )
    else:
        out_shape = (jax.ShapeDtypeStruct((12, nblk, rays), jnp.float32),)
    return pl.pallas_call(
        functools.partial(interp_kernel, plane),
        out_shape=out_shape,
        in_specs=[whole(SMEM), whole()] + [whole()] * len(state),
        out_specs=(whole(),) * len(out_shape),
        scratch_shapes=[
            VMEM((18, nblk, rays), jnp.float32),
            VMEM((6, nblk, rays), jnp.float32),
        ],
        compiler_params=GRANT,
    )(slots, windows, *state)


def body(start_x, start_y, gradients, tile_map, row_anchor, col_anchor):
    peers = lax.axis_size("sky")
    nblk = start_x.shape[0]
    cap = max(2, 2 * nblk // peers)
    relays = peers // 2
    chips = relays // 2
    direct = chips > 4 or chips & (chips - 1) != 0
    outs = 1 if direct else chips
    groups = [[h * relays + r for r in range(relays)] for h in range(2)]
    mirror_pairs = [(i, (i + relays) % peers) for i in range(peers)]

    def swap(bits):
        return [(i, i ^ bits) for i in range(peers)]

    def exchange(x):
        return lax.all_to_all(
            x, "sky", split_axis=0, concat_axis=0, axis_index_groups=groups, tiled=True
        )

    def ship(parts):
        if direct:
            return exchange(parts[0].reshape(relays, -1, 2 * WR, WC))
        got = [parts[0]]
        for m in range(1, chips):
            got.append(lax.ppermute(parts[m], "sky", swap(2 * m)))
        half = parts[0].shape[0] // 2
        mine = [part[:half] for part in got]
        other = jnp.concatenate([part[half:] for part in got], axis=0)
        other = lax.ppermute(other, "sky", swap(1))
        return jnp.concatenate(mine + [other], axis=0).reshape(relays, -1, 2 * WR, WC)

    mirrors = []
    for plane in range(PLANES):
        mirrors.append(lax.ppermute(gradients[plane], "sky", mirror_pairs))
    index = lax.axis_index("sky").astype(jnp.int32)
    place = jnp.stack([index // relays, jnp.zeros_like(index) if direct else index % relays])
    tiles = tile_map.transpose(0, 2, 1)
    requests = want(tiles, row_anchor, col_anchor, peers, cap)
    asked = exchange(requests)
    slots = find_slots(place, tiles, peers, cap, direct)
    parts = cut(tuple(range(PLANES)), cap, outs, place, asked, gradients)
    own = ship(parts).reshape(relays, PLANES, cap, 2 * WR, WC)
    windows = []
    for plane in range(PLANES):
        parts = cut((plane,), cap, outs, place, asked, mirrors[plane])
        far = ship(parts)
        both = [x.reshape(relays * cap, 2 * WR, WC) for x in (own[:, plane], far)]
        windows.append(jnp.concatenate(both, axis=0))
    state = (start_x, start_y)
    for plane in range(PLANES):
        state = interp(plane, slots, windows[plane], state)
    return state


def solution(mesh):
    return jax.shard_map(
        body,
        mesh=mesh,
        in_specs=(
            P(("runs", "sky"), None),
            P(("runs", "sky"), None),
            P(None, None, ("runs", "sky"), None),
            P(None, ("runs", "sky"), None),
            P(None, ("runs", "sky")),
            P(None, ("runs", "sky")),
        ),
        out_specs=(P(("runs", "sky"), None, None), P(("runs", "sky"), None, None)),
        check_vma=False,
    )
```

```python
import functools

import jax
import jax.numpy as jnp
from jax import lax
from jax.experimental import pallas as pl
from jax.experimental.pallas import tpu as pltpu
from jax.sharding import PartitionSpec as P


WR = 16
WC = 128
PLANES = 3

lens_ratio = (0.85, 0.7, 0.9)
lens_strength = (0.5, 0.6, 0.45)

GRANT = pltpu.CompilerParams(vmem_limit_bytes=16 << 20)
VMEM = pltpu.VMEM
SMEM = pltpu.SMEM


def whole(space=VMEM):
    return pl.BlockSpec(memory_space=space)


def dot_last(a, b):
    return lax.dot_general(
        a, b, (((1,), (1,)), ((), ())), preferred_element_type=jnp.float32
    )


def ranks(peers, tile_ref, plane):
    nblk = tile_ref.shape[2]
    tile = tile_ref[plane]
    hit = (lax.broadcasted_iota(jnp.int32, (peers, nblk), 0) == tile).astype(jnp.float32)
    earlier = (
        lax.broadcasted_iota(jnp.int32, (nblk, nblk), 1)
        < lax.broadcasted_iota(jnp.int32, (nblk, nblk), 0)
    ).astype(jnp.float32).astype(jnp.bfloat16)
    before = dot_last(hit.astype(jnp.bfloat16), earlier)
    return tile, hit, jnp.sum(before * hit, axis=0, keepdims=True).astype(jnp.int32)


def want_kernel(peers, cap, tile_ref, row_ref, col_ref, req_ref):
    nblk = tile_ref.shape[2]
    relays, lanes = req_ref.shape
    lane = lax.broadcasted_iota(jnp.int32, (lanes, nblk), 0)
    rows = jnp.zeros((relays, lanes), jnp.float32)
    cols = jnp.zeros((relays, lanes), jnp.float32)
    for k in range(PLANES):
        tile, hit, rank = ranks(peers, tile_ref, k)
        here = lane == (rank + (tile // relays + 2 * k) * cap)
        zero = jnp.zeros((), jnp.float32)
        row = jnp.where(here, row_ref[k : k + 1, :].astype(jnp.float32), zero)
        col = jnp.where(here, col_ref[k : k + 1, :].astype(jnp.float32), zero)
        fold = (hit[:relays] + hit[relays:]).astype(jnp.bfloat16)
        rows += dot_last(fold, row.astype(jnp.bfloat16))
        cols += dot_last(fold, col.astype(jnp.bfloat16))
    req_ref[...] = rows.astype(jnp.int32) * 65536 + cols.astype(jnp.int32)


def want(tile_map, row_anchor, col_anchor, peers, cap):
    lanes = -(-PLANES * 2 * cap // 128) * 128
    return pl.pallas_call(
        functools.partial(want_kernel, peers, cap),
        out_shape=jax.ShapeDtypeStruct((peers // 2, lanes), jnp.int32),
        in_specs=[whole()] * 3,
        out_specs=whole(),
        name="want",
    )(tile_map, row_anchor, col_anchor)


def slot_kernel(peers, cap, direct, place_ref, tile_ref, slot_ref):
    relays = peers // 2
    for k in range(PLANES):
        tile, _, rank = ranks(peers, tile_ref, k)
        side = tile // relays
        relay = (tile - side * relays) ^ place_ref[1]
        if not direct:
            relay = (relay & 1) * (relays // 2) + (relay >> 1)
        far = (side != place_ref[0]).astype(jnp.int32)
        slot_ref[k : k + 1, :] = (far * relays + relay) * cap + rank


def find_slots(place, tile_map, peers, cap, direct):
    return pl.pallas_call(
        functools.partial(slot_kernel, peers, cap, direct),
        out_shape=jax.ShapeDtypeStruct((PLANES, tile_map.shape[2]), jnp.int32),
        in_specs=[whole(SMEM), whole()],
        out_specs=whole(),
        compiler_params=GRANT,
        name="slots",
    )(place, tile_map)


def cut_kernel(planes, cap, mirrored, place_ref, req_ref, sheet_ref, *refs):
    out_refs, half_ref = refs[:-1], refs[-1]
    parts = sheet_ref.shape[-1] // WC
    for at, k in enumerate(planes):
        for c in range(2):
            for h in range(parts):
                lanes = slice(h * WC, (h + 1) * WC)
                part = sheet_ref[c, :, lanes] if mirrored else sheet_ref[k, c, :, lanes]
                half_ref[(at * 2 + c) * parts + h] = part.astype(jnp.float32)
    lane = lax.broadcasted_iota(jnp.int32, (WR, WC), 1)
    me = place_ref[1]
    side = 1 - place_ref[0] if mirrored else place_ref[0]
    span = req_ref.shape[0] // len(out_refs)

    def one(now, carry):
        for m, out_ref in enumerate(out_refs):
            source = (m * span + now) ^ me
            for at, k in enumerate(planes):
                for place in range(cap):
                    packed = req_ref[source, (2 * k + side) * cap + place]
                    row = packed >> 16
                    col = packed & 65535
                    turn = (WC - col) & (WC - 1)
                    left = lane < WC - col
                    slot = (now * len(planes) + at) * cap + place
                    for c in range(2):
                        part = [
                            pltpu.roll(half_ref[(at * 2 + c) * parts + h, pl.ds(row, WR), :], turn, 1)
                            for h in range(parts)
                        ]
                        out_ref[slot, c * WR : (c + 1) * WR, :] = jnp.where(
                            left, part[0], part[1]
                        ).astype(jnp.bfloat16)
        return carry

    lax.fori_loop(0, span, one, 0)


def cut(planes, cap, outs, place, requests, sheet):
    mirrored = sheet.ndim == 3
    count = requests.shape[0] // outs * len(planes) * cap
    height, width = sheet.shape[-2:]
    return pl.pallas_call(
        functools.partial(cut_kernel, planes, cap, mirrored),
        out_shape=(jax.ShapeDtypeStruct((count, 2 * WR, WC), jnp.bfloat16),) * outs,
        in_specs=[whole(SMEM), whole(SMEM), whole()],
        out_specs=(whole(),) * outs,
        scratch_shapes=[VMEM((len(planes) * 2 * width // WC, height, WC), jnp.float32)],
        compiler_params=GRANT,
        name="cut",
    )(place, requests, sheet)


def taps(pos):
    cell = jnp.floor(pos)
    f = pos - cell
    g = 1.0 - f
    f2, g2 = f * f, g * g
    value = (
        g2 * g / 6.0,
        2.0 / 3.0 - f2 + 0.5 * f2 * f,
        2.0 / 3.0 - g2 + 0.5 * g2 * g,
        f2 * f / 6.0,
    )
    slope = (-0.5 * g2, -2.0 * f + 1.5 * f2, 2.0 * g - 1.5 * g2, 0.5 * f2)
    return cell, value, slope


def interp_kernel(plane, slot_ref, win_ref, *refs):
    first, last = plane == 0, plane == PLANES - 1
    if first:
        x_ref, y_ref = refs[:2]
        refs = refs[2:]
    else:
        state_ref = refs[0]
        refs = refs[1:]
    if last:
        pos_out, jac_out = refs[:2]
        refs = refs[2:]
    else:
        state_out = refs[0]
        refs = refs[1:]
    tap_ref, res_ref = refs
    nblk, rays = res_ref.shape[1:]

    if first:
        px, py = x_ref[...], y_ref[...]
    else:
        px, py = state_ref[0], state_ref[1]
    for at, pos in ((0, px), (9, py)):
        cell, value, slope = taps(pos)
        tap_ref[at] = jnp.clip(cell, -4.0, WC + 4.0)
        for j in range(4):
            tap_ref[at + 1 + j] = value[j]
            tap_ref[at + 5 + j] = slope[j]

    def one(b, carry):
        def row(j):
            return tap_ref[j, pl.ds(b, 1), :]

        def spread(at, size, dtype):
            tile = 8 * 4 // jnp.dtype(dtype).itemsize

            def lay(j):
                return jnp.broadcast_to(row(j), (tile, rays)).astype(dtype)[None]

            place = lax.broadcasted_iota(jnp.int32, (size // tile, tile, rays), 0) * tile
            place = (place + lax.broadcasted_iota(jnp.int32, place.shape, 1)).astype(jnp.float32)
            near = place.astype(dtype) - lay(at)
            value = jnp.zeros(near.shape, dtype)
            slope = value
            for j in range(4):
                here = near == jnp.asarray(j - 1, dtype)
                value = jnp.where(here, lay(at + 1 + j), value)
                slope = jnp.where(here, lay(at + 5 + j), slope)
            return value.reshape(size, rays), slope.reshape(size, rays)

        kern = jnp.concatenate(spread(0, WC, jnp.bfloat16), axis=1)
        mixed = jnp.dot(win_ref[slot_ref[plane, b]], kern, preferred_element_type=jnp.float32)
        ky, kyd = spread(9, WR, jnp.float32)
        for c in range(2):
            part = mixed[c * WR : (c + 1) * WR]
            mixed0, mixed1 = part[:, :rays], part[:, rays:]
            for at, product in ((0, ky * mixed0), (2, ky * mixed1), (4, kyd * mixed0)):
                res_ref[at + c, pl.ds(b, 1), :] = jnp.sum(product, axis=0, keepdims=True)
        return carry

    lax.fori_loop(0, nblk, one, 0, unroll=16)

    ratio, strength = lens_ratio[plane], lens_strength[plane]
    ax, ay = res_ref[0], res_ref[1]
    hxx, hyx, hxy, hyy = res_ref[2], res_ref[3], res_ref[4], res_ref[5]
    if first:
        vx, vy = -strength * ax, -strength * ay
        dj = [-strength * h for h in (hxx, hxy, hyx, hyy)]
        jac = [1.0 + dj[0], dj[1], dj[2], 1.0 + dj[3]]
    else:
        vx = ratio * state_ref[2] - strength * ax
        vy = ratio * state_ref[3] - strength * ay
        axx, axy, ayx, ayy = [state_ref[4 + j] for j in range(4)]
        product = (
            hxx * axx + hxy * ayx,
            hxx * axy + hxy * ayy,
            hyx * axx + hyy * ayx,
            hyx * axy + hyy * ayy,
        )
        dj = [ratio * state_ref[8 + j] - strength * product[j] for j in range(4)]
        jac = [old + d for old, d in zip((axx, axy, ayx, ayy), dj)]
    px, py = px + vx, py + vy
    if last:
        pos_out[:, 0, :] = px
        pos_out[:, 1, :] = py
        for j in range(4):
            jac_out[:, j, :] = jac[j]
    else:
        for j, value in enumerate([px, py, vx, vy] + jac + dj):
            state_out[j] = value


def interp(plane, slots, windows, state):
    nblk = slots.shape[1]
    rays = state[0].shape[-1]
    if plane == PLANES - 1:
        out_shape = (
            jax.ShapeDtypeStruct((nblk, 2, rays), jnp.float32),
            jax.ShapeDtypeStruct((nblk, 4, rays), jnp.float32),
        )
    else:
        out_shape = (jax.ShapeDtypeStruct((12, nblk, rays), jnp.float32),)
    return pl.pallas_call(
        functools.partial(interp_kernel, plane),
        out_shape=out_shape,
        in_specs=[whole(SMEM), whole()] + [whole()] * len(state),
        out_specs=(whole(),) * len(out_shape),
        scratch_shapes=[
            VMEM((18, nblk, rays), jnp.float32),
            VMEM((6, nblk, rays), jnp.float32),
        ],
        compiler_params=GRANT,
    )(slots, windows, *state)


def body(start_x, start_y, gradients, tile_map, row_anchor, col_anchor):
    peers = lax.axis_size("sky")
    nblk = start_x.shape[0]
    cap = max(2, 2 * nblk // peers)
    relays = peers // 2
    chips = relays // 2
    direct = chips > 4 or chips & (chips - 1) != 0
    outs = 1 if direct else chips
    groups = [[h * relays + r for r in range(relays)] for h in range(2)]
    mirror_pairs = [(i, (i + relays) % peers) for i in range(peers)]

    def swap(bits):
        return [(i, i ^ bits) for i in range(peers)]

    def exchange(x):
        return lax.all_to_all(
            x, "sky", split_axis=0, concat_axis=0, axis_index_groups=groups, tiled=True
        )

    def ship(parts):
        if direct:
            return exchange(parts[0].reshape(relays, -1, 2 * WR, WC))
        got = [parts[0]]
        for m in range(1, chips):
            got.append(lax.ppermute(parts[m], "sky", swap(2 * m)))
        half = parts[0].shape[0] // 2
        mine = [part[:half] for part in got]
        other = jnp.concatenate([part[half:] for part in got], axis=0)
        other = lax.ppermute(other, "sky", swap(1))
        return jnp.concatenate(mine + [other], axis=0).reshape(relays, -1, 2 * WR, WC)

    def mirror(plane, sheet):
        return lax.ppermute(sheet[plane], "sky", mirror_pairs)

    index = lax.axis_index("sky").astype(jnp.int32)
    place = jnp.stack([index // relays, jnp.zeros_like(index) if direct else index % relays])
    tiles = tile_map.transpose(0, 2, 1)
    requests = want(tiles, row_anchor, col_anchor, peers, cap)
    mirrors = [mirror(0, gradients)]
    requests, late = lax.optimization_barrier((requests, gradients))
    mirrors += [mirror(plane, late) for plane in range(1, PLANES)]
    asked = exchange(requests)
    slots = find_slots(place, tiles, peers, cap, direct)
    parts = cut(tuple(range(PLANES)), cap, outs, place, asked, gradients)
    own = ship(parts).reshape(relays, PLANES, cap, 2 * WR, WC)
    windows = []
    for plane in range(PLANES):
        parts = cut((plane,), cap, outs, place, asked, mirrors[plane])
        far = ship(parts)
        both = [x.reshape(relays * cap, 2 * WR, WC) for x in (own[:, plane], far)]
        windows.append(jnp.concatenate(both, axis=0))
    state = (start_x, start_y)
    for plane in range(PLANES):
        state = interp(plane, slots, windows[plane], state)
    return state


def solution(mesh):
    return jax.shard_map(
        body,
        mesh=mesh,
        in_specs=(
            P(("runs", "sky"), None),
            P(("runs", "sky"), None),
            P(None, None, ("runs", "sky"), None),
            P(None, ("runs", "sky"), None),
            P(None, ("runs", "sky")),
            P(None, ("runs", "sky")),
        ),
        out_specs=(P(("runs", "sky"), None, None), P(("runs", "sky"), None, None)),
        check_vma=False,
    )
```

```python
import functools

import jax
import jax.numpy as jnp
from jax import lax
from jax.experimental import pallas as pl
from jax.experimental.pallas import tpu as pltpu
from jax.sharding import PartitionSpec as P


WR = 16
WC = 128
PLANES = 3

lens_ratio = (0.85, 0.7, 0.9)
lens_strength = (0.5, 0.6, 0.45)

GRANT = pltpu.CompilerParams(vmem_limit_bytes=16 << 20)
VMEM = pltpu.VMEM
SMEM = pltpu.SMEM


def whole(space=VMEM):
    return pl.BlockSpec(memory_space=space)


def dot_last(a, b):
    return lax.dot_general(
        a, b, (((1,), (1,)), ((), ())), preferred_element_type=jnp.float32
    )


def ranks(peers, tile_ref, plane):
    nblk = tile_ref.shape[2]
    tile = tile_ref[plane]
    hit = (lax.broadcasted_iota(jnp.int32, (peers, nblk), 0) == tile).astype(jnp.float32)
    earlier = (
        lax.broadcasted_iota(jnp.int32, (nblk, nblk), 1)
        < lax.broadcasted_iota(jnp.int32, (nblk, nblk), 0)
    ).astype(jnp.float32).astype(jnp.bfloat16)
    before = dot_last(hit.astype(jnp.bfloat16), earlier)
    return tile, hit, jnp.sum(before * hit, axis=0, keepdims=True).astype(jnp.int32)


def want_kernel(peers, cap, tile_ref, row_ref, col_ref, req_ref):
    nblk = tile_ref.shape[2]
    relays, lanes = req_ref.shape
    lane = lax.broadcasted_iota(jnp.int32, (lanes, nblk), 0)
    rows = jnp.zeros((relays, lanes), jnp.float32)
    cols = jnp.zeros((relays, lanes), jnp.float32)
    for k in range(PLANES):
        tile, hit, rank = ranks(peers, tile_ref, k)
        here = lane == (rank + (tile // relays + 2 * k) * cap)
        zero = jnp.zeros((), jnp.float32)
        row = jnp.where(here, row_ref[k : k + 1, :].astype(jnp.float32), zero)
        col = jnp.where(here, col_ref[k : k + 1, :].astype(jnp.float32), zero)
        fold = (hit[:relays] + hit[relays:]).astype(jnp.bfloat16)
        rows += dot_last(fold, row.astype(jnp.bfloat16))
        cols += dot_last(fold, col.astype(jnp.bfloat16))
    req_ref[...] = rows.astype(jnp.int32) * 65536 + cols.astype(jnp.int32)


def want(tile_map, row_anchor, col_anchor, peers, cap):
    lanes = -(-PLANES * 2 * cap // 128) * 128
    return pl.pallas_call(
        functools.partial(want_kernel, peers, cap),
        out_shape=jax.ShapeDtypeStruct((peers // 2, lanes), jnp.int32),
        in_specs=[whole()] * 3,
        out_specs=whole(),
        name="want",
    )(tile_map, row_anchor, col_anchor)


def slot_kernel(peers, cap, direct, place_ref, tile_ref, slot_ref):
    relays = peers // 2
    for k in range(PLANES):
        tile, _, rank = ranks(peers, tile_ref, k)
        side = tile // relays
        relay = (tile - side * relays) ^ place_ref[1]
        if not direct:
            relay = (relay & 1) * (relays // 2) + (relay >> 1)
        far = (side != place_ref[0]).astype(jnp.int32)
        slot_ref[k : k + 1, :] = (far * relays + relay) * cap + rank


def find_slots(place, tile_map, peers, cap, direct):
    return pl.pallas_call(
        functools.partial(slot_kernel, peers, cap, direct),
        out_shape=jax.ShapeDtypeStruct((PLANES, tile_map.shape[2]), jnp.int32),
        in_specs=[whole(SMEM), whole()],
        out_specs=whole(),
        compiler_params=GRANT,
        name="slots",
    )(place, tile_map)


def cut_kernel(planes, cap, mirrored, place_ref, req_ref, *refs):
    sheet_refs, out_refs, half_ref = refs[: len(planes)], refs[len(planes) : -1], refs[-1]
    parts = sheet_refs[0].shape[-1] // WC
    for at, sheet_ref in enumerate(sheet_refs):
        for c in range(2):
            for h in range(parts):
                part = sheet_ref[c, :, h * WC : (h + 1) * WC]
                half_ref[(at * 2 + c) * parts + h] = part.astype(jnp.float32)
    lane = lax.broadcasted_iota(jnp.int32, (WR, WC), 1)
    me = place_ref[1]
    side = 1 - place_ref[0] if mirrored else place_ref[0]
    span = req_ref.shape[0] // len(out_refs)

    def one(now, carry):
        for m, out_ref in enumerate(out_refs):
            source = (m * span + now) ^ me
            for at, k in enumerate(planes):
                for place in range(cap):
                    packed = req_ref[source, (2 * k + side) * cap + place]
                    row = packed >> 16
                    col = packed & 65535
                    turn = (WC - col) & (WC - 1)
                    left = lane < WC - col
                    slot = (now * len(planes) + at) * cap + place
                    for c in range(2):
                        part = [
                            pltpu.roll(half_ref[(at * 2 + c) * parts + h, pl.ds(row, WR), :], turn, 1)
                            for h in range(parts)
                        ]
                        out_ref[slot, c * WR : (c + 1) * WR, :] = jnp.where(
                            left, part[0], part[1]
                        ).astype(jnp.bfloat16)
        return carry

    lax.fori_loop(0, span, one, 0)


def cut(planes, cap, outs, mirrored, place, requests, sheets):
    count = requests.shape[0] // outs * len(planes) * cap
    height, width = sheets[0].shape[-2:]
    return pl.pallas_call(
        functools.partial(cut_kernel, planes, cap, mirrored),
        out_shape=(jax.ShapeDtypeStruct((count, 2 * WR, WC), jnp.bfloat16),) * outs,
        in_specs=[whole(SMEM), whole(SMEM)] + [whole()] * len(planes),
        out_specs=(whole(),) * outs,
        scratch_shapes=[VMEM((len(planes) * 2 * width // WC, height, WC), jnp.float32)],
        compiler_params=GRANT,
        name="cut",
    )(place, requests, *sheets)


def taps(pos):
    cell = jnp.floor(pos)
    f = pos - cell
    g = 1.0 - f
    f2, g2 = f * f, g * g
    value = (
        g2 * g / 6.0,
        2.0 / 3.0 - f2 + 0.5 * f2 * f,
        2.0 / 3.0 - g2 + 0.5 * g2 * g,
        f2 * f / 6.0,
    )
    slope = (-0.5 * g2, -2.0 * f + 1.5 * f2, 2.0 * g - 1.5 * g2, 0.5 * f2)
    return cell, value, slope


def interp_kernel(plane, slot_ref, win_ref, *refs):
    first, last = plane == 0, plane == PLANES - 1
    if first:
        x_ref, y_ref = refs[:2]
        refs = refs[2:]
    else:
        state_ref = refs[0]
        refs = refs[1:]
    if last:
        pos_out, jac_out = refs[:2]
        refs = refs[2:]
    else:
        state_out = refs[0]
        refs = refs[1:]
    tap_ref, res_ref = refs
    nblk, rays = res_ref.shape[1:]

    if first:
        px, py = x_ref[...], y_ref[...]
    else:
        px, py = state_ref[0], state_ref[1]
    for at, pos in ((0, px), (9, py)):
        cell, value, slope = taps(pos)
        tap_ref[at] = jnp.clip(cell, -4.0, WC + 4.0)
        for j in range(4):
            tap_ref[at + 1 + j] = value[j]
            tap_ref[at + 5 + j] = slope[j]

    def one(b, carry):
        def row(j):
            return tap_ref[j, pl.ds(b, 1), :]

        def spread(at, size, dtype):
            tile = 8 * 4 // jnp.dtype(dtype).itemsize

            def lay(j):
                return jnp.broadcast_to(row(j), (tile, rays)).astype(dtype)[None]

            place = lax.broadcasted_iota(jnp.int32, (size // tile, tile, rays), 0) * tile
            place = (place + lax.broadcasted_iota(jnp.int32, place.shape, 1)).astype(jnp.float32)
            near = place.astype(dtype) - lay(at)
            value = jnp.zeros(near.shape, dtype)
            slope = value
            for j in range(4):
                here = near == jnp.asarray(j - 1, dtype)
                value = jnp.where(here, lay(at + 1 + j), value)
                slope = jnp.where(here, lay(at + 5 + j), slope)
            return value.reshape(size, rays), slope.reshape(size, rays)

        kern = jnp.concatenate(spread(0, WC, jnp.bfloat16), axis=1)
        mixed = jnp.dot(win_ref[slot_ref[plane, b]], kern, preferred_element_type=jnp.float32)
        ky, kyd = spread(9, WR, jnp.float32)
        for c in range(2):
            part = mixed[c * WR : (c + 1) * WR]
            mixed0, mixed1 = part[:, :rays], part[:, rays:]
            for at, product in ((0, ky * mixed0), (2, ky * mixed1), (4, kyd * mixed0)):
                res_ref[at + c, pl.ds(b, 1), :] = jnp.sum(product, axis=0, keepdims=True)
        return carry

    lax.fori_loop(0, nblk, one, 0, unroll=16)

    ratio, strength = lens_ratio[plane], lens_strength[plane]
    ax, ay = res_ref[0], res_ref[1]
    hxx, hyx, hxy, hyy = res_ref[2], res_ref[3], res_ref[4], res_ref[5]
    if first:
        vx, vy = -strength * ax, -strength * ay
        dj = [-strength * h for h in (hxx, hxy, hyx, hyy)]
        jac = [1.0 + dj[0], dj[1], dj[2], 1.0 + dj[3]]
    else:
        vx = ratio * state_ref[2] - strength * ax
        vy = ratio * state_ref[3] - strength * ay
        axx, axy, ayx, ayy = [state_ref[4 + j] for j in range(4)]
        product = (
            hxx * axx + hxy * ayx,
            hxx * axy + hxy * ayy,
            hyx * axx + hyy * ayx,
            hyx * axy + hyy * ayy,
        )
        dj = [ratio * state_ref[8 + j] - strength * product[j] for j in range(4)]
        jac = [old + d for old, d in zip((axx, axy, ayx, ayy), dj)]
    px, py = px + vx, py + vy
    if last:
        pos_out[:, 0, :] = px
        pos_out[:, 1, :] = py
        for j in range(4):
            jac_out[:, j, :] = jac[j]
    else:
        for j, value in enumerate([px, py, vx, vy] + jac + dj):
            state_out[j] = value


def interp(plane, slots, windows, state):
    nblk = slots.shape[1]
    rays = state[0].shape[-1]
    if plane == PLANES - 1:
        out_shape = (
            jax.ShapeDtypeStruct((nblk, 2, rays), jnp.float32),
            jax.ShapeDtypeStruct((nblk, 4, rays), jnp.float32),
        )
    else:
        out_shape = (jax.ShapeDtypeStruct((12, nblk, rays), jnp.float32),)
    return pl.pallas_call(
        functools.partial(interp_kernel, plane),
        out_shape=out_shape,
        in_specs=[whole(SMEM), whole()] + [whole()] * len(state),
        out_specs=(whole(),) * len(out_shape),
        scratch_shapes=[
            VMEM((18, nblk, rays), jnp.float32),
            VMEM((6, nblk, rays), jnp.float32),
        ],
        compiler_params=GRANT,
    )(slots, windows, *state)


def body(start_x, start_y, gradients, tile_map, row_anchor, col_anchor):
    peers = lax.axis_size("sky")
    nblk = start_x.shape[0]
    cap = max(2, 2 * nblk // peers)
    relays = peers // 2
    chips = relays // 2
    direct = chips > 4 or chips & (chips - 1) != 0
    outs = 1 if direct else chips
    groups = [[h * relays + r for r in range(relays)] for h in range(2)]
    mirror_pairs = [(i, (i + relays) % peers) for i in range(peers)]

    def swap(bits):
        return [(i, i ^ bits) for i in range(peers)]

    def exchange(x):
        return lax.all_to_all(
            x, "sky", split_axis=0, concat_axis=0, axis_index_groups=groups, tiled=True
        )

    def ship(parts, count):
        if direct:
            got = exchange(parts[0].reshape(relays, -1, 2 * WR, WC))
            got = got.reshape(relays, count, cap, 2 * WR, WC)
            return [([got[:, at].reshape(relays * cap, 2 * WR, WC)], []) for at in range(count)]
        got = [parts[0]]
        for m in range(1, chips):
            got.append(lax.ppermute(parts[m], "sky", swap(2 * m)))

        def pieces(at):
            return [part[at * cap : (at + 1) * cap] for part in got]

        return [(pieces(at), pieces(count + at)) for at in range(count)]

    def across(lists):
        if direct:
            return [[] for _ in lists]
        got = lax.ppermute(jnp.concatenate(sum(lists, []), axis=0), "sky", swap(1))
        size = chips * cap
        return [[got[at * size : (at + 1) * size]] for at in range(len(lists))]

    def tile(plane, sheet):
        return sheet[plane]

    def mirror(plane):
        return lax.ppermute(sheets[plane], "sky", mirror_pairs)

    def cut_sent(planes, mirrored, tiles_of):
        parts = cut(planes, cap, outs, mirrored, place, asked, tiles_of)
        return ship(parts, len(planes))

    index = lax.axis_index("sky").astype(jnp.int32)
    place = jnp.stack([index // relays, jnp.zeros_like(index) if direct else index % relays])
    tiles = tile_map.transpose(0, 2, 1)
    requests = want(tiles, row_anchor, col_anchor, peers, cap)
    requests, late = lax.optimization_barrier((requests, gradients))
    sheets = [tile(0, gradients)] + [tile(plane, late) for plane in range(1, PLANES)]
    mirrors = [mirror(plane) for plane in range(PLANES)]
    asked = exchange(requests)
    slots = find_slots(place, tiles, peers, cap, direct)
    rest = tuple(range(1, PLANES))
    own = cut_sent((0,), False, sheets[:1])
    far = cut_sent((0,), True, mirrors[:1])
    own += cut_sent(rest, False, sheets[1:])
    for plane in rest:
        far += cut_sent((plane,), True, mirrors[plane : plane + 1])
    state = (start_x, start_y)
    held = {}
    for plane in range(PLANES):
        news = [("own", plane)] if plane == 0 else [("own", k) for k in rest] if plane == 1 else []
        news.append(("far", plane))
        source = {"own": own, "far": far}
        held.update(zip(news, across([source[kind][k][1] for kind, k in news])))
        windows = own[plane][0] + held["own", plane] + far[plane][0] + held["far", plane]
        state = interp(plane, slots, jnp.concatenate(windows, axis=0), state)
    return state


def solution(mesh):
    return jax.shard_map(
        body,
        mesh=mesh,
        in_specs=(
            P(("runs", "sky"), None),
            P(("runs", "sky"), None),
            P(None, None, ("runs", "sky"), None),
            P(None, ("runs", "sky"), None),
            P(None, ("runs", "sky")),
            P(None, ("runs", "sky")),
        ),
        out_specs=(P(("runs", "sky"), None, None), P(("runs", "sky"), None, None)),
        check_vma=False,
    )
```

```python
import functools

import jax
import jax.numpy as jnp
from jax import lax
from jax.experimental import pallas as pl
from jax.experimental.pallas import tpu as pltpu
from jax.sharding import PartitionSpec as P


WR = 16
WC = 128
PLANES = 3

lens_ratio = (0.85, 0.7, 0.9)
lens_strength = (0.5, 0.6, 0.45)

GRANT = pltpu.CompilerParams(vmem_limit_bytes=16 << 20)
VMEM = pltpu.VMEM
SMEM = pltpu.SMEM


def whole(space=VMEM):
    return pl.BlockSpec(memory_space=space)


def dot_last(a, b):
    return lax.dot_general(
        a, b, (((1,), (1,)), ((), ())), preferred_element_type=jnp.float32
    )


def ranks(peers, tile_ref, plane):
    nblk = tile_ref.shape[2]
    tile = tile_ref[plane]
    hit = (lax.broadcasted_iota(jnp.int32, (peers, nblk), 0) == tile).astype(jnp.float32)
    earlier = (
        lax.broadcasted_iota(jnp.int32, (nblk, nblk), 1)
        < lax.broadcasted_iota(jnp.int32, (nblk, nblk), 0)
    ).astype(jnp.float32).astype(jnp.bfloat16)
    before = dot_last(hit.astype(jnp.bfloat16), earlier)
    return tile, hit, jnp.sum(before * hit, axis=0, keepdims=True).astype(jnp.int32)


def want_kernel(peers, cap, tile_ref, row_ref, col_ref, req_ref):
    nblk = tile_ref.shape[2]
    relays, lanes = req_ref.shape
    lane = lax.broadcasted_iota(jnp.int32, (lanes, nblk), 0)
    rows = jnp.zeros((relays, lanes), jnp.float32)
    cols = jnp.zeros((relays, lanes), jnp.float32)
    for k in range(PLANES):
        tile, hit, rank = ranks(peers, tile_ref, k)
        here = lane == (rank + (tile // relays + 2 * k) * cap)
        zero = jnp.zeros((), jnp.float32)
        row = jnp.where(here, row_ref[k : k + 1, :].astype(jnp.float32), zero)
        col = jnp.where(here, col_ref[k : k + 1, :].astype(jnp.float32), zero)
        fold = (hit[:relays] + hit[relays:]).astype(jnp.bfloat16)
        rows += dot_last(fold, row.astype(jnp.bfloat16))
        cols += dot_last(fold, col.astype(jnp.bfloat16))
    req_ref[...] = rows.astype(jnp.int32) * 65536 + cols.astype(jnp.int32)


def want(tile_map, row_anchor, col_anchor, peers, cap):
    lanes = -(-PLANES * 2 * cap // 128) * 128
    return pl.pallas_call(
        functools.partial(want_kernel, peers, cap),
        out_shape=jax.ShapeDtypeStruct((peers // 2, lanes), jnp.int32),
        in_specs=[whole()] * 3,
        out_specs=whole(),
        name="want",
    )(tile_map, row_anchor, col_anchor)


def slot_kernel(peers, cap, direct, place_ref, tile_ref, slot_ref):
    relays = peers // 2
    for k in range(PLANES):
        tile, _, rank = ranks(peers, tile_ref, k)
        side = tile // relays
        relay = (tile - side * relays) ^ place_ref[1]
        if not direct:
            relay = (relay & 1) * (relays // 2) + (relay >> 1)
        far = (side != place_ref[0]).astype(jnp.int32)
        slot_ref[k : k + 1, :] = (far * relays + relay) * cap + rank


def find_slots(place, tile_map, peers, cap, direct):
    return pl.pallas_call(
        functools.partial(slot_kernel, peers, cap, direct),
        out_shape=jax.ShapeDtypeStruct((PLANES, tile_map.shape[2]), jnp.int32),
        in_specs=[whole(SMEM), whole()],
        out_specs=whole(),
        compiler_params=GRANT,
        name="slots",
    )(place, tile_map)


def cut_kernel(planes, cap, mirrored, place_ref, req_ref, *refs):
    sheet_refs, out_refs, half_ref = refs[: len(planes)], refs[len(planes) : -1], refs[-1]
    parts = sheet_refs[0].shape[-1] // WC
    for at, sheet_ref in enumerate(sheet_refs):
        for c in range(2):
            for h in range(parts):
                part = sheet_ref[c, :, h * WC : (h + 1) * WC]
                half_ref[(at * 2 + c) * parts + h] = part.astype(jnp.float32)
    lane = lax.broadcasted_iota(jnp.int32, (WR, WC), 1)
    me = place_ref[1]
    side = 1 - place_ref[0] if mirrored else place_ref[0]
    span = req_ref.shape[0] // len(out_refs)

    def one(now, carry):
        for m, out_ref in enumerate(out_refs):
            source = (m * span + now) ^ me
            for at, k in enumerate(planes):
                for place in range(cap):
                    packed = req_ref[source, (2 * k + side) * cap + place]
                    row = packed >> 16
                    col = packed & 65535
                    turn = (WC - col) & (WC - 1)
                    left = lane < WC - col
                    slot = (now * len(planes) + at) * cap + place
                    for c in range(2):
                        part = [
                            pltpu.roll(half_ref[(at * 2 + c) * parts + h, pl.ds(row, WR), :], turn, 1)
                            for h in range(parts)
                        ]
                        out_ref[slot, c * WR : (c + 1) * WR, :] = jnp.where(
                            left, part[0], part[1]
                        ).astype(jnp.bfloat16)
        return carry

    lax.fori_loop(0, span, one, 0)


def cut(planes, cap, outs, mirrored, place, requests, sheets):
    count = requests.shape[0] // outs * len(planes) * cap
    height, width = sheets[0].shape[-2:]
    return pl.pallas_call(
        functools.partial(cut_kernel, planes, cap, mirrored),
        out_shape=(jax.ShapeDtypeStruct((count, 2 * WR, WC), jnp.bfloat16),) * outs,
        in_specs=[whole(SMEM), whole(SMEM)] + [whole()] * len(planes),
        out_specs=(whole(),) * outs,
        scratch_shapes=[VMEM((len(planes) * 2 * width // WC, height, WC), jnp.float32)],
        compiler_params=GRANT,
        name="cut",
    )(place, requests, *sheets)


def taps(pos):
    cell = jnp.floor(pos)
    f = pos - cell
    g = 1.0 - f
    f2, g2 = f * f, g * g
    value = (
        g2 * g / 6.0,
        2.0 / 3.0 - f2 + 0.5 * f2 * f,
        2.0 / 3.0 - g2 + 0.5 * g2 * g,
        f2 * f / 6.0,
    )
    slope = (-0.5 * g2, -2.0 * f + 1.5 * f2, 2.0 * g - 1.5 * g2, 0.5 * f2)
    return cell, value, slope


def interp_kernel(plane, slot_ref, win_ref, *refs):
    first, last = plane == 0, plane == PLANES - 1
    if first:
        x_ref, y_ref = refs[:2]
        refs = refs[2:]
    else:
        state_ref = refs[0]
        refs = refs[1:]
    if last:
        pos_out, jac_out = refs[:2]
        refs = refs[2:]
    else:
        state_out = refs[0]
        refs = refs[1:]
    tap_ref, res_ref = refs
    nblk, rays = res_ref.shape[1:]

    if first:
        px, py = x_ref[...], y_ref[...]
    else:
        px, py = state_ref[0], state_ref[1]
    for at, pos in ((0, px), (9, py)):
        cell, value, slope = taps(pos)
        tap_ref[at] = jnp.clip(cell, -4.0, WC + 4.0)
        for j in range(4):
            tap_ref[at + 1 + j] = value[j]
            tap_ref[at + 5 + j] = slope[j]

    def one(b, carry):
        def row(j):
            return tap_ref[j, pl.ds(b, 1), :]

        def spread(at, size, dtype):
            tile = 8 * 4 // jnp.dtype(dtype).itemsize

            def lay(j):
                return jnp.broadcast_to(row(j), (tile, rays)).astype(dtype)[None]

            place = lax.broadcasted_iota(jnp.int32, (size // tile, tile, rays), 0) * tile
            place = (place + lax.broadcasted_iota(jnp.int32, place.shape, 1)).astype(jnp.float32)
            near = place.astype(dtype) - lay(at)
            value = jnp.zeros(near.shape, dtype)
            slope = value
            for j in range(4):
                here = near == jnp.asarray(j - 1, dtype)
                value = jnp.where(here, lay(at + 1 + j), value)
                slope = jnp.where(here, lay(at + 5 + j), slope)
            return value.reshape(size, rays), slope.reshape(size, rays)

        kern = jnp.concatenate(spread(0, WC, jnp.bfloat16), axis=1)
        mixed = jnp.dot(win_ref[slot_ref[plane, b]], kern, preferred_element_type=jnp.float32)
        ky, kyd = spread(9, WR, jnp.float32)
        for c in range(2):
            part = mixed[c * WR : (c + 1) * WR]
            mixed0, mixed1 = part[:, :rays], part[:, rays:]
            for at, product in ((0, ky * mixed0), (2, ky * mixed1), (4, kyd * mixed0)):
                res_ref[at + c, pl.ds(b, 1), :] = jnp.sum(product, axis=0, keepdims=True)
        return carry

    lax.fori_loop(0, nblk, one, 0, unroll=16)

    ratio, strength = lens_ratio[plane], lens_strength[plane]
    ax, ay = res_ref[0], res_ref[1]
    hxx, hyx, hxy, hyy = res_ref[2], res_ref[3], res_ref[4], res_ref[5]
    if first:
        vx, vy = -strength * ax, -strength * ay
        dj = [-strength * h for h in (hxx, hxy, hyx, hyy)]
        jac = [1.0 + dj[0], dj[1], dj[2], 1.0 + dj[3]]
    else:
        vx = ratio * state_ref[2] - strength * ax
        vy = ratio * state_ref[3] - strength * ay
        axx, axy, ayx, ayy = [state_ref[4 + j] for j in range(4)]
        product = (
            hxx * axx + hxy * ayx,
            hxx * axy + hxy * ayy,
            hyx * axx + hyy * ayx,
            hyx * axy + hyy * ayy,
        )
        dj = [ratio * state_ref[8 + j] - strength * product[j] for j in range(4)]
        jac = [old + d for old, d in zip((axx, axy, ayx, ayy), dj)]
    px, py = px + vx, py + vy
    if last:
        pos_out[:, 0, :] = px
        pos_out[:, 1, :] = py
        for j in range(4):
            jac_out[:, j, :] = jac[j]
    else:
        for j, value in enumerate([px, py, vx, vy] + jac + dj):
            state_out[j] = value


def interp(plane, slots, windows, state):
    nblk = slots.shape[1]
    rays = state[0].shape[-1]
    if plane == PLANES - 1:
        out_shape = (
            jax.ShapeDtypeStruct((nblk, 2, rays), jnp.float32),
            jax.ShapeDtypeStruct((nblk, 4, rays), jnp.float32),
        )
    else:
        out_shape = (jax.ShapeDtypeStruct((12, nblk, rays), jnp.float32),)
    return pl.pallas_call(
        functools.partial(interp_kernel, plane),
        out_shape=out_shape,
        in_specs=[whole(SMEM), whole()] + [whole()] * len(state),
        out_specs=(whole(),) * len(out_shape),
        scratch_shapes=[
            VMEM((18, nblk, rays), jnp.float32),
            VMEM((6, nblk, rays), jnp.float32),
        ],
        compiler_params=GRANT,
    )(slots, windows, *state)


def body(start_x, start_y, gradients, tile_map, row_anchor, col_anchor):
    peers = lax.axis_size("sky")
    nblk = start_x.shape[0]
    cap = max(2, 2 * nblk // peers)
    relays = peers // 2
    chips = relays // 2
    direct = chips > 4 or chips & (chips - 1) != 0
    outs = 1 if direct else chips
    groups = [[h * relays + r for r in range(relays)] for h in range(2)]
    mirror_pairs = [(i, (i + relays) % peers) for i in range(peers)]

    def swap(bits):
        return [(i, i ^ bits) for i in range(peers)]

    def exchange(x):
        return lax.all_to_all(
            x, "sky", split_axis=0, concat_axis=0, axis_index_groups=groups, tiled=True
        )

    def ship(parts, count):
        if direct:
            got = exchange(parts[0].reshape(relays, -1, 2 * WR, WC))
            got = got.reshape(relays, count, cap, 2 * WR, WC)
            return [([got[:, at].reshape(relays * cap, 2 * WR, WC)], []) for at in range(count)]
        got = [parts[0]]
        step = relays // len(parts)
        for m in range(1, len(parts)):
            got.append(lax.ppermute(parts[m], "sky", swap(step * m)))
        if step == 1:
            return [(got[::2] + got[1::2], [])]

        def pieces(at):
            return [part[at * cap : (at + 1) * cap] for part in got]

        return [(pieces(at), pieces(count + at)) for at in range(count)]

    def across(lists):
        if direct:
            return [[] for _ in lists]
        got = lax.ppermute(jnp.concatenate(sum(lists, []), axis=0), "sky", swap(1))
        size = chips * cap
        return [[got[at * size : (at + 1) * size]] for at in range(len(lists))]

    def tile(plane, sheet):
        return sheet[plane]

    def mirror(plane):
        return lax.ppermute(sheets[plane], "sky", mirror_pairs)

    def cut_sent(plane, mirrored, sheet, straight=False):
        count = outs * 2 if straight and not direct else outs
        parts = cut((plane,), cap, count, mirrored, place, asked, (sheet,))
        return ship(parts, 1)[0]

    index = lax.axis_index("sky").astype(jnp.int32)
    place = jnp.stack([index // relays, jnp.zeros_like(index) if direct else index % relays])
    tiles = tile_map.transpose(0, 2, 1)
    requests = want(tiles, row_anchor, col_anchor, peers, cap)
    requests, late = lax.optimization_barrier((requests, gradients))
    sheets = [tile(0, gradients)] + [tile(plane, late) for plane in range(1, PLANES)]
    mirrors = [mirror(plane) for plane in range(PLANES)]
    asked = exchange(requests)
    slots = find_slots(place, tiles, peers, cap, direct)
    own, far = [], []
    for plane in range(PLANES):
        own.append(cut_sent(plane, False, sheets[plane]))
        far.append(cut_sent(plane, True, mirrors[plane], plane == PLANES - 1))
    state = (start_x, start_y)
    for plane in range(PLANES):
        sets = (own[plane], far[plane])
        held = iter(across([other for _, other in sets if other]))
        windows = sum((mine + (next(held) if other else []) for mine, other in sets), [])
        state = interp(plane, slots, jnp.concatenate(windows, axis=0), state)
    return state


def solution(mesh):
    return jax.shard_map(
        body,
        mesh=mesh,
        in_specs=(
            P(("runs", "sky"), None),
            P(("runs", "sky"), None),
            P(None, None, ("runs", "sky"), None),
            P(None, ("runs", "sky"), None),
            P(None, ("runs", "sky")),
            P(None, ("runs", "sky")),
        ),
        out_specs=(P(("runs", "sky"), None, None), P(("runs", "sky"), None, None)),
        check_vma=False,
    )
```

```python
import functools

import jax
import jax.numpy as jnp
from jax import lax
from jax.experimental import pallas as pl
from jax.experimental.pallas import tpu as pltpu
from jax.sharding import PartitionSpec as P


WR = 16
WC = 128
PLANES = 3

lens_ratio = (0.85, 0.7, 0.9)
lens_strength = (0.5, 0.6, 0.45)

GRANT = pltpu.CompilerParams(vmem_limit_bytes=16 << 20)
VMEM = pltpu.VMEM
SMEM = pltpu.SMEM


def whole(space=VMEM):
    return pl.BlockSpec(memory_space=space)


def dot_last(a, b):
    return lax.dot_general(
        a, b, (((1,), (1,)), ((), ())), preferred_element_type=jnp.float32
    )


def ranks(peers, tile_ref, plane):
    nblk = tile_ref.shape[2]
    tile = tile_ref[plane]
    hit = (lax.broadcasted_iota(jnp.int32, (peers, nblk), 0) == tile).astype(jnp.float32)
    earlier = (
        lax.broadcasted_iota(jnp.int32, (nblk, nblk), 1)
        < lax.broadcasted_iota(jnp.int32, (nblk, nblk), 0)
    ).astype(jnp.float32).astype(jnp.bfloat16)
    before = dot_last(hit.astype(jnp.bfloat16), earlier)
    return tile, hit, jnp.sum(before * hit, axis=0, keepdims=True).astype(jnp.int32)


def want_kernel(peers, cap, tile_ref, row_ref, col_ref, req_ref):
    nblk = tile_ref.shape[2]
    relays, lanes = req_ref.shape
    lane = lax.broadcasted_iota(jnp.int32, (lanes, nblk), 0)
    rows = jnp.zeros((relays, lanes), jnp.float32)
    cols = jnp.zeros((relays, lanes), jnp.float32)
    for k in range(PLANES):
        tile, hit, rank = ranks(peers, tile_ref, k)
        here = lane == (rank + (tile // relays + 2 * k) * cap)
        zero = jnp.zeros((), jnp.float32)
        row = jnp.where(here, row_ref[k : k + 1, :].astype(jnp.float32), zero)
        col = jnp.where(here, col_ref[k : k + 1, :].astype(jnp.float32), zero)
        fold = (hit[:relays] + hit[relays:]).astype(jnp.bfloat16)
        rows += dot_last(fold, row.astype(jnp.bfloat16))
        cols += dot_last(fold, col.astype(jnp.bfloat16))
    req_ref[...] = rows.astype(jnp.int32) * 65536 + cols.astype(jnp.int32)


def want(tile_map, row_anchor, col_anchor, peers, cap):
    lanes = -(-PLANES * 2 * cap // 128) * 128
    return pl.pallas_call(
        functools.partial(want_kernel, peers, cap),
        out_shape=jax.ShapeDtypeStruct((peers // 2, lanes), jnp.int32),
        in_specs=[whole()] * 3,
        out_specs=whole(),
        name="want",
    )(tile_map, row_anchor, col_anchor)


def slot_kernel(peers, cap, direct, place_ref, tile_ref, slot_ref):
    relays = peers // 2
    for k in range(PLANES):
        tile, _, rank = ranks(peers, tile_ref, k)
        side = tile // relays
        relay = (tile - side * relays) ^ place_ref[1]
        if not direct:
            relay = (relay & 1) * (relays // 2) + (relay >> 1)
        far = (side != place_ref[0]).astype(jnp.int32)
        slot_ref[k : k + 1, :] = (far * relays + relay) * cap + rank


def find_slots(place, tile_map, peers, cap, direct):
    return pl.pallas_call(
        functools.partial(slot_kernel, peers, cap, direct),
        out_shape=jax.ShapeDtypeStruct((PLANES, tile_map.shape[2]), jnp.int32),
        in_specs=[whole(SMEM), whole()],
        out_specs=whole(),
        compiler_params=GRANT,
        name="slots",
    )(place, tile_map)


def cut_kernel(plane, cap, kinds, place_ref, req_ref, *refs):
    sheet_refs, out_refs, half_ref = refs[: len(kinds)], refs[len(kinds) : -1], refs[-1]
    parts = sheet_refs[0].shape[-1] // WC
    for at, sheet_ref in enumerate(sheet_refs):
        for c in range(2):
            for h in range(parts):
                part = sheet_ref[c, :, h * WC : (h + 1) * WC]
                half_ref[(at * 2 + c) * parts + h] = part.astype(jnp.float32)
    lane = lax.broadcasted_iota(jnp.int32, (WR, WC), 1)
    me = place_ref[1]
    sides = [1 - place_ref[0] if mirrored else place_ref[0] for mirrored in kinds]
    span = req_ref.shape[0] // len(out_refs)

    def one(now, carry):
        for m, out_ref in enumerate(out_refs):
            source = (m * span + now) ^ me
            for at, side in enumerate(sides):
                for place in range(cap):
                    packed = req_ref[source, (2 * plane + side) * cap + place]
                    row = packed >> 16
                    col = packed & 65535
                    turn = (WC - col) & (WC - 1)
                    left = lane < WC - col
                    slot = (now * len(kinds) + at) * cap + place
                    for c in range(2):
                        part = [
                            pltpu.roll(half_ref[(at * 2 + c) * parts + h, pl.ds(row, WR), :], turn, 1)
                            for h in range(parts)
                        ]
                        out_ref[slot, c * WR : (c + 1) * WR, :] = jnp.where(
                            left, part[0], part[1]
                        ).astype(jnp.bfloat16)
        return carry

    lax.fori_loop(0, span, one, 0)


def cut(plane, cap, outs, kinds, place, requests, sheets):
    count = requests.shape[0] // outs * len(kinds) * cap
    height, width = sheets[0].shape[-2:]
    return pl.pallas_call(
        functools.partial(cut_kernel, plane, cap, kinds),
        out_shape=(jax.ShapeDtypeStruct((count, 2 * WR, WC), jnp.bfloat16),) * outs,
        in_specs=[whole(SMEM), whole(SMEM)] + [whole()] * len(kinds),
        out_specs=(whole(),) * outs,
        scratch_shapes=[VMEM((len(kinds) * 2 * width // WC, height, WC), jnp.float32)],
        compiler_params=GRANT,
        name="cut",
    )(place, requests, *sheets)


def taps(pos):
    cell = jnp.floor(pos)
    f = pos - cell
    g = 1.0 - f
    f2, g2 = f * f, g * g
    value = (
        g2 * g / 6.0,
        2.0 / 3.0 - f2 + 0.5 * f2 * f,
        2.0 / 3.0 - g2 + 0.5 * g2 * g,
        f2 * f / 6.0,
    )
    slope = (-0.5 * g2, -2.0 * f + 1.5 * f2, 2.0 * g - 1.5 * g2, 0.5 * f2)
    return cell, value, slope


def interp_kernel(plane, slot_ref, win_ref, *refs):
    first, last = plane == 0, plane == PLANES - 1
    if first:
        x_ref, y_ref = refs[:2]
        refs = refs[2:]
    else:
        state_ref = refs[0]
        refs = refs[1:]
    if last:
        pos_out, jac_out = refs[:2]
        refs = refs[2:]
    else:
        state_out = refs[0]
        refs = refs[1:]
    tap_ref, res_ref = refs
    nblk, rays = res_ref.shape[1:]

    if first:
        px, py = x_ref[...], y_ref[...]
    else:
        px, py = state_ref[0], state_ref[1]
    for at, pos in ((0, px), (9, py)):
        cell, value, slope = taps(pos)
        tap_ref[at] = jnp.clip(cell, -4.0, WC + 4.0)
        for j in range(4):
            tap_ref[at + 1 + j] = value[j]
            tap_ref[at + 5 + j] = slope[j]

    def one(b, carry):
        def row(j):
            return tap_ref[j, pl.ds(b, 1), :]

        def spread(at, size, dtype):
            tile = 8 * 4 // jnp.dtype(dtype).itemsize

            def lay(j):
                return jnp.broadcast_to(row(j), (tile, rays)).astype(dtype)[None]

            place = lax.broadcasted_iota(jnp.int32, (size // tile, tile, rays), 0) * tile
            place = (place + lax.broadcasted_iota(jnp.int32, place.shape, 1)).astype(jnp.float32)
            near = place.astype(dtype) - lay(at)
            value = jnp.zeros(near.shape, dtype)
            slope = value
            for j in range(4):
                here = near == jnp.asarray(j - 1, dtype)
                value = jnp.where(here, lay(at + 1 + j), value)
                slope = jnp.where(here, lay(at + 5 + j), slope)
            return value.reshape(size, rays), slope.reshape(size, rays)

        kern = jnp.concatenate(spread(0, WC, jnp.bfloat16), axis=1)
        mixed = jnp.dot(win_ref[slot_ref[plane, b]], kern, preferred_element_type=jnp.float32)
        ky, kyd = spread(9, WR, jnp.float32)
        for c in range(2):
            part = mixed[c * WR : (c + 1) * WR]
            mixed0, mixed1 = part[:, :rays], part[:, rays:]
            for at, product in ((0, ky * mixed0), (2, ky * mixed1), (4, kyd * mixed0)):
                res_ref[at + c, pl.ds(b, 1), :] = jnp.sum(product, axis=0, keepdims=True)
        return carry

    lax.fori_loop(0, nblk, one, 0, unroll=16)

    ratio, strength = lens_ratio[plane], lens_strength[plane]
    ax, ay = res_ref[0], res_ref[1]
    hxx, hyx, hxy, hyy = res_ref[2], res_ref[3], res_ref[4], res_ref[5]
    if first:
        vx, vy = -strength * ax, -strength * ay
        dj = [-strength * h for h in (hxx, hxy, hyx, hyy)]
        jac = [1.0 + dj[0], dj[1], dj[2], 1.0 + dj[3]]
    else:
        vx = ratio * state_ref[2] - strength * ax
        vy = ratio * state_ref[3] - strength * ay
        axx, axy, ayx, ayy = [state_ref[4 + j] for j in range(4)]
        product = (
            hxx * axx + hxy * ayx,
            hxx * axy + hxy * ayy,
            hyx * axx + hyy * ayx,
            hyx * axy + hyy * ayy,
        )
        dj = [ratio * state_ref[8 + j] - strength * product[j] for j in range(4)]
        jac = [old + d for old, d in zip((axx, axy, ayx, ayy), dj)]
    px, py = px + vx, py + vy
    if last:
        pos_out[:, 0, :] = px
        pos_out[:, 1, :] = py
        for j in range(4):
            jac_out[:, j, :] = jac[j]
    else:
        for j, value in enumerate([px, py, vx, vy] + jac + dj):
            state_out[j] = value


def interp(plane, slots, windows, state):
    nblk = slots.shape[1]
    rays = state[0].shape[-1]
    if plane == PLANES - 1:
        out_shape = (
            jax.ShapeDtypeStruct((nblk, 2, rays), jnp.float32),
            jax.ShapeDtypeStruct((nblk, 4, rays), jnp.float32),
        )
    else:
        out_shape = (jax.ShapeDtypeStruct((12, nblk, rays), jnp.float32),)
    return pl.pallas_call(
        functools.partial(interp_kernel, plane),
        out_shape=out_shape,
        in_specs=[whole(SMEM), whole()] + [whole()] * len(state),
        out_specs=(whole(),) * len(out_shape),
        scratch_shapes=[
            VMEM((18, nblk, rays), jnp.float32),
            VMEM((6, nblk, rays), jnp.float32),
        ],
        compiler_params=GRANT,
    )(slots, windows, *state)


def body(start_x, start_y, gradients, tile_map, row_anchor, col_anchor):
    peers = lax.axis_size("sky")
    nblk = start_x.shape[0]
    cap = max(2, 2 * nblk // peers)
    relays = peers // 2
    chips = relays // 2
    direct = chips > 4 or chips & (chips - 1) != 0
    outs = 1 if direct else chips
    groups = [[h * relays + r for r in range(relays)] for h in range(2)]
    mirror_pairs = [(i, (i + relays) % peers) for i in range(peers)]

    def swap(bits):
        return [(i, i ^ bits) for i in range(peers)]

    def exchange(x):
        return lax.all_to_all(
            x, "sky", split_axis=0, concat_axis=0, axis_index_groups=groups, tiled=True
        )

    def ship(parts, count):
        if direct:
            got = exchange(parts[0].reshape(relays, -1, 2 * WR, WC))
            got = got.reshape(relays, count, cap, 2 * WR, WC)
            return [([got[:, at].reshape(relays * cap, 2 * WR, WC)], []) for at in range(count)]
        got = [parts[0]]
        step = relays // len(parts)
        for m in range(1, len(parts)):
            got.append(lax.ppermute(parts[m], "sky", swap(step * m)))

        def pieces(at, of=got):
            return [part[at * cap : (at + 1) * cap] for part in of]

        if step == 1:
            return [(pieces(at, got[::2] + got[1::2]), []) for at in range(count)]
        return [(pieces(at), pieces(count + at)) for at in range(count)]

    def across(lists):
        if not lists:
            return []
        got = lax.ppermute(jnp.concatenate(sum(lists, []), axis=0), "sky", swap(1))
        size = chips * cap
        return [[got[at * size : (at + 1) * size]] for at in range(len(lists))]

    def tile(plane, sheet):
        return sheet[plane]

    def mirror(plane):
        return lax.ppermute(sheets[plane], "sky", mirror_pairs)

    def cut_sent(plane, kinds, straight=False):
        count = outs * 2 if straight and not direct else outs
        tiles_of = [mirrors[plane] if mirrored else sheets[plane] for mirrored in kinds]
        parts = cut(plane, cap, count, kinds, place, asked, tiles_of)
        return ship(parts, len(kinds))

    index = lax.axis_index("sky").astype(jnp.int32)
    place = jnp.stack([index // relays, jnp.zeros_like(index) if direct else index % relays])
    tiles = tile_map.transpose(0, 2, 1)
    requests = want(tiles, row_anchor, col_anchor, peers, cap)
    requests, late = lax.optimization_barrier((requests, gradients))
    sheets = [tile(0, gradients)] + [tile(plane, late) for plane in range(1, PLANES)]
    mirrors = [mirror(plane) for plane in range(PLANES)]
    asked = exchange(requests)
    slots = find_slots(place, tiles, peers, cap, direct)
    sent = [cut_sent(0, (False,)) + cut_sent(0, (True,))]
    for plane in range(1, PLANES):
        sent.append(cut_sent(plane, (False, True), plane == PLANES - 1))
    state = (start_x, start_y)
    for plane in range(PLANES):
        sets = sent[plane]
        held = iter(across([other for _, other in sets if other]))
        windows = sum((mine + (next(held) if other else []) for mine, other in sets), [])
        state = interp(plane, slots, jnp.concatenate(windows, axis=0), state)
    return state


def solution(mesh):
    return jax.shard_map(
        body,
        mesh=mesh,
        in_specs=(
            P(("runs", "sky"), None),
            P(("runs", "sky"), None),
            P(None, None, ("runs", "sky"), None),
            P(None, ("runs", "sky"), None),
            P(None, ("runs", "sky")),
            P(None, ("runs", "sky")),
        ),
        out_specs=(P(("runs", "sky"), None, None), P(("runs", "sky"), None, None)),
        check_vma=False,
    )
```

```python
import functools

import jax
import jax.numpy as jnp
from jax import lax
from jax.experimental import pallas as pl
from jax.experimental.pallas import tpu as pltpu
from jax.sharding import PartitionSpec as P


WR = 16
WC = 128
PLANES = 3

lens_ratio = (0.85, 0.7, 0.9)
lens_strength = (0.5, 0.6, 0.45)

GRANT = pltpu.CompilerParams(vmem_limit_bytes=16 << 20)
VMEM = pltpu.VMEM
SMEM = pltpu.SMEM


def whole(space=VMEM):
    return pl.BlockSpec(memory_space=space)


def dot_last(a, b):
    return lax.dot_general(
        a, b, (((1,), (1,)), ((), ())), preferred_element_type=jnp.float32
    )


def ranks(peers, tile_ref, plane):
    nblk = tile_ref.shape[2]
    tile = tile_ref[plane]
    hit = (lax.broadcasted_iota(jnp.int32, (peers, nblk), 0) == tile).astype(jnp.float32)
    earlier = (
        lax.broadcasted_iota(jnp.int32, (nblk, nblk), 1)
        < lax.broadcasted_iota(jnp.int32, (nblk, nblk), 0)
    ).astype(jnp.float32).astype(jnp.bfloat16)
    before = dot_last(hit.astype(jnp.bfloat16), earlier)
    return tile, hit, jnp.sum(before * hit, axis=0, keepdims=True).astype(jnp.int32)


def want_kernel(peers, cap, tile_ref, row_ref, col_ref, req_ref):
    nblk = tile_ref.shape[2]
    relays, lanes = req_ref.shape
    lane = lax.broadcasted_iota(jnp.int32, (lanes, nblk), 0)
    rows = jnp.zeros((relays, lanes), jnp.float32)
    cols = jnp.zeros((relays, lanes), jnp.float32)
    for k in range(PLANES):
        tile, hit, rank = ranks(peers, tile_ref, k)
        here = lane == (rank + (tile // relays + 2 * k) * cap)
        zero = jnp.zeros((), jnp.float32)
        row = jnp.where(here, row_ref[k : k + 1, :].astype(jnp.float32), zero)
        col = jnp.where(here, col_ref[k : k + 1, :].astype(jnp.float32), zero)
        fold = (hit[:relays] + hit[relays:]).astype(jnp.bfloat16)
        rows += dot_last(fold, row.astype(jnp.bfloat16))
        cols += dot_last(fold, col.astype(jnp.bfloat16))
    req_ref[...] = rows.astype(jnp.int32) * 65536 + cols.astype(jnp.int32)


def want(tile_map, row_anchor, col_anchor, peers, cap):
    lanes = -(-PLANES * 2 * cap // 128) * 128
    return pl.pallas_call(
        functools.partial(want_kernel, peers, cap),
        out_shape=jax.ShapeDtypeStruct((peers // 2, lanes), jnp.int32),
        in_specs=[whole()] * 3,
        out_specs=whole(),
        name="want",
    )(tile_map, row_anchor, col_anchor)


def slot_kernel(peers, cap, direct, place_ref, tile_ref, slot_ref):
    relays = peers // 2
    for k in range(PLANES):
        tile, _, rank = ranks(peers, tile_ref, k)
        side = tile // relays
        relay = (tile - side * relays) ^ place_ref[1]
        if not direct:
            relay = (relay & 1) * (relays // 2) + (relay >> 1)
        far = (side != place_ref[0]).astype(jnp.int32)
        slot_ref[k : k + 1, :] = (far * relays + relay) * cap + rank


def find_slots(place, tile_map, peers, cap, direct):
    return pl.pallas_call(
        functools.partial(slot_kernel, peers, cap, direct),
        out_shape=jax.ShapeDtypeStruct((PLANES, tile_map.shape[2]), jnp.int32),
        in_specs=[whole(SMEM), whole()],
        out_specs=whole(),
        compiler_params=GRANT,
        name="slots",
    )(place, tile_map)


def cut_kernel(kinds, cap, place_ref, req_ref, *refs):
    sheet_refs, out_refs, half_ref = refs[: len(kinds)], refs[len(kinds) : -1], refs[-1]
    legs = len(out_refs) // len(kinds)
    parts = sheet_refs[0].shape[-1] // WC
    for at, sheet_ref in enumerate(sheet_refs):
        for c in range(2):
            for h in range(parts):
                part = sheet_ref[c, :, h * WC : (h + 1) * WC]
                half_ref[(at * 2 + c) * parts + h] = part.astype(jnp.float32)
    lane = lax.broadcasted_iota(jnp.int32, (WR, WC), 1)
    me = place_ref[1]
    span = req_ref.shape[0] // legs

    def one(now, carry):
        for at, (plane, mirrored) in enumerate(kinds):
            side = 1 - place_ref[0] if mirrored else place_ref[0]
            for m in range(legs):
                source = (m * span + now) ^ me
                for place in range(cap):
                    packed = req_ref[source, (2 * plane + side) * cap + place]
                    row = packed >> 16
                    col = packed & 65535
                    turn = (WC - col) & (WC - 1)
                    left = lane < WC - col
                    for c in range(2):
                        part = [
                            pltpu.roll(half_ref[(at * 2 + c) * parts + h, pl.ds(row, WR), :], turn, 1)
                            for h in range(parts)
                        ]
                        out_refs[at * legs + m][now * cap + place, c * WR : (c + 1) * WR, :] = jnp.where(
                            left, part[0], part[1]
                        ).astype(jnp.bfloat16)
        return carry

    lax.fori_loop(0, span, one, 0)


def cut(kinds, cap, legs, place, requests, sheets):
    count = requests.shape[0] // legs * cap
    height, width = sheets[0].shape[-2:]
    outs = pl.pallas_call(
        functools.partial(cut_kernel, kinds, cap),
        out_shape=(jax.ShapeDtypeStruct((count, 2 * WR, WC), jnp.bfloat16),) * (legs * len(kinds)),
        in_specs=[whole(SMEM), whole(SMEM)] + [whole()] * len(kinds),
        out_specs=(whole(),) * (legs * len(kinds)),
        scratch_shapes=[VMEM((len(kinds) * 2 * width // WC, height, WC), jnp.float32)],
        compiler_params=GRANT,
        name="cut",
    )(place, requests, *sheets)
    return [outs[at * legs : (at + 1) * legs] for at in range(len(kinds))]


def taps(pos):
    cell = jnp.floor(pos)
    f = pos - cell
    g = 1.0 - f
    f2, g2 = f * f, g * g
    value = (
        g2 * g / 6.0,
        2.0 / 3.0 - f2 + 0.5 * f2 * f,
        2.0 / 3.0 - g2 + 0.5 * g2 * g,
        f2 * f / 6.0,
    )
    slope = (-0.5 * g2, -2.0 * f + 1.5 * f2, 2.0 * g - 1.5 * g2, 0.5 * f2)
    return cell, value, slope


def interp_kernel(plane, slot_ref, win_ref, *refs):
    first, last = plane == 0, plane == PLANES - 1
    if first:
        x_ref, y_ref = refs[:2]
        refs = refs[2:]
    else:
        state_ref = refs[0]
        refs = refs[1:]
    if last:
        pos_out, jac_out = refs[:2]
        refs = refs[2:]
    else:
        state_out = refs[0]
        refs = refs[1:]
    tap_ref, res_ref = refs
    nblk, rays = res_ref.shape[1:]

    if first:
        px, py = x_ref[...], y_ref[...]
    else:
        px, py = state_ref[0], state_ref[1]
    for at, pos in ((0, px), (9, py)):
        cell, value, slope = taps(pos)
        tap_ref[at] = jnp.clip(cell, -4.0, WC + 4.0)
        for j in range(4):
            tap_ref[at + 1 + j] = value[j]
            tap_ref[at + 5 + j] = slope[j]

    def one(b, carry):
        def row(j):
            return tap_ref[j, pl.ds(b, 1), :]

        def spread(at, size, dtype):
            tile = 8 * 4 // jnp.dtype(dtype).itemsize

            def lay(j):
                return jnp.broadcast_to(row(j), (tile, rays)).astype(dtype)[None]

            place = lax.broadcasted_iota(jnp.int32, (size // tile, tile, rays), 0) * tile
            place = (place + lax.broadcasted_iota(jnp.int32, place.shape, 1)).astype(jnp.float32)
            near = place.astype(dtype) - lay(at)
            value = jnp.zeros(near.shape, dtype)
            slope = value
            for j in range(4):
                here = near == jnp.asarray(j - 1, dtype)
                value = jnp.where(here, lay(at + 1 + j), value)
                slope = jnp.where(here, lay(at + 5 + j), slope)
            return value.reshape(size, rays), slope.reshape(size, rays)

        kern = jnp.concatenate(spread(0, WC, jnp.bfloat16), axis=1)
        mixed = jnp.dot(win_ref[slot_ref[plane, b]], kern, preferred_element_type=jnp.float32)
        ky, kyd = spread(9, WR, jnp.float32)
        for c in range(2):
            part = mixed[c * WR : (c + 1) * WR]
            mixed0, mixed1 = part[:, :rays], part[:, rays:]
            for at, product in ((0, ky * mixed0), (2, ky * mixed1), (4, kyd * mixed0)):
                res_ref[at + c, pl.ds(b, 1), :] = jnp.sum(product, axis=0, keepdims=True)
        return carry

    lax.fori_loop(0, nblk, one, 0, unroll=16)

    ratio, strength = lens_ratio[plane], lens_strength[plane]
    ax, ay = res_ref[0], res_ref[1]
    hxx, hyx, hxy, hyy = res_ref[2], res_ref[3], res_ref[4], res_ref[5]
    if first:
        vx, vy = -strength * ax, -strength * ay
        dj = [-strength * h for h in (hxx, hxy, hyx, hyy)]
        jac = [1.0 + dj[0], dj[1], dj[2], 1.0 + dj[3]]
    else:
        vx = ratio * state_ref[2] - strength * ax
        vy = ratio * state_ref[3] - strength * ay
        axx, axy, ayx, ayy = [state_ref[4 + j] for j in range(4)]
        product = (
            hxx * axx + hxy * ayx,
            hxx * axy + hxy * ayy,
            hyx * axx + hyy * ayx,
            hyx * axy + hyy * ayy,
        )
        dj = [ratio * state_ref[8 + j] - strength * product[j] for j in range(4)]
        jac = [old + d for old, d in zip((axx, axy, ayx, ayy), dj)]
    px, py = px + vx, py + vy
    if last:
        pos_out[:, 0, :] = px
        pos_out[:, 1, :] = py
        for j in range(4):
            jac_out[:, j, :] = jac[j]
    else:
        for j, value in enumerate([px, py, vx, vy] + jac + dj):
            state_out[j] = value


def interp(plane, slots, windows, state):
    nblk = slots.shape[1]
    rays = state[0].shape[-1]
    if plane == PLANES - 1:
        out_shape = (
            jax.ShapeDtypeStruct((nblk, 2, rays), jnp.float32),
            jax.ShapeDtypeStruct((nblk, 4, rays), jnp.float32),
        )
    else:
        out_shape = (jax.ShapeDtypeStruct((12, nblk, rays), jnp.float32),)
    return pl.pallas_call(
        functools.partial(interp_kernel, plane),
        out_shape=out_shape,
        in_specs=[whole(SMEM), whole()] + [whole()] * len(state),
        out_specs=(whole(),) * len(out_shape),
        scratch_shapes=[
            VMEM((18, nblk, rays), jnp.float32),
            VMEM((6, nblk, rays), jnp.float32),
        ],
        compiler_params=GRANT,
    )(slots, windows, *state)


def body(start_x, start_y, gradients, tile_map, row_anchor, col_anchor):
    peers = lax.axis_size("sky")
    nblk = start_x.shape[0]
    cap = max(2, 2 * nblk // peers)
    relays = peers // 2
    chips = relays // 2
    direct = chips > 4 or chips & (chips - 1) != 0
    outs = 1 if direct else chips
    groups = [[h * relays + r for r in range(relays)] for h in range(2)]
    mirror_pairs = [(i, (i + relays) % peers) for i in range(peers)]

    def swap(bits):
        return [(i, i ^ bits) for i in range(peers)]

    def exchange(x):
        return lax.all_to_all(
            x, "sky", split_axis=0, concat_axis=0, axis_index_groups=groups, tiled=True
        )

    def ship(parts):
        if direct:
            got = exchange(parts[0].reshape(relays, cap, 2 * WR, WC))
            return [got.reshape(relays * cap, 2 * WR, WC)], []
        got = [parts[0]]
        for m in range(1, chips):
            got.append(lax.ppermute(parts[m], "sky", swap(2 * m)))
        return [part[:cap] for part in got], [part[cap:] for part in got]

    def across(lists):
        if not lists:
            return []
        got = lax.ppermute(jnp.concatenate(sum(lists, []), axis=0), "sky", swap(1))
        size = chips * cap
        return [[got[at * size : (at + 1) * size]] for at in range(len(lists))]

    def tile(plane, sheet):
        return sheet[plane]

    def mirror(plane):
        return lax.ppermute(sheets[plane], "sky", mirror_pairs)

    def cut_sent(*kinds):
        tiles_of = [mirrors[plane] if mirrored else sheets[plane] for plane, mirrored in kinds]
        parts = cut(kinds, cap, outs, place, asked, tiles_of)
        for (plane, mirrored), part in zip(kinds, parts):
            sent[plane, mirrored] = ship(part)

    index = lax.axis_index("sky").astype(jnp.int32)
    place = jnp.stack([index // relays, jnp.zeros_like(index) if direct else index % relays])
    tiles = tile_map.transpose(0, 2, 1)
    requests = want(tiles, row_anchor, col_anchor, peers, cap)
    requests, late = lax.optimization_barrier((requests, gradients))
    sheets = [tile(0, gradients)] + [tile(plane, late) for plane in range(1, PLANES)]
    mirrors = [mirror(plane) for plane in range(PLANES)]
    asked = exchange(requests)
    slots = find_slots(place, tiles, peers, cap, direct)
    sent = {}
    cut_sent((0, False))
    cut_sent((0, True))
    cut_sent(*[(plane, False) for plane in range(1, PLANES)])
    for plane in range(1, PLANES):
        cut_sent((plane, True))
    state = (start_x, start_y)
    for plane in range(PLANES):
        sets = (sent[plane, False], sent[plane, True])
        held = iter(across([other for _, other in sets if other]))
        windows = sum((mine + (next(held) if other else []) for mine, other in sets), [])
        state = interp(plane, slots, jnp.concatenate(windows, axis=0), state)
    return state


def solution(mesh):
    return jax.shard_map(
        body,
        mesh=mesh,
        in_specs=(
            P(("runs", "sky"), None),
            P(("runs", "sky"), None),
            P(None, None, ("runs", "sky"), None),
            P(None, ("runs", "sky"), None),
            P(None, ("runs", "sky")),
            P(None, ("runs", "sky")),
        ),
        out_specs=(P(("runs", "sky"), None, None), P(("runs", "sky"), None, None)),
        check_vma=False,
    )
```

```python
import functools

import jax
import jax.numpy as jnp
from jax import lax
from jax.experimental import pallas as pl
from jax.experimental.pallas import tpu as pltpu
from jax.sharding import PartitionSpec as P


WR = 16
WC = 128
PLANES = 3

lens_ratio = (0.85, 0.7, 0.9)
lens_strength = (0.5, 0.6, 0.45)

GRANT = pltpu.CompilerParams(vmem_limit_bytes=16 << 20)
VMEM = pltpu.VMEM
SMEM = pltpu.SMEM


def whole(space=VMEM):
    return pl.BlockSpec(memory_space=space)


def dot_last(a, b):
    return lax.dot_general(
        a, b, (((1,), (1,)), ((), ())), preferred_element_type=jnp.float32
    )


def ranks(peers, tile_ref, plane):
    nblk = tile_ref.shape[2]
    tile = tile_ref[plane]
    hit = (lax.broadcasted_iota(jnp.int32, (peers, nblk), 0) == tile).astype(jnp.float32)
    earlier = (
        lax.broadcasted_iota(jnp.int32, (nblk, nblk), 1)
        < lax.broadcasted_iota(jnp.int32, (nblk, nblk), 0)
    ).astype(jnp.float32).astype(jnp.bfloat16)
    before = dot_last(hit.astype(jnp.bfloat16), earlier)
    return tile, hit, jnp.sum(before * hit, axis=0, keepdims=True).astype(jnp.int32)


def want_kernel(peers, cap, tile_ref, row_ref, col_ref, req_ref):
    nblk = tile_ref.shape[2]
    relays, lanes = req_ref.shape
    lane = lax.broadcasted_iota(jnp.int32, (lanes, nblk), 0)
    rows = jnp.zeros((relays, lanes), jnp.float32)
    cols = jnp.zeros((relays, lanes), jnp.float32)
    for k in range(PLANES):
        tile, hit, rank = ranks(peers, tile_ref, k)
        here = lane == (rank + (tile // relays + 2 * k) * cap)
        zero = jnp.zeros((), jnp.float32)
        row = jnp.where(here, row_ref[k : k + 1, :].astype(jnp.float32), zero)
        col = jnp.where(here, col_ref[k : k + 1, :].astype(jnp.float32), zero)
        fold = (hit[:relays] + hit[relays:]).astype(jnp.bfloat16)
        rows += dot_last(fold, row.astype(jnp.bfloat16))
        cols += dot_last(fold, col.astype(jnp.bfloat16))
    req_ref[...] = rows.astype(jnp.int32) * 65536 + cols.astype(jnp.int32)


def want(tile_map, row_anchor, col_anchor, peers, cap):
    lanes = -(-PLANES * 2 * cap // 128) * 128
    return pl.pallas_call(
        functools.partial(want_kernel, peers, cap),
        out_shape=jax.ShapeDtypeStruct((peers // 2, lanes), jnp.int32),
        in_specs=[whole()] * 3,
        out_specs=whole(),
        name="want",
    )(tile_map, row_anchor, col_anchor)


def slot_kernel(planes, peers, cap, direct, place_ref, tile_ref, slot_ref):
    relays = peers // 2
    for at, k in enumerate(planes):
        tile, _, rank = ranks(peers, tile_ref, k)
        side = tile // relays
        relay = (tile - side * relays) ^ place_ref[1]
        if not direct:
            relay = (relay & 1) * (relays // 2) + (relay >> 1)
        far = (side != place_ref[0]).astype(jnp.int32)
        slot_ref[at : at + 1, :] = (far * relays + relay) * cap + rank


def find_slots(planes, place, tile_map, peers, cap, direct):
    return pl.pallas_call(
        functools.partial(slot_kernel, planes, peers, cap, direct),
        out_shape=jax.ShapeDtypeStruct((len(planes), tile_map.shape[2]), jnp.int32),
        in_specs=[whole(SMEM), whole()],
        out_specs=whole(),
        compiler_params=GRANT,
        name="find",
    )(place, tile_map)


def cut_kernel(plane, cap, kinds, place_ref, req_ref, *refs):
    sheet_refs, out_refs, half_ref = refs[: len(kinds)], refs[len(kinds) : -1], refs[-1]
    parts = sheet_refs[0].shape[-1] // WC
    for at, sheet_ref in enumerate(sheet_refs):
        for c in range(2):
            for h in range(parts):
                part = sheet_ref[c, :, h * WC : (h + 1) * WC]
                half_ref[(at * 2 + c) * parts + h] = part.astype(jnp.float32)
    lane = lax.broadcasted_iota(jnp.int32, (WR, WC), 1)
    me = place_ref[1]
    sides = [1 - place_ref[0] if mirrored else place_ref[0] for mirrored in kinds]
    span = req_ref.shape[0] // len(out_refs)

    def one(now, carry):
        for m, out_ref in enumerate(out_refs):
            source = (m * span + now) ^ me
            for at, side in enumerate(sides):
                for place in range(cap):
                    packed = req_ref[source, (2 * plane + side) * cap + place]
                    row = packed >> 16
                    col = packed & 65535
                    turn = (WC - col) & (WC - 1)
                    left = lane < WC - col
                    slot = (now * len(kinds) + at) * cap + place
                    for c in range(2):
                        part = [
                            pltpu.roll(half_ref[(at * 2 + c) * parts + h, pl.ds(row, WR), :], turn, 1)
                            for h in range(parts)
                        ]
                        out_ref[slot, c * WR : (c + 1) * WR, :] = jnp.where(
                            left, part[0], part[1]
                        ).astype(jnp.bfloat16)
        return carry

    lax.fori_loop(0, span, one, 0)


def cut(plane, cap, outs, kinds, place, requests, sheets):
    count = requests.shape[0] // outs * len(kinds) * cap
    height, width = sheets[0].shape[-2:]
    return pl.pallas_call(
        functools.partial(cut_kernel, plane, cap, kinds),
        out_shape=(jax.ShapeDtypeStruct((count, 2 * WR, WC), jnp.bfloat16),) * outs,
        in_specs=[whole(SMEM), whole(SMEM)] + [whole()] * len(kinds),
        out_specs=(whole(),) * outs,
        scratch_shapes=[VMEM((len(kinds) * 2 * width // WC, height, WC), jnp.float32)],
        compiler_params=GRANT,
        name="cut",
    )(place, requests, *sheets)


def taps(pos):
    cell = jnp.floor(pos)
    f = pos - cell
    g = 1.0 - f
    f2, g2 = f * f, g * g
    value = (
        g2 * g / 6.0,
        2.0 / 3.0 - f2 + 0.5 * f2 * f,
        2.0 / 3.0 - g2 + 0.5 * g2 * g,
        f2 * f / 6.0,
    )
    slope = (-0.5 * g2, -2.0 * f + 1.5 * f2, 2.0 * g - 1.5 * g2, 0.5 * f2)
    return cell, value, slope


def interp_kernel(plane, at_slots, slot_ref, win_ref, *refs):
    first, last = plane == 0, plane == PLANES - 1
    if first:
        x_ref, y_ref = refs[:2]
        refs = refs[2:]
    else:
        state_ref = refs[0]
        refs = refs[1:]
    if last:
        pos_out, jac_out = refs[:2]
        refs = refs[2:]
    else:
        state_out = refs[0]
        refs = refs[1:]
    tap_ref, res_ref = refs
    nblk, rays = res_ref.shape[1:]

    if first:
        px, py = x_ref[...], y_ref[...]
    else:
        px, py = state_ref[0], state_ref[1]
    for at, pos in ((0, px), (9, py)):
        cell, value, slope = taps(pos)
        tap_ref[at] = jnp.clip(cell, -4.0, WC + 4.0)
        for j in range(4):
            tap_ref[at + 1 + j] = value[j]
            tap_ref[at + 5 + j] = slope[j]

    def one(b, carry):
        def row(j):
            return tap_ref[j, pl.ds(b, 1), :]

        def spread(at, size, dtype):
            tile = 8 * 4 // jnp.dtype(dtype).itemsize

            def lay(j):
                return jnp.broadcast_to(row(j), (tile, rays)).astype(dtype)[None]

            place = lax.broadcasted_iota(jnp.int32, (size // tile, tile, rays), 0) * tile
            place = (place + lax.broadcasted_iota(jnp.int32, place.shape, 1)).astype(jnp.float32)
            near = place.astype(dtype) - lay(at)
            value = jnp.zeros(near.shape, dtype)
            slope = value
            for j in range(4):
                here = near == jnp.asarray(j - 1, dtype)
                value = jnp.where(here, lay(at + 1 + j), value)
                slope = jnp.where(here, lay(at + 5 + j), slope)
            return value.reshape(size, rays), slope.reshape(size, rays)

        kern = jnp.concatenate(spread(0, WC, jnp.bfloat16), axis=1)
        mixed = jnp.dot(win_ref[slot_ref[at_slots, b]], kern, preferred_element_type=jnp.float32)
        ky, kyd = spread(9, WR, jnp.float32)
        for c in range(2):
            part = mixed[c * WR : (c + 1) * WR]
            mixed0, mixed1 = part[:, :rays], part[:, rays:]
            for at, product in ((0, ky * mixed0), (2, ky * mixed1), (4, kyd * mixed0)):
                res_ref[at + c, pl.ds(b, 1), :] = jnp.sum(product, axis=0, keepdims=True)
        return carry

    lax.fori_loop(0, nblk, one, 0, unroll=16)

    ratio, strength = lens_ratio[plane], lens_strength[plane]
    ax, ay = res_ref[0], res_ref[1]
    hxx, hyx, hxy, hyy = res_ref[2], res_ref[3], res_ref[4], res_ref[5]
    if first:
        vx, vy = -strength * ax, -strength * ay
        dj = [-strength * h for h in (hxx, hxy, hyx, hyy)]
        jac = [1.0 + dj[0], dj[1], dj[2], 1.0 + dj[3]]
    else:
        vx = ratio * state_ref[2] - strength * ax
        vy = ratio * state_ref[3] - strength * ay
        axx, axy, ayx, ayy = [state_ref[4 + j] for j in range(4)]
        product = (
            hxx * axx + hxy * ayx,
            hxx * axy + hxy * ayy,
            hyx * axx + hyy * ayx,
            hyx * axy + hyy * ayy,
        )
        dj = [ratio * state_ref[8 + j] - strength * product[j] for j in range(4)]
        jac = [old + d for old, d in zip((axx, axy, ayx, ayy), dj)]
    px, py = px + vx, py + vy
    if last:
        pos_out[:, 0, :] = px
        pos_out[:, 1, :] = py
        for j in range(4):
            jac_out[:, j, :] = jac[j]
    else:
        for j, value in enumerate([px, py, vx, vy] + jac + dj):
            state_out[j] = value


def interp(plane, found, windows, state):
    slots, at_slots = found
    nblk = slots.shape[1]
    rays = state[0].shape[-1]
    if plane == PLANES - 1:
        out_shape = (
            jax.ShapeDtypeStruct((nblk, 2, rays), jnp.float32),
            jax.ShapeDtypeStruct((nblk, 4, rays), jnp.float32),
        )
    else:
        out_shape = (jax.ShapeDtypeStruct((12, nblk, rays), jnp.float32),)
    return pl.pallas_call(
        functools.partial(interp_kernel, plane, at_slots),
        out_shape=out_shape,
        in_specs=[whole(SMEM), whole()] + [whole()] * len(state),
        out_specs=(whole(),) * len(out_shape),
        scratch_shapes=[
            VMEM((18, nblk, rays), jnp.float32),
            VMEM((6, nblk, rays), jnp.float32),
        ],
        compiler_params=GRANT,
    )(slots, windows, *state)


def body(start_x, start_y, gradients, tile_map, row_anchor, col_anchor):
    peers = lax.axis_size("sky")
    nblk = start_x.shape[0]
    cap = max(2, 2 * nblk // peers)
    relays = peers // 2
    chips = relays // 2
    direct = chips > 4 or chips & (chips - 1) != 0
    outs = 1 if direct else chips
    groups = [[h * relays + r for r in range(relays)] for h in range(2)]
    mirror_pairs = [(i, (i + relays) % peers) for i in range(peers)]

    def swap(bits):
        return [(i, i ^ bits) for i in range(peers)]

    def exchange(x):
        return lax.all_to_all(
            x, "sky", split_axis=0, concat_axis=0, axis_index_groups=groups, tiled=True
        )

    def ship(parts, count):
        if direct:
            got = exchange(parts[0].reshape(relays, -1, 2 * WR, WC))
            got = got.reshape(relays, count, cap, 2 * WR, WC)
            return [([got[:, at].reshape(relays * cap, 2 * WR, WC)], []) for at in range(count)]
        got = [parts[0]]
        step = relays // len(parts)
        for m in range(1, len(parts)):
            got.append(lax.ppermute(parts[m], "sky", swap(step * m)))

        def pieces(at, of=got):
            return [part[at * cap : (at + 1) * cap] for part in of]

        if step == 1:
            return [(pieces(at, got[::2] + got[1::2]), []) for at in range(count)]
        return [(pieces(at), pieces(count + at)) for at in range(count)]

    def across(lists):
        if not lists:
            return []
        got = lax.ppermute(jnp.concatenate(sum(lists, []), axis=0), "sky", swap(1))
        size = chips * cap
        return [[got[at * size : (at + 1) * size]] for at in range(len(lists))]

    def tile(plane, sheet):
        return sheet[plane]

    def mirror(plane):
        return lax.ppermute(sheets[plane], "sky", mirror_pairs)

    def cut_sent(plane, kinds, straight=False):
        count = outs * 2 if straight and not direct else outs
        tiles_of = [mirrors[plane] if mirrored else sheets[plane] for mirrored in kinds]
        parts = cut(plane, cap, count, kinds, place, asked, tiles_of)
        return ship(parts, len(kinds))

    index = lax.axis_index("sky").astype(jnp.int32)
    place = jnp.stack([index // relays, jnp.zeros_like(index) if direct else index % relays])
    tiles = tile_map.transpose(0, 2, 1)
    requests = want(tiles, row_anchor, col_anchor, peers, cap)
    requests, late = lax.optimization_barrier((requests, gradients))
    sheets = [tile(0, gradients)] + [tile(plane, late) for plane in range(1, PLANES)]
    mirrors = [mirror(plane) for plane in range(PLANES)]
    asked = exchange(requests)
    slots = [(find_slots((0,), place, tiles, peers, cap, direct), 0)]
    more = find_slots(tuple(range(1, PLANES)), place, tiles, peers, cap, direct)
    slots += [(more, at) for at in range(PLANES - 1)]
    sent = []
    for plane in range(PLANES - 1):
        sent.append(cut_sent(plane, (False,)) + cut_sent(plane, (True,)))
    sent.append(cut_sent(PLANES - 1, (False, True), True))
    state = (start_x, start_y)
    for plane in range(PLANES):
        sets = sent[plane]
        held = iter(across([other for _, other in sets if other]))
        windows = sum((mine + (next(held) if other else []) for mine, other in sets), [])
        state = interp(plane, slots[plane], jnp.concatenate(windows, axis=0), state)
    return state


def solution(mesh):
    return jax.shard_map(
        body,
        mesh=mesh,
        in_specs=(
            P(("runs", "sky"), None),
            P(("runs", "sky"), None),
            P(None, None, ("runs", "sky"), None),
            P(None, ("runs", "sky"), None),
            P(None, ("runs", "sky")),
            P(None, ("runs", "sky")),
        ),
        out_specs=(P(("runs", "sky"), None, None), P(("runs", "sky"), None, None)),
        check_vma=False,
    )
```

```python
import functools

import jax
import jax.numpy as jnp
from jax import lax
from jax.experimental import pallas as pl
from jax.experimental.pallas import tpu as pltpu
from jax.sharding import PartitionSpec as P


WR = 16
WC = 128
PLANES = 3

lens_ratio = (0.85, 0.7, 0.9)
lens_strength = (0.5, 0.6, 0.45)

GRANT = pltpu.CompilerParams(vmem_limit_bytes=16 << 20)
VMEM = pltpu.VMEM
SMEM = pltpu.SMEM


def whole(space=VMEM):
    return pl.BlockSpec(memory_space=space)


def dot_last(a, b):
    return lax.dot_general(
        a, b, (((1,), (1,)), ((), ())), preferred_element_type=jnp.float32
    )


def ranks(peers, tile_ref, plane):
    nblk = tile_ref.shape[2]
    tile = tile_ref[plane]
    hit = (lax.broadcasted_iota(jnp.int32, (peers, nblk), 0) == tile).astype(jnp.float32)
    earlier = (
        lax.broadcasted_iota(jnp.int32, (nblk, nblk), 1)
        < lax.broadcasted_iota(jnp.int32, (nblk, nblk), 0)
    ).astype(jnp.float32).astype(jnp.bfloat16)
    before = dot_last(hit.astype(jnp.bfloat16), earlier)
    return tile, hit, jnp.sum(before * hit, axis=0, keepdims=True).astype(jnp.int32)


def want_kernel(peers, cap, tile_ref, row_ref, col_ref, req_ref):
    nblk = tile_ref.shape[2]
    relays, lanes = req_ref.shape
    lane = lax.broadcasted_iota(jnp.int32, (lanes, nblk), 0)
    rows = jnp.zeros((relays, lanes), jnp.float32)
    cols = jnp.zeros((relays, lanes), jnp.float32)
    for k in range(PLANES):
        tile, hit, rank = ranks(peers, tile_ref, k)
        here = lane == (rank + (tile // relays + 2 * k) * cap)
        zero = jnp.zeros((), jnp.float32)
        row = jnp.where(here, row_ref[k : k + 1, :].astype(jnp.float32), zero)
        col = jnp.where(here, col_ref[k : k + 1, :].astype(jnp.float32), zero)
        fold = (hit[:relays] + hit[relays:]).astype(jnp.bfloat16)
        rows += dot_last(fold, row.astype(jnp.bfloat16))
        cols += dot_last(fold, col.astype(jnp.bfloat16))
    req_ref[...] = rows.astype(jnp.int32) * 65536 + cols.astype(jnp.int32)


def want(tile_map, row_anchor, col_anchor, peers, cap):
    lanes = -(-PLANES * 2 * cap // 128) * 128
    return pl.pallas_call(
        functools.partial(want_kernel, peers, cap),
        out_shape=jax.ShapeDtypeStruct((peers // 2, lanes), jnp.int32),
        in_specs=[whole()] * 3,
        out_specs=whole(),
        name="want",
    )(tile_map, row_anchor, col_anchor)


def slot_kernel(peers, cap, direct, place_ref, tile_ref, *refs):
    start_refs, slot_ref, moved_refs, sem = refs[:2], refs[2], refs[3:5], refs[5]
    moves = [
        pltpu.make_async_copy(src, dst, sem.at[at])
        for at, (src, dst) in enumerate(zip(start_refs, moved_refs))
    ]
    for move in moves:
        move.start()
    relays = peers // 2
    for k in range(PLANES):
        tile, _, rank = ranks(peers, tile_ref, k)
        side = tile // relays
        relay = (tile - side * relays) ^ place_ref[1]
        if not direct:
            relay = (relay & 1) * (relays // 2) + (relay >> 1)
        far = (side != place_ref[0]).astype(jnp.int32)
        slot_ref[k : k + 1, :] = (far * relays + relay) * cap + rank
    for move in moves:
        move.wait()


def find_slots(place, tile_map, start, peers, cap, direct):
    shapes = [jax.ShapeDtypeStruct((PLANES, tile_map.shape[2]), jnp.int32)]
    shapes += [jax.ShapeDtypeStruct(x.shape, x.dtype) for x in start]
    return pl.pallas_call(
        functools.partial(slot_kernel, peers, cap, direct),
        out_shape=tuple(shapes),
        in_specs=[whole(SMEM), whole()] + [whole(pltpu.MemorySpace.HBM)] * 2,
        out_specs=(whole(),) * 3,
        scratch_shapes=[pltpu.SemaphoreType.DMA((2,))],
        compiler_params=GRANT,
        name="slots",
    )(place, tile_map, *start)


def cut_kernel(planes, cap, mirrored, place_ref, req_ref, *refs):
    sheet_refs, out_refs, half_ref = refs[: len(planes)], refs[len(planes) : -1], refs[-1]
    parts = sheet_refs[0].shape[-1] // WC
    for at, sheet_ref in enumerate(sheet_refs):
        for c in range(2):
            for h in range(parts):
                part = sheet_ref[c, :, h * WC : (h + 1) * WC]
                half_ref[(at * 2 + c) * parts + h] = part.astype(jnp.float32)
    lane = lax.broadcasted_iota(jnp.int32, (WR, WC), 1)
    me = place_ref[1]
    side = 1 - place_ref[0] if mirrored else place_ref[0]
    span = req_ref.shape[0] // len(out_refs)

    def one(now, carry):
        for m, out_ref in enumerate(out_refs):
            source = (m * span + now) ^ me
            for at, k in enumerate(planes):
                for place in range(cap):
                    packed = req_ref[source, (2 * k + side) * cap + place]
                    row = packed >> 16
                    col = packed & 65535
                    turn = (WC - col) & (WC - 1)
                    left = lane < WC - col
                    slot = (now * len(planes) + at) * cap + place
                    for c in range(2):
                        part = [
                            pltpu.roll(half_ref[(at * 2 + c) * parts + h, pl.ds(row, WR), :], turn, 1)
                            for h in range(parts)
                        ]
                        out_ref[slot, c * WR : (c + 1) * WR, :] = jnp.where(
                            left, part[0], part[1]
                        ).astype(jnp.bfloat16)
        return carry

    lax.fori_loop(0, span, one, 0)


def cut(planes, cap, outs, mirrored, place, requests, sheets):
    count = requests.shape[0] // outs * len(planes) * cap
    height, width = sheets[0].shape[-2:]
    return pl.pallas_call(
        functools.partial(cut_kernel, planes, cap, mirrored),
        out_shape=(jax.ShapeDtypeStruct((count, 2 * WR, WC), jnp.bfloat16),) * outs,
        in_specs=[whole(SMEM), whole(SMEM)] + [whole()] * len(planes),
        out_specs=(whole(),) * outs,
        scratch_shapes=[VMEM((len(planes) * 2 * width // WC, height, WC), jnp.float32)],
        compiler_params=GRANT,
        name="cut",
    )(place, requests, *sheets)


def taps(pos):
    cell = jnp.floor(pos)
    f = pos - cell
    g = 1.0 - f
    f2, g2 = f * f, g * g
    value = (
        g2 * g / 6.0,
        2.0 / 3.0 - f2 + 0.5 * f2 * f,
        2.0 / 3.0 - g2 + 0.5 * g2 * g,
        f2 * f / 6.0,
    )
    slope = (-0.5 * g2, -2.0 * f + 1.5 * f2, 2.0 * g - 1.5 * g2, 0.5 * f2)
    return cell, value, slope


def interp_kernel(plane, slot_ref, win_ref, *refs):
    first, last = plane == 0, plane == PLANES - 1
    if first:
        x_ref, y_ref = refs[:2]
        refs = refs[2:]
    else:
        state_ref = refs[0]
        refs = refs[1:]
    if last:
        pos_out, jac_out = refs[:2]
        refs = refs[2:]
    else:
        state_out = refs[0]
        refs = refs[1:]
    tap_ref, res_ref = refs
    nblk, rays = res_ref.shape[1:]

    if first:
        px, py = x_ref[...], y_ref[...]
    else:
        px, py = state_ref[0], state_ref[1]
    for at, pos in ((0, px), (9, py)):
        cell, value, slope = taps(pos)
        tap_ref[at] = jnp.clip(cell, -4.0, WC + 4.0)
        for j in range(4):
            tap_ref[at + 1 + j] = value[j]
            tap_ref[at + 5 + j] = slope[j]

    def one(b, carry):
        def row(j):
            return tap_ref[j, pl.ds(b, 1), :]

        def spread(at, size, dtype):
            tile = 8 * 4 // jnp.dtype(dtype).itemsize

            def lay(j):
                return jnp.broadcast_to(row(j), (tile, rays)).astype(dtype)[None]

            place = lax.broadcasted_iota(jnp.int32, (size // tile, tile, rays), 0) * tile
            place = (place + lax.broadcasted_iota(jnp.int32, place.shape, 1)).astype(jnp.float32)
            near = place.astype(dtype) - lay(at)
            value = jnp.zeros(near.shape, dtype)
            slope = value
            for j in range(4):
                here = near == jnp.asarray(j - 1, dtype)
                value = jnp.where(here, lay(at + 1 + j), value)
                slope = jnp.where(here, lay(at + 5 + j), slope)
            return value.reshape(size, rays), slope.reshape(size, rays)

        kern = jnp.concatenate(spread(0, WC, jnp.bfloat16), axis=1)
        mixed = jnp.dot(win_ref[slot_ref[plane, b]], kern, preferred_element_type=jnp.float32)
        ky, kyd = spread(9, WR, jnp.float32)
        for c in range(2):
            part = mixed[c * WR : (c + 1) * WR]
            mixed0, mixed1 = part[:, :rays], part[:, rays:]
            for at, product in ((0, ky * mixed0), (2, ky * mixed1), (4, kyd * mixed0)):
                res_ref[at + c, pl.ds(b, 1), :] = jnp.sum(product, axis=0, keepdims=True)
        return carry

    lax.fori_loop(0, nblk, one, 0, unroll=16)

    ratio, strength = lens_ratio[plane], lens_strength[plane]
    ax, ay = res_ref[0], res_ref[1]
    hxx, hyx, hxy, hyy = res_ref[2], res_ref[3], res_ref[4], res_ref[5]
    if first:
        vx, vy = -strength * ax, -strength * ay
        dj = [-strength * h for h in (hxx, hxy, hyx, hyy)]
        jac = [1.0 + dj[0], dj[1], dj[2], 1.0 + dj[3]]
    else:
        vx = ratio * state_ref[2] - strength * ax
        vy = ratio * state_ref[3] - strength * ay
        axx, axy, ayx, ayy = [state_ref[4 + j] for j in range(4)]
        product = (
            hxx * axx + hxy * ayx,
            hxx * axy + hxy * ayy,
            hyx * axx + hyy * ayx,
            hyx * axy + hyy * ayy,
        )
        dj = [ratio * state_ref[8 + j] - strength * product[j] for j in range(4)]
        jac = [old + d for old, d in zip((axx, axy, ayx, ayy), dj)]
    px, py = px + vx, py + vy
    if last:
        pos_out[:, 0, :] = px
        pos_out[:, 1, :] = py
        for j in range(4):
            jac_out[:, j, :] = jac[j]
    else:
        for j, value in enumerate([px, py, vx, vy] + jac + dj):
            state_out[j] = value


def interp(plane, slots, windows, state):
    nblk = slots.shape[1]
    rays = state[0].shape[-1]
    if plane == PLANES - 1:
        out_shape = (
            jax.ShapeDtypeStruct((nblk, 2, rays), jnp.float32),
            jax.ShapeDtypeStruct((nblk, 4, rays), jnp.float32),
        )
    else:
        out_shape = (jax.ShapeDtypeStruct((12, nblk, rays), jnp.float32),)
    return pl.pallas_call(
        functools.partial(interp_kernel, plane),
        out_shape=out_shape,
        in_specs=[whole(SMEM), whole()] + [whole()] * len(state),
        out_specs=(whole(),) * len(out_shape),
        scratch_shapes=[
            VMEM((18, nblk, rays), jnp.float32),
            VMEM((6, nblk, rays), jnp.float32),
        ],
        compiler_params=GRANT,
    )(slots, windows, *state)


def body(start_x, start_y, gradients, tile_map, row_anchor, col_anchor):
    peers = lax.axis_size("sky")
    nblk = start_x.shape[0]
    cap = max(2, 2 * nblk // peers)
    relays = peers // 2
    chips = relays // 2
    direct = chips > 4 or chips & (chips - 1) != 0
    outs = 1 if direct else chips
    groups = [[h * relays + r for r in range(relays)] for h in range(2)]
    mirror_pairs = [(i, (i + relays) % peers) for i in range(peers)]

    def swap(bits):
        return [(i, i ^ bits) for i in range(peers)]

    def exchange(x):
        return lax.all_to_all(
            x, "sky", split_axis=0, concat_axis=0, axis_index_groups=groups, tiled=True
        )

    def ship(parts, count):
        if direct:
            got = exchange(parts[0].reshape(relays, -1, 2 * WR, WC))
            got = got.reshape(relays, count, cap, 2 * WR, WC)
            return [([got[:, at].reshape(relays * cap, 2 * WR, WC)], []) for at in range(count)]
        got = [parts[0]]
        step = relays // len(parts)
        for m in range(1, len(parts)):
            got.append(lax.ppermute(parts[m], "sky", swap(step * m)))
        if step == 1:
            return [(got[::2] + got[1::2], [])]

        def pieces(at):
            return [part[at * cap : (at + 1) * cap] for part in got]

        return [(pieces(at), pieces(count + at)) for at in range(count)]

    def across(lists):
        if not lists:
            return []
        got = lax.ppermute(jnp.concatenate(sum(lists, []), axis=0), "sky", swap(1))
        size = chips * cap
        return [[got[at * size : (at + 1) * size]] for at in range(len(lists))]

    def tile(plane, sheet):
        return sheet[plane]

    def mirror(plane):
        return lax.ppermute(sheets[plane], "sky", mirror_pairs)

    def cut_sent(plane, mirrored, sheet, straight=False):
        count = outs * 2 if straight and not direct else outs
        parts = cut((plane,), cap, count, mirrored, place, asked, (sheet,))
        return ship(parts, 1)[0]

    index = lax.axis_index("sky").astype(jnp.int32)
    place = jnp.stack([index // relays, jnp.zeros_like(index) if direct else index % relays])
    tiles = tile_map.transpose(0, 2, 1)
    requests = want(tiles, row_anchor, col_anchor, peers, cap)
    requests, late = lax.optimization_barrier((requests, gradients))
    sheets = [tile(0, gradients)] + [tile(plane, late) for plane in range(1, PLANES)]
    mirrors = [mirror(plane) for plane in range(PLANES)]
    asked = exchange(requests)
    slots, *state = find_slots(place, tiles, (start_x, start_y), peers, cap, direct)
    own, far = [], []
    for plane in range(PLANES):
        own.append(cut_sent(plane, False, sheets[plane]))
        far.append(cut_sent(plane, True, mirrors[plane], plane == PLANES - 1))
    for plane in range(PLANES):
        sets = (own[plane], far[plane])
        held = iter(across([other for _, other in sets if other]))
        windows = sum((mine + (next(held) if other else []) for mine, other in sets), [])
        state = interp(plane, slots, jnp.concatenate(windows, axis=0), state)
    return state


def solution(mesh):
    return jax.shard_map(
        body,
        mesh=mesh,
        in_specs=(
            P(("runs", "sky"), None),
            P(("runs", "sky"), None),
            P(None, None, ("runs", "sky"), None),
            P(None, ("runs", "sky"), None),
            P(None, ("runs", "sky")),
            P(None, ("runs", "sky")),
        ),
        out_specs=(P(("runs", "sky"), None, None), P(("runs", "sky"), None, None)),
        check_vma=False,
    )
```

```python
import functools

import jax
import jax.numpy as jnp
from jax import lax
from jax.experimental import pallas as pl
from jax.experimental.pallas import tpu as pltpu
from jax.sharding import PartitionSpec as P


WR = 16
WC = 128
PLANES = 3

lens_ratio = (0.85, 0.7, 0.9)
lens_strength = (0.5, 0.6, 0.45)

GRANT = pltpu.CompilerParams(vmem_limit_bytes=16 << 20)
VMEM = pltpu.VMEM
SMEM = pltpu.SMEM


def whole(space=VMEM):
    return pl.BlockSpec(memory_space=space)


def dot_last(a, b):
    return lax.dot_general(
        a, b, (((1,), (1,)), ((), ())), preferred_element_type=jnp.float32
    )


def ranks(peers, tile_ref, plane):
    nblk = tile_ref.shape[2]
    tile = tile_ref[plane]
    hit = (lax.broadcasted_iota(jnp.int32, (peers, nblk), 0) == tile).astype(jnp.float32)
    earlier = (
        lax.broadcasted_iota(jnp.int32, (nblk, nblk), 1)
        < lax.broadcasted_iota(jnp.int32, (nblk, nblk), 0)
    ).astype(jnp.float32).astype(jnp.bfloat16)
    before = dot_last(hit.astype(jnp.bfloat16), earlier)
    return tile, hit, jnp.sum(before * hit, axis=0, keepdims=True).astype(jnp.int32)


def want_kernel(peers, cap, near, place_ref, tile_ref, row_ref, col_ref, req_ref):
    nblk = tile_ref.shape[2]
    relays, lanes = req_ref.shape
    lane = lax.broadcasted_iota(jnp.int32, (lanes, nblk), 0)
    rows = jnp.zeros((relays, lanes), jnp.float32)
    cols = jnp.zeros((relays, lanes), jnp.float32)
    for k in range(PLANES):
        tile, _, rank = ranks(peers, tile_ref, k)
        side = tile // relays
        relay = tile - side * relays
        group = side + 2 * k
        if near and k == 0:
            turn = ((relay ^ place_ref[1]) & near) * (side == place_ref[0]).astype(jnp.int32)
            relay = relay ^ turn
            group = jnp.where(turn != 0, 2 * PLANES + side, group)
        here = lane == (rank + group * cap)
        zero = jnp.zeros((), jnp.float32)
        row = jnp.where(here, row_ref[k : k + 1, :].astype(jnp.float32), zero)
        col = jnp.where(here, col_ref[k : k + 1, :].astype(jnp.float32), zero)
        fold = lax.broadcasted_iota(jnp.int32, (relays, nblk), 0) == relay
        fold = fold.astype(jnp.float32).astype(jnp.bfloat16)
        rows += dot_last(fold, row.astype(jnp.bfloat16))
        cols += dot_last(fold, col.astype(jnp.bfloat16))
    req_ref[...] = rows.astype(jnp.int32) * 65536 + cols.astype(jnp.int32)


def want(place, tile_map, row_anchor, col_anchor, peers, cap, near):
    lanes = -(-(PLANES + 1) * 2 * cap // 128) * 128
    return pl.pallas_call(
        functools.partial(want_kernel, peers, cap, near),
        out_shape=jax.ShapeDtypeStruct((peers // 2, lanes), jnp.int32),
        in_specs=[whole(SMEM)] + [whole()] * 3,
        out_specs=whole(),
        name="want",
    )(place, tile_map, row_anchor, col_anchor)


def slot_kernel(peers, cap, direct, place_ref, tile_ref, *refs):
    start_refs, slot_ref, moved_refs, sem = refs[:2], refs[2], refs[3:5], refs[5]
    moves = [
        pltpu.make_async_copy(src, dst, sem.at[at])
        for at, (src, dst) in enumerate(zip(start_refs, moved_refs))
    ]
    for move in moves:
        move.start()
    relays = peers // 2
    for k in range(PLANES):
        tile, _, rank = ranks(peers, tile_ref, k)
        side = tile // relays
        relay = (tile - side * relays) ^ place_ref[1]
        if not direct:
            relay = (relay & 1) * (relays // 2) + (relay >> 1)
        far = (side != place_ref[0]).astype(jnp.int32)
        slot_ref[k : k + 1, :] = (far * relays + relay) * cap + rank
    for move in moves:
        move.wait()


def find_slots(place, tile_map, start, peers, cap, direct):
    shapes = [jax.ShapeDtypeStruct((PLANES, tile_map.shape[2]), jnp.int32)]
    shapes += [jax.ShapeDtypeStruct(x.shape, x.dtype) for x in start]
    return pl.pallas_call(
        functools.partial(slot_kernel, peers, cap, direct),
        out_shape=tuple(shapes),
        in_specs=[whole(SMEM), whole()] + [whole(pltpu.MemorySpace.HBM)] * 2,
        out_specs=(whole(),) * 3,
        scratch_shapes=[pltpu.SemaphoreType.DMA((2,))],
        compiler_params=GRANT,
        name="slots",
    )(place, tile_map, *start)


def cut_kernel(planes, cap, mirrored, span, place_ref, req_ref, *refs):
    sheet_refs, out_refs, half_ref = refs[: len(planes)], refs[len(planes) : -1], refs[-1]
    parts = sheet_refs[0].shape[-1] // WC
    for at, sheet_ref in enumerate(sheet_refs):
        for c in range(2):
            for h in range(parts):
                part = sheet_ref[c, :, h * WC : (h + 1) * WC]
                half_ref[(at * 2 + c) * parts + h] = part.astype(jnp.float32)
    lane = lax.broadcasted_iota(jnp.int32, (WR, WC), 1)
    me = place_ref[1]
    side = 1 - place_ref[0] if mirrored else place_ref[0]

    def one(now, carry):
        for m, out_ref in enumerate(out_refs):
            source = (m * span + now) ^ me
            for at, k in enumerate(planes):
                for place in range(cap):
                    packed = req_ref[source, (2 * k + side) * cap + place]
                    row = packed >> 16
                    col = packed & 65535
                    turn = (WC - col) & (WC - 1)
                    left = lane < WC - col
                    slot = (now * len(planes) + at) * cap + place
                    for c in range(2):
                        part = [
                            pltpu.roll(half_ref[(at * 2 + c) * parts + h, pl.ds(row, WR), :], turn, 1)
                            for h in range(parts)
                        ]
                        out_ref[slot, c * WR : (c + 1) * WR, :] = jnp.where(
                            left, part[0], part[1]
                        ).astype(jnp.bfloat16)
        return carry

    lax.fori_loop(0, span, one, 0)


def cut(planes, cap, outs, span, mirrored, place, requests, sheets):
    count = span * len(planes) * cap
    height, width = sheets[0].shape[-2:]
    return pl.pallas_call(
        functools.partial(cut_kernel, planes, cap, mirrored, span),
        out_shape=(jax.ShapeDtypeStruct((count, 2 * WR, WC), jnp.bfloat16),) * outs,
        in_specs=[whole(SMEM), whole(SMEM)] + [whole()] * len(planes),
        out_specs=(whole(),) * outs,
        scratch_shapes=[VMEM((len(planes) * 2 * width // WC, height, WC), jnp.float32)],
        compiler_params=GRANT,
        name="cut",
    )(place, requests, *sheets)


def taps(pos):
    cell = jnp.floor(pos)
    f = pos - cell
    g = 1.0 - f
    f2, g2 = f * f, g * g
    value = (
        g2 * g / 6.0,
        2.0 / 3.0 - f2 + 0.5 * f2 * f,
        2.0 / 3.0 - g2 + 0.5 * g2 * g,
        f2 * f / 6.0,
    )
    slope = (-0.5 * g2, -2.0 * f + 1.5 * f2, 2.0 * g - 1.5 * g2, 0.5 * f2)
    return cell, value, slope


def interp_kernel(plane, slot_ref, win_ref, *refs):
    first, last = plane == 0, plane == PLANES - 1
    if first:
        x_ref, y_ref = refs[:2]
        refs = refs[2:]
    else:
        state_ref = refs[0]
        refs = refs[1:]
    if last:
        pos_out, jac_out = refs[:2]
        refs = refs[2:]
    else:
        state_out = refs[0]
        refs = refs[1:]
    tap_ref, res_ref = refs
    nblk, rays = res_ref.shape[1:]

    if first:
        px, py = x_ref[...], y_ref[...]
    else:
        px, py = state_ref[0], state_ref[1]
    for at, pos in ((0, px), (9, py)):
        cell, value, slope = taps(pos)
        tap_ref[at] = jnp.clip(cell, -4.0, WC + 4.0)
        for j in range(4):
            tap_ref[at + 1 + j] = value[j]
            tap_ref[at + 5 + j] = slope[j]

    def one(b, carry):
        def row(j):
            return tap_ref[j, pl.ds(b, 1), :]

        def spread(at, size, dtype):
            tile = 8 * 4 // jnp.dtype(dtype).itemsize

            def lay(j):
                return jnp.broadcast_to(row(j), (tile, rays)).astype(dtype)[None]

            place = lax.broadcasted_iota(jnp.int32, (size // tile, tile, rays), 0) * tile
            place = (place + lax.broadcasted_iota(jnp.int32, place.shape, 1)).astype(jnp.float32)
            near = place.astype(dtype) - lay(at)
            value = jnp.zeros(near.shape, dtype)
            slope = value
            for j in range(4):
                here = near == jnp.asarray(j - 1, dtype)
                value = jnp.where(here, lay(at + 1 + j), value)
                slope = jnp.where(here, lay(at + 5 + j), slope)
            return value.reshape(size, rays), slope.reshape(size, rays)

        kern = jnp.concatenate(spread(0, WC, jnp.bfloat16), axis=1)
        mixed = jnp.dot(win_ref[slot_ref[plane, b]], kern, preferred_element_type=jnp.float32)
        ky, kyd = spread(9, WR, jnp.float32)
        for c in range(2):
            part = mixed[c * WR : (c + 1) * WR]
            mixed0, mixed1 = part[:, :rays], part[:, rays:]
            for at, product in ((0, ky * mixed0), (2, ky * mixed1), (4, kyd * mixed0)):
                res_ref[at + c, pl.ds(b, 1), :] = jnp.sum(product, axis=0, keepdims=True)
        return carry

    lax.fori_loop(0, nblk, one, 0, unroll=16)

    ratio, strength = lens_ratio[plane], lens_strength[plane]
    ax, ay = res_ref[0], res_ref[1]
    hxx, hyx, hxy, hyy = res_ref[2], res_ref[3], res_ref[4], res_ref[5]
    if first:
        vx, vy = -strength * ax, -strength * ay
        dj = [-strength * h for h in (hxx, hxy, hyx, hyy)]
        jac = [1.0 + dj[0], dj[1], dj[2], 1.0 + dj[3]]
    else:
        vx = ratio * state_ref[2] - strength * ax
        vy = ratio * state_ref[3] - strength * ay
        axx, axy, ayx, ayy = [state_ref[4 + j] for j in range(4)]
        product = (
            hxx * axx + hxy * ayx,
            hxx * axy + hxy * ayy,
            hyx * axx + hyy * ayx,
            hyx * axy + hyy * ayy,
        )
        dj = [ratio * state_ref[8 + j] - strength * product[j] for j in range(4)]
        jac = [old + d for old, d in zip((axx, axy, ayx, ayy), dj)]
    px, py = px + vx, py + vy
    if last:
        pos_out[:, 0, :] = px
        pos_out[:, 1, :] = py
        for j in range(4):
            jac_out[:, j, :] = jac[j]
    else:
        for j, value in enumerate([px, py, vx, vy] + jac + dj):
            state_out[j] = value


def interp(plane, slots, windows, state):
    nblk = slots.shape[1]
    rays = state[0].shape[-1]
    if plane == PLANES - 1:
        out_shape = (
            jax.ShapeDtypeStruct((nblk, 2, rays), jnp.float32),
            jax.ShapeDtypeStruct((nblk, 4, rays), jnp.float32),
        )
    else:
        out_shape = (jax.ShapeDtypeStruct((12, nblk, rays), jnp.float32),)
    return pl.pallas_call(
        functools.partial(interp_kernel, plane),
        out_shape=out_shape,
        in_specs=[whole(SMEM), whole()] + [whole()] * len(state),
        out_specs=(whole(),) * len(out_shape),
        scratch_shapes=[
            VMEM((18, nblk, rays), jnp.float32),
            VMEM((6, nblk, rays), jnp.float32),
        ],
        compiler_params=GRANT,
    )(slots, windows, *state)


def body(start_x, start_y, gradients, tile_map, row_anchor, col_anchor):
    peers = lax.axis_size("sky")
    nblk = start_x.shape[0]
    cap = max(2, 2 * nblk // peers)
    relays = peers // 2
    chips = relays // 2
    direct = chips > 4 or chips & (chips - 1) != 0
    outs = 1 if direct else chips
    near = relays // 2 if chips == 4 else 0
    groups = [[h * relays + r for r in range(relays)] for h in range(2)]
    mirror_pairs = [(i, (i + relays) % peers) for i in range(peers)]

    def swap(bits):
        return [(i, i ^ bits) for i in range(peers)]

    def exchange(x):
        return lax.all_to_all(
            x, "sky", split_axis=0, concat_axis=0, axis_index_groups=groups, tiled=True
        )

    def ship(parts, count, step):
        if direct:
            got = exchange(parts[0].reshape(relays, -1, 2 * WR, WC))
            got = got.reshape(relays, count, cap, 2 * WR, WC)
            return [([got[:, at].reshape(relays * cap, 2 * WR, WC)], []) for at in range(count)]
        got = [parts[0]]
        for m in range(1, len(parts)):
            got.append(lax.ppermute(parts[m], "sky", swap(step * m)))
        if step == 1:
            return [(got[::2] + got[1::2], [])]

        def pieces(at):
            return [part[at * cap : (at + 1) * cap] for part in got]

        return [(pieces(at), pieces(count + at)) for at in range(count)]

    def across(lists):
        if not lists:
            return []
        got = lax.ppermute(jnp.concatenate(sum(lists, []), axis=0), "sky", swap(1))
        size = chips * cap
        return [[got[at * size : (at + 1) * size]] for at in range(len(lists))]

    def tile(plane, sheet):
        return sheet[plane]

    def mirror(plane):
        return lax.ppermute(sheets[plane], "sky", mirror_pairs)

    def cut_sent(plane, mirrored, sheet, straight=False):
        count = outs * 2 if straight and not direct else outs
        parts = cut((plane,), cap, count, relays // count, mirrored, place, asked, (sheet,))
        return ship(parts, 1, relays // count)[0]

    def near_sent():
        both = (sheets[0], beside)
        parts = cut((0, PLANES), cap, chips // 2, 2, False, place, asked, both)
        kinds = ship(parts, 2, 2)
        return sum([mine for mine, _ in kinds], []), sum([other for _, other in kinds], [])

    index = lax.axis_index("sky").astype(jnp.int32)
    place = jnp.stack([index // relays, jnp.zeros_like(index) if direct else index % relays])
    tiles = tile_map.transpose(0, 2, 1)
    requests = want(place, tiles, row_anchor, col_anchor, peers, cap, near)
    requests, late = lax.optimization_barrier((requests, gradients))
    sheets = [tile(0, gradients)] + [tile(plane, late) for plane in range(1, PLANES)]
    mirrors = [mirror(plane) for plane in range(PLANES)]
    if near:
        beside = lax.ppermute(sheets[0], "sky", swap(near))
    asked = exchange(requests)
    slots, *state = find_slots(place, tiles, (start_x, start_y), peers, cap, direct)
    own, far = [], []
    for plane in range(PLANES):
        if near and plane == 0:
            own.append(near_sent())
        else:
            own.append(cut_sent(plane, False, sheets[plane]))
        far.append(cut_sent(plane, True, mirrors[plane], plane == PLANES - 1))
    for plane in range(PLANES):
        sets = (own[plane], far[plane])
        held = iter(across([other for _, other in sets if other]))
        windows = sum((mine + (next(held) if other else []) for mine, other in sets), [])
        state = interp(plane, slots, jnp.concatenate(windows, axis=0), state)
    return state


def solution(mesh):
    return jax.shard_map(
        body,
        mesh=mesh,
        in_specs=(
            P(("runs", "sky"), None),
            P(("runs", "sky"), None),
            P(None, None, ("runs", "sky"), None),
            P(None, ("runs", "sky"), None),
            P(None, ("runs", "sky")),
            P(None, ("runs", "sky")),
        ),
        out_specs=(P(("runs", "sky"), None, None), P(("runs", "sky"), None, None)),
        check_vma=False,
    )
```

```python
import functools

import jax
import jax.numpy as jnp
from jax import lax
from jax.experimental import pallas as pl
from jax.experimental.pallas import tpu as pltpu
from jax.sharding import PartitionSpec as P


WR = 16
WC = 128
PLANES = 3

lens_ratio = (0.85, 0.7, 0.9)
lens_strength = (0.5, 0.6, 0.45)

GRANT = pltpu.CompilerParams(vmem_limit_bytes=16 << 20)
VMEM = pltpu.VMEM
SMEM = pltpu.SMEM


def whole(space=VMEM):
    return pl.BlockSpec(memory_space=space)


def dot_last(a, b):
    return lax.dot_general(
        a, b, (((1,), (1,)), ((), ())), preferred_element_type=jnp.float32
    )


def spot(place_ref, relays, direct=False):
    return lax.div(place_ref[0], relays), 0 if direct else lax.rem(place_ref[0], relays)


def ranks(peers, tile_ref, plane):
    nblk = tile_ref.shape[2]
    tile = tile_ref[plane]
    hit = (lax.broadcasted_iota(jnp.int32, (peers, nblk), 0) == tile).astype(jnp.float32)
    earlier = (
        lax.broadcasted_iota(jnp.int32, (nblk, nblk), 1)
        < lax.broadcasted_iota(jnp.int32, (nblk, nblk), 0)
    ).astype(jnp.float32).astype(jnp.bfloat16)
    before = dot_last(hit.astype(jnp.bfloat16), earlier)
    return tile, hit, jnp.sum(before * hit, axis=0, keepdims=True).astype(jnp.int32)


def want_kernel(peers, cap, near, place_ref, tile_ref, row_ref, col_ref, req_ref):
    nblk = tile_ref.shape[2]
    relays, lanes = req_ref.shape
    lane = lax.broadcasted_iota(jnp.int32, (lanes, nblk), 0)
    rows = jnp.zeros((relays, lanes), jnp.float32)
    cols = jnp.zeros((relays, lanes), jnp.float32)
    for k in range(PLANES):
        tile, _, rank = ranks(peers, tile_ref, k)
        side = tile // relays
        relay = tile - side * relays
        group = side + 2 * k
        if near and k == 0:
            half, me = spot(place_ref, relays)
            turn = ((relay ^ me) & near) * (side == half).astype(jnp.int32)
            relay = relay ^ turn
            group = jnp.where(turn != 0, 2 * PLANES + side, group)
        here = lane == (rank + group * cap)
        zero = jnp.zeros((), jnp.float32)
        row = jnp.where(here, row_ref[k : k + 1, :].astype(jnp.float32), zero)
        col = jnp.where(here, col_ref[k : k + 1, :].astype(jnp.float32), zero)
        fold = lax.broadcasted_iota(jnp.int32, (relays, nblk), 0) == relay
        fold = fold.astype(jnp.float32).astype(jnp.bfloat16)
        rows += dot_last(fold, row.astype(jnp.bfloat16))
        cols += dot_last(fold, col.astype(jnp.bfloat16))
    req_ref[...] = rows.astype(jnp.int32) * 65536 + cols.astype(jnp.int32)


def want(place, tile_map, row_anchor, col_anchor, peers, cap, near):
    lanes = -(-(PLANES + 1) * 2 * cap // 128) * 128
    return pl.pallas_call(
        functools.partial(want_kernel, peers, cap, near),
        out_shape=jax.ShapeDtypeStruct((peers // 2, lanes), jnp.int32),
        in_specs=[whole(SMEM)] + [whole()] * 3,
        out_specs=whole(),
        name="want",
    )(place, tile_map, row_anchor, col_anchor)


def slot_kernel(peers, cap, direct, place_ref, tile_ref, *refs):
    start_refs, slot_ref, moved_refs, sem = refs[:2], refs[2], refs[3:5], refs[5]
    moves = [
        pltpu.make_async_copy(src, dst, sem.at[at])
        for at, (src, dst) in enumerate(zip(start_refs, moved_refs))
    ]
    for move in moves:
        move.start()
    relays = peers // 2
    half, me = spot(place_ref, relays, direct)
    for k in range(PLANES):
        tile, _, rank = ranks(peers, tile_ref, k)
        side = tile // relays
        relay = (tile - side * relays) ^ me
        if not direct:
            relay = (relay & 1) * (relays // 2) + (relay >> 1)
        far = (side != half).astype(jnp.int32)
        slot_ref[k : k + 1, :] = (far * relays + relay) * cap + rank
    for move in moves:
        move.wait()


def find_slots(place, tile_map, start, peers, cap, direct):
    shapes = [jax.ShapeDtypeStruct((PLANES, tile_map.shape[2]), jnp.int32)]
    shapes += [jax.ShapeDtypeStruct(x.shape, x.dtype) for x in start]
    return pl.pallas_call(
        functools.partial(slot_kernel, peers, cap, direct),
        out_shape=tuple(shapes),
        in_specs=[whole(SMEM), whole()] + [whole(pltpu.MemorySpace.HBM)] * 2,
        out_specs=(whole(),) * 3,
        scratch_shapes=[pltpu.SemaphoreType.DMA((2,))],
        compiler_params=GRANT,
        name="slots",
    )(place, tile_map, *start)


def cut_kernel(planes, cap, mirrored, span, place_ref, req_ref, *refs):
    sheet_refs, out_refs, half_ref = refs[: len(planes)], refs[len(planes) : -1], refs[-1]
    parts = sheet_refs[0].shape[-1] // WC
    for at, sheet_ref in enumerate(sheet_refs):
        for c in range(2):
            for h in range(parts):
                part = sheet_ref[c, :, h * WC : (h + 1) * WC]
                half_ref[(at * 2 + c) * parts + h] = part.astype(jnp.float32)
    lane = lax.broadcasted_iota(jnp.int32, (WR, WC), 1)
    half, me = spot(place_ref, req_ref.shape[0], len(out_refs) == 1)
    side = 1 - half if mirrored else half

    def one(now, carry):
        for m, out_ref in enumerate(out_refs):
            source = (m * span + now) ^ me
            for at, k in enumerate(planes):
                for place in range(cap):
                    packed = req_ref[source, (2 * k + side) * cap + place]
                    row = packed >> 16
                    col = packed & 65535
                    turn = (WC - col) & (WC - 1)
                    left = lane < WC - col
                    slot = (now * len(planes) + at) * cap + place
                    for c in range(2):
                        part = [
                            pltpu.roll(half_ref[(at * 2 + c) * parts + h, pl.ds(row, WR), :], turn, 1)
                            for h in range(parts)
                        ]
                        out_ref[slot, c * WR : (c + 1) * WR, :] = jnp.where(
                            left, part[0], part[1]
                        ).astype(jnp.bfloat16)
        return carry

    lax.fori_loop(0, span, one, 0)


def cut(planes, cap, outs, span, mirrored, place, requests, sheets):
    count = span * len(planes) * cap
    height, width = sheets[0].shape[-2:]
    return pl.pallas_call(
        functools.partial(cut_kernel, planes, cap, mirrored, span),
        out_shape=(jax.ShapeDtypeStruct((count, 2 * WR, WC), jnp.bfloat16),) * outs,
        in_specs=[whole(SMEM), whole(SMEM)] + [whole()] * len(planes),
        out_specs=(whole(),) * outs,
        scratch_shapes=[VMEM((len(planes) * 2 * width // WC, height, WC), jnp.float32)],
        compiler_params=GRANT,
        name="cut",
    )(place, requests, *sheets)


def taps(pos):
    cell = jnp.floor(pos)
    f = pos - cell
    g = 1.0 - f
    f2, g2 = f * f, g * g
    value = (
        g2 * g / 6.0,
        2.0 / 3.0 - f2 + 0.5 * f2 * f,
        2.0 / 3.0 - g2 + 0.5 * g2 * g,
        f2 * f / 6.0,
    )
    slope = (-0.5 * g2, -2.0 * f + 1.5 * f2, 2.0 * g - 1.5 * g2, 0.5 * f2)
    return cell, value, slope


def interp_kernel(plane, slot_ref, win_ref, *refs):
    first, last = plane == 0, plane == PLANES - 1
    if first:
        x_ref, y_ref = refs[:2]
        refs = refs[2:]
    else:
        state_ref = refs[0]
        refs = refs[1:]
    if last:
        pos_out, jac_out = refs[:2]
        refs = refs[2:]
    else:
        state_out = refs[0]
        refs = refs[1:]
    tap_ref, res_ref = refs
    nblk, rays = res_ref.shape[1:]

    if first:
        px, py = x_ref[...], y_ref[...]
    else:
        px, py = state_ref[0], state_ref[1]
    for at, pos in ((0, px), (9, py)):
        cell, value, slope = taps(pos)
        tap_ref[at] = jnp.clip(cell, -4.0, WC + 4.0)
        for j in range(4):
            tap_ref[at + 1 + j] = value[j]
            tap_ref[at + 5 + j] = slope[j]

    def one(b, carry):
        def row(j):
            return tap_ref[j, pl.ds(b, 1), :]

        def spread(at, size, dtype):
            tile = 8 * 4 // jnp.dtype(dtype).itemsize

            def lay(j):
                return jnp.broadcast_to(row(j), (tile, rays)).astype(dtype)[None]

            place = lax.broadcasted_iota(jnp.int32, (size // tile, tile, rays), 0) * tile
            place = (place + lax.broadcasted_iota(jnp.int32, place.shape, 1)).astype(jnp.float32)
            near = place.astype(dtype) - lay(at)
            value = jnp.zeros(near.shape, dtype)
            slope = value
            for j in range(4):
                here = near == jnp.asarray(j - 1, dtype)
                value = jnp.where(here, lay(at + 1 + j), value)
                slope = jnp.where(here, lay(at + 5 + j), slope)
            return value.reshape(size, rays), slope.reshape(size, rays)

        kern = jnp.concatenate(spread(0, WC, jnp.bfloat16), axis=1)
        mixed = jnp.dot(win_ref[slot_ref[plane, b]], kern, preferred_element_type=jnp.float32)
        ky, kyd = spread(9, WR, jnp.float32)
        for c in range(2):
            part = mixed[c * WR : (c + 1) * WR]
            mixed0, mixed1 = part[:, :rays], part[:, rays:]
            for at, product in ((0, ky * mixed0), (2, ky * mixed1), (4, kyd * mixed0)):
                res_ref[at + c, pl.ds(b, 1), :] = jnp.sum(product, axis=0, keepdims=True)
        return carry

    lax.fori_loop(0, nblk, one, 0, unroll=16)

    ratio, strength = lens_ratio[plane], lens_strength[plane]
    ax, ay = res_ref[0], res_ref[1]
    hxx, hyx, hxy, hyy = res_ref[2], res_ref[3], res_ref[4], res_ref[5]
    if first:
        vx, vy = -strength * ax, -strength * ay
        dj = [-strength * h for h in (hxx, hxy, hyx, hyy)]
        jac = [1.0 + dj[0], dj[1], dj[2], 1.0 + dj[3]]
    else:
        vx = ratio * state_ref[2] - strength * ax
        vy = ratio * state_ref[3] - strength * ay
        axx, axy, ayx, ayy = [state_ref[4 + j] for j in range(4)]
        product = (
            hxx * axx + hxy * ayx,
            hxx * axy + hxy * ayy,
            hyx * axx + hyy * ayx,
            hyx * axy + hyy * ayy,
        )
        dj = [ratio * state_ref[8 + j] - strength * product[j] for j in range(4)]
        jac = [old + d for old, d in zip((axx, axy, ayx, ayy), dj)]
    px, py = px + vx, py + vy
    if last:
        pos_out[:, 0, :] = px
        pos_out[:, 1, :] = py
        for j in range(4):
            jac_out[:, j, :] = jac[j]
    else:
        for j, value in enumerate([px, py, vx, vy] + jac + dj):
            state_out[j] = value


def interp(plane, slots, windows, state):
    nblk = slots.shape[1]
    rays = state[0].shape[-1]
    if plane == PLANES - 1:
        out_shape = (
            jax.ShapeDtypeStruct((nblk, 2, rays), jnp.float32),
            jax.ShapeDtypeStruct((nblk, 4, rays), jnp.float32),
        )
    else:
        out_shape = (jax.ShapeDtypeStruct((12, nblk, rays), jnp.float32),)
    return pl.pallas_call(
        functools.partial(interp_kernel, plane),
        out_shape=out_shape,
        in_specs=[whole(SMEM), whole()] + [whole()] * len(state),
        out_specs=(whole(),) * len(out_shape),
        scratch_shapes=[
            VMEM((18, nblk, rays), jnp.float32),
            VMEM((6, nblk, rays), jnp.float32),
        ],
        compiler_params=GRANT,
    )(slots, windows, *state)


def body(start_x, start_y, gradients, tile_map, row_anchor, col_anchor):
    peers = lax.axis_size("sky")
    nblk = start_x.shape[0]
    cap = max(2, 2 * nblk // peers)
    relays = peers // 2
    chips = relays // 2
    direct = chips > 4 or chips & (chips - 1) != 0
    outs = 1 if direct else chips
    near = relays // 2 if chips == 4 else 0
    groups = [[h * relays + r for r in range(relays)] for h in range(2)]
    mirror_pairs = [(i, (i + relays) % peers) for i in range(peers)]

    def swap(bits):
        return [(i, i ^ bits) for i in range(peers)]

    def exchange(x):
        return lax.all_to_all(
            x, "sky", split_axis=0, concat_axis=0, axis_index_groups=groups, tiled=True
        )

    def ship(parts, count, step):
        if direct:
            got = exchange(parts[0].reshape(relays, -1, 2 * WR, WC))
            got = got.reshape(relays, count, cap, 2 * WR, WC)
            return [([got[:, at].reshape(relays * cap, 2 * WR, WC)], []) for at in range(count)]
        got = [parts[0]]
        for m in range(1, len(parts)):
            got.append(lax.ppermute(parts[m], "sky", swap(step * m)))
        if step == 1:
            return [(got[::2] + got[1::2], [])]

        def pieces(at):
            return [part[at * cap : (at + 1) * cap] for part in got]

        return [(pieces(at), pieces(count + at)) for at in range(count)]

    def across(lists):
        if not lists:
            return []
        got = lax.ppermute(jnp.concatenate(sum(lists, []), axis=0), "sky", swap(1))
        size = chips * cap
        return [[got[at * size : (at + 1) * size]] for at in range(len(lists))]

    def tile(plane, sheet):
        return sheet[plane]

    def mirror(plane):
        return lax.ppermute(sheets[plane], "sky", mirror_pairs)

    def cut_sent(plane, mirrored, sheet, straight=False):
        count = outs * 2 if straight and not direct else outs
        parts = cut((plane,), cap, count, relays // count, mirrored, place, asked, (sheet,))
        return ship(parts, 1, relays // count)[0]

    def near_sent():
        both = (sheets[0], beside)
        parts = cut((0, PLANES), cap, chips // 2, 2, False, place, asked, both)
        kinds = ship(parts, 2, 2)
        return sum([mine for mine, _ in kinds], []), sum([other for _, other in kinds], [])

    index = lax.axis_index("sky").astype(jnp.int32)
    place = index.reshape(1)
    tiles = tile_map.transpose(0, 2, 1)
    requests = want(place, tiles, row_anchor, col_anchor, peers, cap, near)
    requests, late = lax.optimization_barrier((requests, gradients))
    sheets = [tile(0, gradients)] + [tile(plane, late) for plane in range(1, PLANES)]
    mirrors = [mirror(plane) for plane in range(PLANES)]
    if near:
        beside = lax.ppermute(sheets[0], "sky", swap(near))
    asked = exchange(requests)
    slots, *state = find_slots(place, tiles, (start_x, start_y), peers, cap, direct)
    own, far = [], []
    for plane in range(PLANES):
        if near and plane == 0:
            own.append(near_sent())
        else:
            own.append(cut_sent(plane, False, sheets[plane]))
        far.append(cut_sent(plane, True, mirrors[plane], plane == PLANES - 1))
    for plane in range(PLANES):
        sets = (own[plane], far[plane])
        held = iter(across([other for _, other in sets if other]))
        windows = sum((mine + (next(held) if other else []) for mine, other in sets), [])
        state = interp(plane, slots, jnp.concatenate(windows, axis=0), state)
    return state


def solution(mesh):
    return jax.shard_map(
        body,
        mesh=mesh,
        in_specs=(
            P(("runs", "sky"), None),
            P(("runs", "sky"), None),
            P(None, None, ("runs", "sky"), None),
            P(None, ("runs", "sky"), None),
            P(None, ("runs", "sky")),
            P(None, ("runs", "sky")),
        ),
        out_specs=(P(("runs", "sky"), None, None), P(("runs", "sky"), None, None)),
        check_vma=False,
    )
```
